32 devices in a mesh: groups: 16 (over z, y, x), batch: 2 (over core).
Axes of the slice: x: 2, y: 2, z: 4, core: 2. Of those that a mesh axis runs over, the one named last changes fastest.
Arguments:
- frames: bfloat16 [32, 1024, 1024], P(('groups', 'batch')), may hold values from -6 to 6
- time_embed: bfloat16 [32, 1024], P(('groups', 'batch')), may hold values from -6 to 6
- lengths: int32 [32], P(('groups', 'batch')), may hold values from 512 to 1024, as said below
- mod_weight: bfloat16 [1024, 6144], replicated, may hold values from -0.1875 to 0.1875
- mod_bias: bfloat16 [6144], replicated, may hold values from -3 to 3
- qkv_weight: bfloat16 [1024, 3072], replicated, may hold values from -0.1875 to 0.1875
- qkv_bias: bfloat16 [3072], replicated, may hold values from -2 to 2
- out_weight: bfloat16 [1024, 1024], replicated, may hold values from -1.5 to 1.5
- out_bias: bfloat16 [1024], replicated, may hold values from -2 to 2
- up_weight: bfloat16 [1024, 2048], replicated, may hold values from -0.1875 to 0.1875
- up_bias: bfloat16 [2048], replicated, may hold values from -2 to 2
- down_weight: bfloat16 [2048, 1024], replicated, may hold values from -0.125 to 0.125
- down_bias: bfloat16 [1024], replicated, may hold values from -2 to 2
- cotangent: bfloat16 [32, 1024, 1024], P(('groups', 'batch')), may hold values from -6 to 6
Outputs:
- frames_out: bfloat16 [32, 1024, 1024], P(('groups', 'batch'))
- frames_grad: float32 [32, 1024, 1024], P(('groups', 'batch'))
- time_grad: float32 [32, 1024], P(('groups', 'batch'))
- mod_weight_grad: float32 [1024, 6144], P('groups')
- mod_bias_grad: float32 [6144], P('groups')
- qkv_weight_grad: float32 [1024, 3072], P('groups')
- qkv_bias_grad: float32 [3072], P('groups')
- out_weight_grad: float32 [1024, 1024], P('groups')
- out_bias_grad: float32 [1024], P('groups')
- up_weight_grad: float32 [1024, 2048], P('groups')
- up_bias_grad: float32 [2048], P('groups')
- down_weight_grad: float32 [2048, 1024], P('groups')
- down_bias_grad: float32 [1024], P('groups')
The draws below stay inside these ranges and needn't reach their ends.
Inputs may be any that keep to these rules, and one draw needn't show every extreme that they name: `lengths`: in every draw some clip has exactly 1024 frames and some other exactly 512; most clips are far shorter than 1024.
All inputs are finite; a program needn't handle non-finite values.
Results may differ from the reference program's by a relative error of at most 0.02.
The reference program's roundings to bfloat16 on the way count: a program that leaves them out, or rounds other values in their place, can miss the bound.
Values may be sent and summed in bfloat16 or wider, within the bound.
A program may use at most 320 MiB of HBM per device.

```python
import jax
import jax.numpy as jnp
from jax import lax

D = 1024
HEADS = 16
HEAD = 64
FF = 2048
LEN = 1024
MINLEN = 512
ITEMS = 32


def draw_lengths(key, part):
    span = LEN - MINLEN
    key_first, key_second, key_top, key_bottom = jax.random.split(jax.random.fold_in(key, 17), 4)
    first = jax.random.randint(key_first, (ITEMS,), 0, span + 1)
    second = jax.random.randint(key_second, (ITEMS,), 0, span + 1)
    base = MINLEN + first * second // max(span, 1)
    top_at = jax.random.randint(key_top, (), 0, ITEMS)
    bottom_at = (top_at + 1 + jax.random.randint(key_bottom, (), 0, ITEMS - 1)) % ITEMS
    position = jnp.arange(ITEMS)
    chosen = jnp.where(position == top_at, LEN, jnp.where(position == bottom_at, MINLEN, base))
    return chosen.astype(jnp.int32)


def shard_levels(key, dims, shards, smallest, high):
    def one(axis_at, parts):
        draws = jax.random.uniform(jax.random.fold_in(jax.random.fold_in(key, 6), axis_at), (parts,), jnp.float32, smallest / len(shards), high / len(shards))
        return jnp.repeat(jnp.exp(draws), dims[axis_at] // parts).reshape((-1,) + (1,) * (len(dims) - axis_at - 1))

    loudness = one(*shards[0])
    for cut in shards[1:]:
        loudness = loudness * one(*cut)
    return loudness


def noise(key, shape, width, limit, cuts=(), held_as=jnp.bfloat16):
    level = shard_levels(key, shape, cuts, -0.22, 0.18) if cuts else 1.0
    drawn = jax.random.normal(key, shape, jnp.float32) * width * level
    return jnp.minimum(jnp.maximum(drawn, -limit), limit).astype(held_as)


def setup_inputs(seed: int = 0) -> dict:
    splits = jax.random.split(jax.random.key(seed), 15)
    return {
        "frames": noise(splits[0], (ITEMS, LEN, D), 1.0, 6.0, ((0, 32),)),
        "time_embed": noise(splits[1], (ITEMS, D), 1.0, 6.0, ((0, 32),)),
        "lengths": draw_lengths(jax.random.fold_in(splits[14], 71), 0),
        "mod_weight": noise(splits[3], (D, 6 * D), D ** -0.5, 0.1875),
        "mod_bias": noise(splits[4], (6 * D,), 0.5, 3.0),
        "qkv_weight": noise(splits[5], (D, 3 * D), D ** -0.5, 0.1875),
        "qkv_bias": noise(splits[6], (3 * D,), 0.3, 2.0),
        "out_weight": noise(splits[7], (D, D), (D // 64) ** -0.5, 1.5),
        "out_bias": noise(splits[8], (D,), 0.3, 2.0),
        "up_weight": noise(splits[9], (D, FF), D ** -0.5, 0.1875),
        "up_bias": noise(splits[10], (FF,), 0.3, 2.0),
        "down_weight": noise(splits[11], (FF, D), FF ** -0.5, 0.125),
        "down_bias": noise(splits[12], (D,), 0.3, 2.0),
        "cotangent": noise(splits[13], (ITEMS, LEN, D), 1.0, 6.0, ((0, 32),)),
    }


@jax.custom_vjp
def low(v):
    return lax.optimization_barrier(v.astype(jnp.bfloat16)).astype(jnp.float32)

@jax.custom_vjp
def low_back(v):
    return v

def low_keep(v):
    return (low(v), None)

def low_pass(kept, grad):
    return (grad,)

def back_keep(v):
    return (v, None)

def back_low(kept, grad):
    return (low(grad),)
low.defvjp(low_keep, low_pass)
low_back.defvjp(back_keep, back_low)
highest = lax.Precision.HIGHEST
norm_eps = 1e-06
neg_fill = -1e+30

def layer_norm(values):
    centred = values - lax.optimization_barrier(jnp.mean(values, axis=-1, keepdims=True))
    spread = lax.optimization_barrier(jnp.mean(centred * centred, axis=-1, keepdims=True))
    return centred * lax.rsqrt(spread + norm_eps)

def rotary_tables(slots, head_size):
    positions = jnp.arange(slots).astype(jnp.float32)[:, None]
    pair_index = jnp.arange(head_size // 2).astype(jnp.float32)[None, :]
    angles = positions * jnp.power(10000.0, -2.0 * pair_index / head_size)
    return (jnp.cos(angles)[:, None, :], jnp.sin(angles)[:, None, :])

def rotate(values, cosine, sine):
    pairs = values.reshape(values.shape[:-1] + (values.shape[-1] // 2, 2))
    first = pairs[..., 0]
    second = pairs[..., 1]
    turned = jnp.stack([first * cosine - second * sine, second * cosine + first * sine], axis=-1)
    return turned.reshape(values.shape)

def item_forward(params, inputs, embeds, length):
    mod_weight, mod_bias, qkv_weight, qkv_bias, out_weight, out_bias, up_weight, up_bias, down_weight, down_bias = params
    embed = low(jax.nn.silu(embeds))
    modulation = low_back(jnp.dot(embed, mod_weight, precision=highest) + mod_bias)
    shift_one = modulation[0 * D:1 * D]
    scale_one = modulation[1 * D:2 * D]
    gate_one = modulation[2 * D:3 * D]
    shift_two = modulation[3 * D:4 * D]
    scale_two = modulation[4 * D:5 * D]
    gate_two = modulation[5 * D:6 * D]
    hidden_one = low(layer_norm(inputs) * (1.0 + scale_one) + shift_one)
    qkv_all = low_back(jnp.dot(hidden_one, qkv_weight, precision=highest) + qkv_bias)
    cosine, sine = rotary_tables(LEN, HEAD)
    query = low(rotate(qkv_all[:, 0:D].reshape(LEN, HEADS, HEAD), cosine, sine))
    keys = low(rotate(qkv_all[:, D:2 * D].reshape(LEN, HEADS, HEAD), cosine, sine))
    values = low(qkv_all[:, 2 * D:3 * D].reshape(LEN, HEADS, HEAD))
    scores = low_back(jnp.einsum('qhd,khd->hqk', query, keys, precision=highest) * HEAD ** (-0.5))
    slot_valid = jnp.arange(LEN).astype(jnp.int32) < length
    scores = jnp.where(slot_valid[None, None, :], scores, neg_fill)
    probs = low(jax.nn.softmax(scores, axis=-1))
    mixed = low_back(low(jnp.einsum('hqk,khd->qhd', probs, values, precision=highest).reshape(LEN, D)))
    attn = low_back(jnp.dot(mixed, out_weight, precision=highest) + out_bias)
    attn = jnp.where(slot_valid[:, None], attn, 0.0)
    middle = inputs + gate_one * attn
    hidden_two = low(layer_norm(middle) * (1.0 + scale_two) + shift_two)
    upper = low_back(jnp.dot(hidden_two, up_weight, precision=highest) + up_bias)
    activ = low(jax.nn.gelu(upper, approximate=True))
    branch = low_back(jnp.dot(activ, down_weight, precision=highest) + down_bias)
    return middle + gate_two * branch

def reference(frames, time_embed, lengths, mod_weight, mod_bias, qkv_weight, qkv_bias, out_weight, out_bias, up_weight, up_bias, down_weight, down_bias, cotangent):
    params = (mod_weight.astype(jnp.float32), mod_bias.astype(jnp.float32), qkv_weight.astype(jnp.float32), qkv_bias.astype(jnp.float32), out_weight.astype(jnp.float32), out_bias.astype(jnp.float32), up_weight.astype(jnp.float32), up_bias.astype(jnp.float32), down_weight.astype(jnp.float32), down_bias.astype(jnp.float32))

    def forward(weights, inputs, embeds):
        step_fn = jax.checkpoint(item_forward)

        def one_item(packed):
            return step_fn(weights, packed[0], packed[1], packed[2])
        return lax.map(one_item, (inputs, embeds, lengths))
    result, backward = jax.vjp(forward, params, frames.astype(jnp.float32), time_embed.astype(jnp.float32))
    param_grads, frames_grad, time_grad = backward(cotangent.astype(jnp.float32))
    return (result.astype(jnp.bfloat16), frames_grad, time_grad, param_grads[0], param_grads[1], param_grads[2], param_grads[3], param_grads[4], param_grads[5], param_grads[6], param_grads[7], param_grads[8], param_grads[9])
```

```python
import jax, jax.numpy as jnp
import numpy as np
from jax import lax
from jax.experimental import pallas as pl
from jax.experimental.pallas import tpu as pltpu
from jax.sharding import PartitionSpec as P

f32 = jnp.float32
bf16 = jnp.bfloat16
HEADS = 16
LOG2E = 1.4426950408889634
EPS = 1e-6
NN = ((1,), (0,))
NT = ((1,), (1,))
TN = ((0,), (0,))
VMEM_LIMIT = 62 * 2**20


def mm(a, b, dims):
    return lax.dot_general(a, b, (dims, ((), ())), preferred_element_type=f32)


def params(**kw):
    return pltpu.CompilerParams(vmem_limit_bytes=VMEM_LIMIT, **kw)


def rot_tables(slots, size):
    pos = np.arange(slots, dtype=np.float64)[:, None]
    pair = np.arange(size // 2, dtype=np.float64)[None, :]
    ang = pos * np.power(10000.0, -2.0 * pair / size)
    cos = np.repeat(np.cos(ang), 2, axis=1)
    sin = np.repeat(np.sin(ang), 2, axis=1) * np.where(np.arange(size) % 2 == 0, -1.0, 1.0)
    return np.tile(cos, (1, 2)).astype(np.float32), np.tile(sin, (1, 2)).astype(np.float32)


def turn(x, cos, sin, even):
    swapped = jnp.where(even, pltpu.roll(x, 127, 1), pltpu.roll(x, 1, 1))
    return x * cos + swapped * sin


def even_lanes(rows):
    return lax.broadcasted_iota(jnp.int32, (rows, 128), 1) % 2 == 0


def full(shape):
    return pl.BlockSpec(shape, lambda *_: (0,) * len(shape), pipeline_mode=pl.Buffered(1))


def mod_kernel(te_ref, w_ref, b_ref, out_ref):
    t = te_ref[...].astype(f32)
    embed = (t * jax.nn.sigmoid(t)).astype(bf16)
    embed = jnp.broadcast_to(embed, (8, embed.shape[1]))
    out_ref[...] = mm(embed, w_ref[...], NN)[:1] + b_ref[...].astype(f32)


def modulation(te, w, b):
    d, n = w.shape
    blk = d
    return pl.pallas_call(
        mod_kernel,
        grid=(n // blk,),
        in_specs=[full((1, d)), pl.BlockSpec((d, blk), lambda i: (0, i)), pl.BlockSpec((1, blk), lambda i: (0, i))],
        out_specs=pl.BlockSpec((1, blk), lambda i: (0, i)),
        out_shape=jax.ShapeDtypeStruct((1, n), f32),
        compiler_params=params(),
        name="modulation",
    )(te, w, b)


def qkv_kernel(x_ref, mod_ref, w_ref, b_ref, cos_ref, sin_ref, h_ref, qkv_ref):
    d = x_ref.shape[1]
    x = x_ref[...].astype(f32)
    c = x - jnp.mean(x, axis=1, keepdims=True)
    r = lax.rsqrt(jnp.mean(c * c, axis=1, keepdims=True) + EPS)
    h = (c * r * (1.0 + mod_ref[:, d : 2 * d]) + mod_ref[:, :d]).astype(bf16)
    h_ref[...] = h
    cos, sin = cos_ref[...], sin_ref[...]
    even = even_lanes(x.shape[0])
    step = 512
    for n in range(0, 3 * d, step):
        y = mm(h, w_ref[:, n : n + step], NN) + b_ref[:, n : n + step].astype(f32)
        for t in range(0, step, 128):
            col = n + t
            z = y[:, t : t + 128]
            if col < 2 * d:
                z = turn(z, cos, sin, even)
            if col < d:
                z = z * 0.125
            qkv_ref[:, col : col + 128] = z.astype(bf16)


def project_qkv(x, mod, w, b, cos, sin, tile=256):
    slots, d = x.shape
    row = lambda n: pl.BlockSpec((tile, n), lambda i: (i, 0))
    return pl.pallas_call(
        qkv_kernel,
        grid=(slots // tile,),
        in_specs=[row(d), full(mod.shape), full(w.shape), full(b.shape), row(128), row(128)],
        out_specs=[row(d), row(3 * d)],
        out_shape=[jax.ShapeDtypeStruct((slots, d), bf16), jax.ShapeDtypeStruct((slots, 3 * d), bf16)],
        compiler_params=params(),
        name="project_qkv",
    )(x, mod, w, b, cos, sin)


def attend_kernel(len_ref, q_ref, k_ref, v_ref, o_ref, e_ref, linv_ref, *, rows_at_once):
    slots = q_ref.shape[0]
    lane = lax.broadcasted_iota(jnp.int32, (1, 128), 1)
    ones = jnp.where(lax.broadcasted_iota(jnp.int32, (slots, 128), 1) == 0, 1.0, 0.0).astype(bf16)
    k = k_ref[...]
    v = jnp.concatenate([v_ref[...], ones], axis=1)
    valid = lax.broadcasted_iota(jnp.int32, (1, slots), 1) < len_ref[0]
    for at in range(0, slots, rows_at_once):
        rows = pl.ds(at, rows_at_once)
        q = q_ref[rows, :]
        outs, invs = [], []
        for h in range(2):
            qh = jnp.where(lane < 64 if h == 0 else lane >= 64, q, jnp.zeros_like(q))
            s = jnp.where(valid, mm(qh, k, NT), -1e30)
            m = jnp.max(s, axis=1, keepdims=True)
            e = jnp.exp2((s - m) * LOG2E).astype(bf16)
            e_ref[h, rows, :] = e
            r = mm(e, v, NN)
            inv = 1.0 / r[:, 128:129]
            outs.append(r[:, :128] * inv)
            invs.append(inv)
        o_ref[rows, :] = jnp.where(lane < 64, outs[0], outs[1]).astype(bf16)
        linv_ref[rows, :] = jnp.where(lane < 64, invs[0], invs[1])


def attend(length, qkv, rows_at_once=128):
    slots, d = qkv.shape[0], qkv.shape[1] // 3
    pairs = d // 128
    col = lambda off: pl.BlockSpec((slots, 128), lambda i, n: (0, off + i))
    return pl.pallas_call(
        lambda *a: attend_kernel(*a, rows_at_once=rows_at_once),
        grid_spec=pltpu.PrefetchScalarGridSpec(
            num_scalar_prefetch=1,
            grid=(pairs,),
            in_specs=[col(0), col(pairs), col(2 * pairs)],
            out_specs=[col(0), pl.BlockSpec((2, slots, slots), lambda i, n: (i, 0, 0)), col(0)],
        ),
        out_shape=[
            jax.ShapeDtypeStruct((slots, d), bf16),
            jax.ShapeDtypeStruct((2 * pairs, slots, slots), bf16),
            jax.ShapeDtypeStruct((slots, d), f32),
        ],
        compiler_params=params(),
        name="attend",
    )(length, qkv, qkv, qkv)


def middle_kernel(
    len_ref, mixed_ref, x_ref, cot_ref, mod_ref, linv_ref, ow_ref, ob_ref, uw_ref, ub_ref, dw_ref, db_ref,
    out_ref, h2_ref, act_ref, dbr_ref, dup_ref, dat_ref, dmix_ref, dmid_ref, dmod_ref,
):
    i = pl.program_id(0)
    tile, d = x_ref.shape
    mod = lambda k: mod_ref[:, k * d : (k + 1) * d]
    gate1, shift2, scale2, gate2 = mod(2), mod(3), mod(4), mod(5)
    slot = lax.broadcasted_iota(jnp.int32, (tile, 1), 0) + i * tile
    valid = slot < len_ref[0]
    attn = jnp.where(valid, mm(mixed_ref[...], ow_ref[...], NN) + ob_ref[...].astype(f32), 0.0)
    mid = x_ref[...].astype(f32) + gate1 * attn
    c = mid - jnp.mean(mid, axis=1, keepdims=True)
    r2 = lax.rsqrt(jnp.mean(c * c, axis=1, keepdims=True) + EPS)
    n2 = c * r2
    h2 = (n2 * (1.0 + scale2) + shift2).astype(bf16)
    h2_ref[...] = h2
    cot = cot_ref[...].astype(f32)
    dbr = (gate2 * cot).astype(bf16)
    dbr_ref[...] = dbr
    ff = uw_ref.shape[1]
    step = 512
    for n in range(0, ff, step):
        u = mm(h2, uw_ref[:, n : n + step], NN) + ub_ref[:, n : n + step].astype(f32)
        c0 = 0.7978845608028654
        th = jnp.tanh(c0 * (u + 0.044715 * u * u * u))
        half = 0.5 * (1.0 + th)
        act_ref[:, n : n + step] = (u * half).astype(bf16)
        grad = half + 0.5 * u * (1.0 - th * th) * (c0 * (1.0 + 3.0 * 0.044715 * u * u))
        da = mm(dbr, dw_ref[n : n + step, :], NT)
        dup_ref[:, n : n + step] = (da * grad).astype(bf16)
    branch = mm(act_ref[...], dw_ref[...], NN) + db_ref[...].astype(f32)
    out_ref[...] = (mid + gate2 * branch).astype(bf16)
    dgate2 = jnp.sum(cot * branch, axis=0, keepdims=True)
    dh2 = mm(dup_ref[...], uw_ref[...], NT)
    dscale2 = jnp.sum(dh2 * n2, axis=0, keepdims=True)
    dshift2 = jnp.sum(dh2, axis=0, keepdims=True)
    dn2 = dh2 * (1.0 + scale2)
    dmid = cot + r2 * (
        dn2 - jnp.mean(dn2, axis=1, keepdims=True) - n2 * jnp.mean(dn2 * n2, axis=1, keepdims=True)
    )
    dmid_ref[...] = dmid
    dgate1 = jnp.sum(dmid * attn, axis=0, keepdims=True)
    dat = jnp.where(valid, gate1 * dmid, 0.0).astype(bf16)
    dat_ref[...] = dat
    dmix_ref[...] = (mm(dat, ow_ref[...], NT) * linv_ref[...]).astype(bf16)
    part = jnp.concatenate([dgate1, dshift2, dscale2, dgate2], axis=1)

    @pl.when(i == 0)
    def _():
        dmod_ref[...] = part

    @pl.when(i > 0)
    def _():
        dmod_ref[...] += part


def middle_part(length, mixed, x, cot, mod, linv, ow, ob, uw, ub, dw, db, tile=256):
    slots, d = x.shape
    ff = uw.shape[1]
    row = lambda n: pl.BlockSpec((tile, n), lambda i, n_: (i, 0))
    S = jax.ShapeDtypeStruct
    return pl.pallas_call(
        middle_kernel,
        grid_spec=pltpu.PrefetchScalarGridSpec(
            num_scalar_prefetch=1,
            grid=(slots // tile,),
            in_specs=[row(d), row(d), row(d), full(mod.shape), row(d), full(ow.shape), full(ob.shape),
                      full(uw.shape), full(ub.shape), full(dw.shape), full(db.shape)],
            out_specs=[row(d), row(d), row(ff), row(d), row(ff), row(d), row(d), row(d),
                       pl.BlockSpec((1, 4 * d), lambda i, n_: (0, 0))],
        ),
        out_shape=[S((slots, d), bf16), S((slots, d), bf16), S((slots, ff), bf16), S((slots, d), bf16),
                   S((slots, ff), bf16), S((slots, d), bf16), S((slots, d), bf16), S((slots, d), f32),
                   S((1, 4 * d), f32)],
        compiler_params=params(),
        name="middle_part",
    )(length, mixed, x, cot, mod, linv, ow, ob, uw, ub, dw, db)


def wgrad_kernel(l_ref, r_ref, w_ref, b_ref):
    w_ref[...] = mm(l_ref[...], r_ref[...], TN).astype(bf16)

    @pl.when(pl.program_id(0) == 0)
    def _():
        b_ref[...] = jnp.sum(r_ref[...].astype(f32), axis=0, keepdims=True)


def wgrad(left, right, tile=256):
    slots, m = left.shape
    n = right.shape[1]
    return pl.pallas_call(
        wgrad_kernel,
        grid=(m // tile,),
        in_specs=[pl.BlockSpec((slots, tile), lambda i: (0, i)), full((slots, n))],
        out_specs=[pl.BlockSpec((tile, n), lambda i: (i, 0)), pl.BlockSpec((1, n), lambda i: (0, 0))],
        out_shape=[jax.ShapeDtypeStruct((m, n), bf16), jax.ShapeDtypeStruct((1, n), f32)],
        compiler_params=params(),
        name="wgrad",
    )(left, right)


def attend_back_kernel(q_ref, k_ref, v_ref, o_ref, do_ref, e_ref, cos_ref, sin_ref, dq_ref, dk_ref, dv_ref, ds_ref, *, rows_at_once):
    slots = q_ref.shape[0]
    lane = lax.broadcasted_iota(jnp.int32, (1, 128), 1)
    q, k, v, do = q_ref[...], k_ref[...], v_ref[...], do_ref[...]
    dqs = []
    for h in range(2):
        mine = lane < 64 if h == 0 else lane >= 64
        parts = []
        for at in range(0, slots, rows_at_once):
            rows = pl.ds(at, rows_at_once)
            d = do_ref[rows, :]
            d = jnp.where(mine, d, jnp.zeros_like(d))
            inner = jnp.sum(d.astype(f32) * o_ref[rows, :].astype(f32), axis=1, keepdims=True)
            ds = (e_ref[h, rows, :].astype(f32) * (mm(d, v, NT) - inner)).astype(bf16)
            ds_ref[h, rows, :] = ds
            parts.append(mm(ds, k, NN))
        dqs.append(jnp.concatenate(parts, axis=0))
    do_t, q_t = do.T, q.T
    dv = jnp.concatenate([mm(do_t[h * 64 : h * 64 + 64], e_ref[h], NN) for h in range(2)], axis=0)
    dk = jnp.concatenate([mm(q_t[h * 64 : h * 64 + 64], ds_ref[h], NN) for h in range(2)], axis=0)
    cos, sin = cos_ref[...], -sin_ref[...]
    even = even_lanes(slots)
    dq = jnp.where(lane < 64, dqs[0], dqs[1]) * 0.125
    dq_ref[...] = turn(dq, cos, sin, even).astype(bf16)
    dk_ref[...] = turn(dk.T, cos, sin, even).astype(bf16)
    dv_ref[...] = dv.T.astype(bf16)


def attend_back(qkv, mixed, dmix, e, cos, sin, rows_at_once=256):
    slots, d = mixed.shape
    pairs = d // 128
    col = lambda off: pl.BlockSpec((slots, 128), lambda i: (0, off + i))
    return pl.pallas_call(
        lambda *a: attend_back_kernel(*a, rows_at_once=rows_at_once),
        grid=(pairs,),
        in_specs=[col(0), col(pairs), col(2 * pairs), col(0), col(0),
                  pl.BlockSpec((2, slots, slots), lambda i: (i, 0, 0)), full((slots, 128)), full((slots, 128))],
        out_specs=[col(0)] * 3,
        out_shape=[jax.ShapeDtypeStruct((slots, d), bf16)] * 3,
        scratch_shapes=[pltpu.VMEM((2, slots, slots), bf16)],
        compiler_params=params(),
        name="attend_back",
    )(qkv, qkv, qkv, mixed, dmix, e, cos, sin)


def front_kernel(dq_ref, dk_ref, dv_ref, w_ref, x_ref, dmid_ref, mod_ref, out_ref, dmod_ref):
    i = pl.program_id(0)
    d = x_ref.shape[1]
    dh = mm(dq_ref[...], w_ref[:, :d], NT) + mm(dk_ref[...], w_ref[:, d : 2 * d], NT) + mm(dv_ref[...], w_ref[:, 2 * d :], NT)
    x = x_ref[...].astype(f32)
    c = x - jnp.mean(x, axis=1, keepdims=True)
    r = lax.rsqrt(jnp.mean(c * c, axis=1, keepdims=True) + EPS)
    n1 = c * r
    dscale = jnp.sum(dh * n1, axis=0, keepdims=True)
    dshift = jnp.sum(dh, axis=0, keepdims=True)
    dn = dh * (1.0 + mod_ref[:, d : 2 * d])
    out_ref[...] = dmid_ref[...] + r * (
        dn - jnp.mean(dn, axis=1, keepdims=True) - n1 * jnp.mean(dn * n1, axis=1, keepdims=True)
    )
    part = jnp.concatenate([dshift, dscale], axis=1)

    @pl.when(i == 0)
    def _():
        dmod_ref[...] = part

    @pl.when(i > 0)
    def _():
        dmod_ref[...] += part


def front_grad(dq, dk, dv, w, x, dmid, mod, tile=256):
    slots, d = x.shape
    row = pl.BlockSpec((tile, d), lambda i: (i, 0))
    return pl.pallas_call(
        front_kernel,
        grid=(slots // tile,),
        in_specs=[row, row, row, full(w.shape), row, row, full(mod.shape)],
        out_specs=[row, pl.BlockSpec((1, 2 * d), lambda i: (0, 0))],
        out_shape=[jax.ShapeDtypeStruct((slots, d), f32), jax.ShapeDtypeStruct((1, 2 * d), f32)],
        compiler_params=params(),
        name="front_grad",
    )(dq, dk, dv, w, x, dmid, mod)


MESH = pl.DeviceIdType.MESH
SMALL = (16, 512)


class Exchange:
    def __init__(self, groups, batch, own, s, sems):
        self.G, self.B, self.H = groups, batch, groups // 4
        self.own = own
        self.s = s
        self.send, self.recv = sems
        g, c = lax.axis_index("groups"), lax.axis_index("batch")
        self.c, self.x, self.y, self.z = c, g % 2, (g // 2) % 2, g // 4
        x, y, z, H, B = self.x, self.y, self.z, self.H, self.B
        pos = lambda z_, y_, x_: z_ * 4 + y_ * 2 + x_
        self.cores = [(g, (c + k) % B) for k in range(1, B)]
        self.across_x = (pos(z, y, 1 - x), c)
        self.across_y = (pos(z, 1 - y, x), c)
        self.across_z = [(pos((z + k) % H, y, x), c) for k in range(1, H)]
        self.n_sems = 2 * (B - 1) + 4 + (H - 1)

    @staticmethod
    def sems_per_chunk(groups, batch):
        return 2 * (batch - 1) + 4 + (groups // 4 - 1)

    def barrier(self):
        sem = pltpu.get_barrier_semaphore()
        peers = self.cores + [self.across_x, self.across_y] + self.across_z
        for p in peers:
            pl.semaphore_signal(sem, inc=1, device_id=p, device_id_type=MESH)
        pl.semaphore_wait(sem, len(peers))

    def copy(self, j, n, src, dst, peer):
        return pltpu.make_async_remote_copy(
            src_ref=src, dst_ref=dst, send_sem=self.send.at[j, n], recv_sem=self.recv.at[j, n],
            device_id=peer, device_id_type=MESH,
        )

    def copies(self, j, phase):
        B, H, x, y, z = self.B, self.H, self.x, self.y, self.z
        s = self.s
        rows, width = s["r0"].shape[-2:]
        half = rows // 2
        if phase == 0:
            out = []
            for k, p in enumerate(self.cores):
                cols = pl.ds(pl.multiple_of(p[1] * width, width), width)
                out.append(self.copy(j, k, self.own(j).at[:, :, :, :, cols], s["r0"].at[j, k], p))
            return out
        n = B - 1
        if phase == 1:
            total = s["r0"].at[j, 0]
            return [
                self.copy(j, n, total.at[:, :, 1 - x, :half], s["r1"].at[j, 0], self.across_x),
                self.copy(j, n + 1, total.at[:, 1 - y, :, half:], s["r1"].at[j, 1], self.across_y),
            ]
        if phase == 2:
            return [
                self.copy(j, n + 2, s["r1"].at[j, 0, :, 1 - y], s["r2"].at[j, :, :half], self.across_y),
                self.copy(j, n + 3, s["r1"].at[j, 1, :, 1 - x], s["r2"].at[j, :, half:], self.across_x),
            ]
        n += 4
        if phase == 3:
            return [
                self.copy(j, n + k, s["r2"].at[j, p[0] // 4], s["r3"].at[j, k], p)
                for k, p in enumerate(self.across_z)
            ]
        n += H - 1
        cols = pl.ds(pl.multiple_of(self.c * width, width), width)
        place = s["out"].at[j, :, cols]
        return [self.copy(j, n + k, place, place, p) for k, p in enumerate(self.cores)]

    def start(self, j, phase):
        for d in self.copies(j, phase):
            d.start()

    def wait(self, j, phase):
        for d in self.copies(j, phase):
            d.wait()

    def finish(self, j, phase):
        self.wait(j, phase)
        s, x, y, z, H = self.s, self.x, self.y, self.z, self.H
        rows, width = s["r0"].shape[-2:]
        half = rows // 2
        cols = pl.ds(pl.multiple_of(self.c * width, width), width)
        if phase == 0:
            own = self.own(j)

            def add(i, _):
                h, b = i // 4, i % 4
                t = own[h, b // 2, b % 2, :, cols].astype(f32)
                for k in range(self.B - 1):
                    t = t + s["r0"][j, k, h, b // 2, b % 2].astype(f32)
                s["r0"][j, 0, h, b // 2, b % 2] = t.astype(bf16)
                return _

            lax.fori_loop(0, 4 * H, add, 0)
        elif phase == 1:

            def add(h, _):
                for i in range(2):
                    a = s["r1"][j, 0, h, i].astype(f32) + s["r0"][j, 0, h, i, x, :half].astype(f32)
                    s["r1"][j, 0, h, i] = a.astype(bf16)
                    b = s["r1"][j, 1, h, i].astype(f32) + s["r0"][j, 0, h, y, i, half:].astype(f32)
                    s["r1"][j, 1, h, i] = b.astype(bf16)
                return _

            lax.fori_loop(0, H, add, 0)
        elif phase == 2:

            def add(h, _):
                a = s["r2"][j, h, :half].astype(f32) + s["r1"][j, 0, h, y].astype(f32)
                s["r2"][j, h, :half] = a.astype(bf16)
                b = s["r2"][j, h, half:].astype(f32) + s["r1"][j, 1, h, x].astype(f32)
                s["r2"][j, h, half:] = b.astype(bf16)
                return _

            lax.fori_loop(0, H, add, 0)
        elif phase == 3:
            t = s["r2"][j, z].astype(f32)
            for k in range(H - 1):
                t = t + s["r3"][j, k].astype(f32)
            s["out"][j, :, cols] = t

    @staticmethod
    def scratch(groups, batch, chunks, rows, cols):
        H, w = groups // 4, cols // batch
        return dict(
            r0=pltpu.VMEM((chunks, batch - 1, H, 2, 2, rows, w), bf16),
            r1=pltpu.VMEM((chunks, 2, H, 2, rows // 2, w), bf16),
            r2=pltpu.VMEM((chunks, H, rows, w), bf16),
            r3=pltpu.VMEM((chunks, H - 1, rows, w), bf16),
            out=pltpu.VMEM((chunks, rows, cols), f32),
        )

    def advance(self, step, chunks):
        for phase in range(4, 0, -1):
            j = step - phase
            if 0 <= j < chunks:
                self.finish(j, phase - 1)
                self.start(j, phase)
        if 0 <= step < chunks:
            self.start(step, 0)


class Small:
    def __init__(self, ex, bias, seen, mine, sems):
        self.ex, self.bias, self.seen, self.mine = ex, bias, seen, mine
        self.send, self.recv = sems

    @staticmethod
    def count(groups, batch):
        return 2 * (batch - 1 + 2 + groups // 4 - 1)

    @staticmethod
    def scratch(groups, batch):
        n = batch - 1 + 2 + groups // 4 - 1
        return dict(
            bias=pltpu.VMEM((n,) + SMALL, f32),
            seen=pltpu.VMEM((groups // 4, 2, 2, batch) + SMALL, bf16),
        )

    def pairs(self, phase):
        ex = self.ex
        B, H, x, y, z, c = ex.B, ex.H, ex.x, ex.y, ex.z, ex.c
        seen = self.seen
        peers = [ex.cores, [ex.across_x], [ex.across_y], ex.across_z][phase]
        first = [0, B - 1, B, B + 1][phase]
        block = [seen.at[z, y, x, c], seen.at[z, y, x], seen.at[z, y], seen.at[z]][phase]
        out = []
        for k, p in enumerate(peers):
            n = 2 * (first + k)
            mk = lambda m, src, dst: pltpu.make_async_remote_copy(
                src_ref=src, dst_ref=dst, send_sem=self.send.at[m], recv_sem=self.recv.at[m],
                device_id=p, device_id_type=MESH)
            out.append(mk(n, self.mine.at[phase], self.bias.at[first + k]))
            out.append(mk(n + 1, block, block))
        return out

    def start(self, phase):
        for d in self.pairs(phase):
            d.start()

    def finish(self, phase):
        for d in self.pairs(phase):
            d.wait()
        ex = self.ex
        n = [ex.B - 1, 1, 1, ex.H - 1][phase]
        first = [0, ex.B - 1, ex.B, ex.B + 1][phase]
        t = self.mine[phase]
        for k in range(n):
            t = t + self.bias[first + k]
        self.mine[phase + 1] = t


def reduce_kernel(groups, batch, chunks, dw_ref, uw_ref, ow_ref, qw_ref, bias_ref, row_ref,
                  dwo_ref, uwo_ref, owo_ref, qwo_ref, bias_out, seen_out,
                  own, r0, r1, r2, r3, out, sbias, seen, mine, send, recv, ssend, srecv, load, store):
    cols = own.shape[-1]
    ex = Exchange(groups, batch, lambda j: own.at[j], dict(r0=r0, r1=r1, r2=r2, r3=r3, out=out), (send, recv))
    sm = Small(ex, sbias, seen, mine, (ssend, srecv))
    src = [dw_ref.at[:, :, :, 0], dw_ref.at[:, :, :, 1]]
    src += [uw_ref.at[:, :, :, :, k * cols : (k + 1) * cols] for k in range(2)]
    src += [ow_ref]
    src += [qw_ref.at[k] for k in range(3)]
    loads = [pltpu.make_async_copy(a, own.at[j], load.at[j]) for j, a in enumerate(src)]
    for d in loads:
        d.start()
    z, y, x, c = ex.z, ex.y, ex.x, ex.c
    mine[0] = bias_ref[...]
    seen[z, y, x, c] = row_ref[...]
    ex.barrier()
    sm.start(0)
    for step in range(chunks + 5):
        if step < chunks:
            loads[step].wait()
        ex.advance(step, chunks)
        if step < 4:
            sm.finish(step)
            if step < 3:
                sm.start(step + 1)
        if 0 <= step - 5 < chunks:
            ex.wait(step - 5, 4)
    bias_out[...] = mine[4]
    dst = [dwo_ref.at[0], dwo_ref.at[1]]
    dst += [uwo_ref.at[:, k * cols : (k + 1) * cols] for k in range(2)]
    dst += [owo_ref]
    dst += [qwo_ref.at[:, k * cols : (k + 1) * cols] for k in range(3)]
    stores = [pltpu.make_async_copy(out.at[j], a, store.at[j]) for j, a in enumerate(dst)]
    stores.append(pltpu.make_async_copy(seen, seen_out, store.at[chunks]))
    for d in stores:
        d.start()
    for d in stores:
        d.wait()


def reduce_all(groups, batch, down, up, outw, qkv3, bias, row):
    d = outw.shape[0]
    H, rows = groups // 4, d // groups
    chunks = 8
    S = jax.ShapeDtypeStruct
    hbm = pl.BlockSpec(memory_space=pl.ANY)
    vm = pl.BlockSpec(memory_space=pltpu.VMEM)
    sc = Exchange.scratch(groups, batch, chunks, rows, d)
    ss = Small.scratch(groups, batch)
    ns, nsm = Exchange.sems_per_chunk(groups, batch), Small.count(groups, batch)
    dma = pltpu.SemaphoreType.DMA
    return pl.pallas_call(
        lambda *a: reduce_kernel(groups, batch, chunks, *a),
        in_specs=[hbm] * 4 + [vm] * 2,
        out_specs=[hbm] * 4 + [vm, hbm],
        out_shape=[S((2, rows, d), f32), S((rows, 2 * d), f32), S((rows, d), f32), S((rows, 3 * d), f32),
                   S(SMALL, f32), S((H, 2, 2, batch) + SMALL, bf16)],
        scratch_shapes=[pltpu.VMEM((chunks, H, 2, 2, rows, d), bf16), sc["r0"], sc["r1"], sc["r2"], sc["r3"], sc["out"],
                        ss["bias"], ss["seen"], pltpu.VMEM((5,) + SMALL, f32),
                        dma((chunks, ns)), dma((chunks, ns)), dma((nsm,)), dma((nsm,)), dma((chunks,)), dma((chunks + 1,))],
        compiler_params=params(collective_id=0, has_side_effects=True),
        name="reduce_all",
    )(down.reshape(H, 2, 2, 2, rows, d), up.reshape(H, 2, 2, rows, 2 * d), outw.reshape(H, 2, 2, rows, d),
      qkv3, bias, row)


def solution(mesh):
    groups, batch = mesh.shape["groups"], mesh.shape["batch"]

    def body(frames, te, lengths, mod_w, mod_b, qkv_w, qkv_b, out_w, out_b, up_w, up_b, down_w, down_b, cot):
        x, ct = frames[0], cot[0]
        slots, d = x.shape
        cos, sin = rot_tables(slots, d // HEADS)
        row = lambda b: b.reshape(1, -1)
        mod = modulation(te, mod_w, row(mod_b))
        h1, qkv = project_qkv(x, mod, qkv_w, row(qkv_b), cos, sin)
        mixed, e, linv = attend(lengths, qkv)
        out, h2, act, dbr, dup, dat, dmix, dmid, dmod_b = middle_part(
            lengths, mixed, x, ct, mod, linv, out_w, row(out_b), up_w, row(up_b), down_w, row(down_b)
        )
        down_g, down_bg = wgrad(act, dbr)
        up_g, up_bg = wgrad(h2, dup)
        out_g, out_bg = wgrad(mixed, dat)
        dq, dk, dv = attend_back(qkv, mixed, dmix, e, cos, sin)
        parts = [wgrad(h1, t) for t in (dq, dk, dv)]
        fg, dmod_a = front_grad(dq, dk, dv, qkv_w, x, dmid, mod)
        dmod = jnp.concatenate([dmod_a, dmod_b], axis=1).astype(bf16)
        embed = jax.nn.silu(te.astype(f32)).astype(bf16)
        pad = jnp.zeros((1, 1024), bf16)
        small = jnp.concatenate([dmod, embed, pad], axis=1).reshape(SMALL)
        bias = jnp.concatenate([p[1] for p in parts] + [out_bg, up_bg, down_bg, pad.astype(f32)], axis=1).reshape(SMALL)
        H, rows = groups // 4, d // groups
        qkv3 = jnp.stack([p[0].reshape(H, 2, 2, rows, d) for p in parts])
        dws, uws, ows, qws, bs, seen = reduce_all(groups, batch, down_g, up_g, out_g, qkv3, bias, small)
        seen = seen.reshape(groups * batch, 8192)
        g = lax.axis_index("groups")
        dm_all, em_all = seen[:, : 6 * d], seen[:, 6 * d : 7 * d]
        em = lax.dynamic_slice_in_dim(em_all, g * rows, rows, 1)
        mod_wg = mm(em, dm_all, TN)
        mod_bg = lax.dynamic_slice_in_dim(jnp.sum(dm_all.astype(f32), axis=0), g * 6 * rows, 6 * rows)
        bs = bs.reshape(8192)
        cut = lambda off, n: lax.dynamic_slice_in_dim(bs, off + g * n, n)
        silu_value, silu_back = jax.vjp(jax.nn.silu, te.astype(f32))
        time_grad = silu_back(mm(dmod, mod_w, NT))[0]
        return (out[None], fg[None], time_grad, mod_wg, mod_bg, qws, cut(0, 3 * rows), ows, cut(3 * d, rows),
                uws, cut(4 * d, 2 * rows), dws.reshape(2 * rows, d), cut(6 * d, 2 * rows // 2))

    split = P(("groups", "batch"))
    own = P("groups")
    return jax.shard_map(
        body, mesh=mesh,
        in_specs=(split,) * 3 + (P(),) * 10 + (split,),
        out_specs=(split,) * 3 + (own,) * 10,
        check_vma=False,
    )
```

```python
import jax, jax.numpy as jnp
import numpy as np
from jax import lax
from jax.experimental import pallas as pl
from jax.experimental.pallas import tpu as pltpu
from jax.sharding import PartitionSpec as P

f32 = jnp.float32
bf16 = jnp.bfloat16
HEADS = 16
LOG2E = 1.4426950408889634
EPS = 1e-6
NN = ((1,), (0,))
NT = ((1,), (1,))
TN = ((0,), (0,))
VMEM_LIMIT = 62 * 2**20


def mm(a, b, dims):
    return lax.dot_general(a, b, (dims, ((), ())), preferred_element_type=f32)


def params(**kw):
    return pltpu.CompilerParams(vmem_limit_bytes=VMEM_LIMIT, **kw)


def rot_tables(slots, size):
    pos = np.arange(slots, dtype=np.float64)[:, None]
    pair = np.arange(size // 2, dtype=np.float64)[None, :]
    ang = pos * np.power(10000.0, -2.0 * pair / size)
    cos = np.repeat(np.cos(ang), 2, axis=1)
    sin = np.repeat(np.sin(ang), 2, axis=1) * np.where(np.arange(size) % 2 == 0, -1.0, 1.0)
    return np.tile(cos, (1, 2)).astype(np.float32), np.tile(sin, (1, 2)).astype(np.float32)


def turn(x, cos, sin, even):
    swapped = jnp.where(even, pltpu.roll(x, 127, 1), pltpu.roll(x, 1, 1))
    return x * cos + swapped * sin


def even_lanes(rows):
    return lax.broadcasted_iota(jnp.int32, (rows, 128), 1) % 2 == 0


def full(shape):
    return pl.BlockSpec(shape, lambda *_: (0,) * len(shape), pipeline_mode=pl.Buffered(1))


def mod_kernel(te_ref, w_ref, b_ref, out_ref):
    t = te_ref[...].astype(f32)
    embed = (t * jax.nn.sigmoid(t)).astype(bf16)
    embed = jnp.broadcast_to(embed, (8, embed.shape[1]))
    out_ref[...] = mm(embed, w_ref[...], NN)[:1] + b_ref[...].astype(f32)


def modulation(te, w, b):
    d, n = w.shape
    blk = d
    return pl.pallas_call(
        mod_kernel,
        grid=(n // blk,),
        in_specs=[full((1, d)), pl.BlockSpec((d, blk), lambda i: (0, i)), pl.BlockSpec((1, blk), lambda i: (0, i))],
        out_specs=pl.BlockSpec((1, blk), lambda i: (0, i)),
        out_shape=jax.ShapeDtypeStruct((1, n), f32),
        compiler_params=params(),
        name="modulation",
    )(te, w, b)


def qkv_kernel(x_ref, mod_ref, w_ref, b_ref, cos_ref, sin_ref, h_ref, qkv_ref):
    d = x_ref.shape[1]
    x = x_ref[...].astype(f32)
    c = x - jnp.mean(x, axis=1, keepdims=True)
    r = lax.rsqrt(jnp.mean(c * c, axis=1, keepdims=True) + EPS)
    h = (c * r * (1.0 + mod_ref[:, d : 2 * d]) + mod_ref[:, :d]).astype(bf16)
    h_ref[...] = h
    cos, sin = cos_ref[...], sin_ref[...]
    even = even_lanes(x.shape[0])
    step = 512
    for n in range(0, 3 * d, step):
        y = mm(h, w_ref[:, n : n + step], NN) + b_ref[:, n : n + step].astype(f32)
        for t in range(0, step, 128):
            col = n + t
            z = y[:, t : t + 128]
            if col < 2 * d:
                z = turn(z, cos, sin, even)
            if col < d:
                z = z * 0.125
            qkv_ref[:, col : col + 128] = z.astype(bf16)


def project_qkv(x, mod, w, b, cos, sin, tile=256):
    slots, d = x.shape
    row = lambda n: pl.BlockSpec((tile, n), lambda i: (i, 0))
    return pl.pallas_call(
        qkv_kernel,
        grid=(slots // tile,),
        in_specs=[row(d), full(mod.shape), full(w.shape), full(b.shape), row(128), row(128)],
        out_specs=[row(d), row(3 * d)],
        out_shape=[jax.ShapeDtypeStruct((slots, d), bf16), jax.ShapeDtypeStruct((slots, 3 * d), bf16)],
        compiler_params=params(),
        name="project_qkv",
    )(x, mod, w, b, cos, sin)


def attend_kernel(len_ref, q_ref, k_ref, v_ref, o_ref, e_ref, linv_ref, *, rows_at_once):
    slots = q_ref.shape[0]
    lane = lax.broadcasted_iota(jnp.int32, (1, 128), 1)
    ones = jnp.where(lax.broadcasted_iota(jnp.int32, (slots, 128), 1) == 0, 1.0, 0.0).astype(bf16)
    k = k_ref[...]
    v = jnp.concatenate([v_ref[...], ones], axis=1)
    valid = lax.broadcasted_iota(jnp.int32, (1, slots), 1) < len_ref[0]
    for at in range(0, slots, rows_at_once):
        rows = pl.ds(at, rows_at_once)
        q = q_ref[rows, :]
        outs, invs = [], []
        for h in range(2):
            qh = jnp.where(lane < 64 if h == 0 else lane >= 64, q, jnp.zeros_like(q))
            s = jnp.where(valid, mm(qh, k, NT), -1e30)
            m = jnp.max(s, axis=1, keepdims=True)
            e = jnp.exp2((s - m) * LOG2E).astype(bf16)
            e_ref[h, rows, :] = e
            r = mm(e, v, NN)
            inv = 1.0 / r[:, 128:129]
            outs.append(r[:, :128] * inv)
            invs.append(inv)
        o_ref[rows, :] = jnp.where(lane < 64, outs[0], outs[1]).astype(bf16)
        linv_ref[rows, :] = jnp.where(lane < 64, invs[0], invs[1])


def attend(length, qkv, rows_at_once=128):
    slots, d = qkv.shape[0], qkv.shape[1] // 3
    pairs = d // 128
    col = lambda off: pl.BlockSpec((slots, 128), lambda i, n: (0, off + i))
    return pl.pallas_call(
        lambda *a: attend_kernel(*a, rows_at_once=rows_at_once),
        grid_spec=pltpu.PrefetchScalarGridSpec(
            num_scalar_prefetch=1,
            grid=(pairs,),
            in_specs=[col(0), col(pairs), col(2 * pairs)],
            out_specs=[col(0), pl.BlockSpec((2, slots, slots), lambda i, n: (i, 0, 0)), col(0)],
        ),
        out_shape=[
            jax.ShapeDtypeStruct((slots, d), bf16),
            jax.ShapeDtypeStruct((2 * pairs, slots, slots), bf16),
            jax.ShapeDtypeStruct((slots, d), f32),
        ],
        compiler_params=params(),
        name="attend",
    )(length, qkv, qkv, qkv)


def middle_kernel(
    len_ref, mixed_ref, x_ref, cot_ref, mod_ref, linv_ref, ow_ref, ob_ref, uw_ref, ub_ref, dw_ref, db_ref,
    out_ref, h2_ref, act_ref, dbr_ref, dup_ref, dat_ref, dmix_ref, dmid_ref, dmod_ref,
):
    i = pl.program_id(0)
    tile, d = x_ref.shape
    mod = lambda k: mod_ref[:, k * d : (k + 1) * d]
    gate1, shift2, scale2, gate2 = mod(2), mod(3), mod(4), mod(5)
    slot = lax.broadcasted_iota(jnp.int32, (tile, 1), 0) + i * tile
    valid = slot < len_ref[0]
    attn = jnp.where(valid, mm(mixed_ref[...], ow_ref[...], NN) + ob_ref[...].astype(f32), 0.0)
    mid = x_ref[...].astype(f32) + gate1 * attn
    c = mid - jnp.mean(mid, axis=1, keepdims=True)
    r2 = lax.rsqrt(jnp.mean(c * c, axis=1, keepdims=True) + EPS)
    n2 = c * r2
    h2 = (n2 * (1.0 + scale2) + shift2).astype(bf16)
    h2_ref[...] = h2
    cot = cot_ref[...].astype(f32)
    dbr = (gate2 * cot).astype(bf16)
    dbr_ref[...] = dbr
    ff = uw_ref.shape[1]
    step = 512
    for n in range(0, ff, step):
        u = mm(h2, uw_ref[:, n : n + step], NN) + ub_ref[:, n : n + step].astype(f32)
        c0 = 0.7978845608028654
        th = jnp.tanh(c0 * (u + 0.044715 * u * u * u))
        half = 0.5 * (1.0 + th)
        act_ref[:, n : n + step] = (u * half).astype(bf16)
        grad = half + 0.5 * u * (1.0 - th * th) * (c0 * (1.0 + 3.0 * 0.044715 * u * u))
        da = mm(dbr, dw_ref[n : n + step, :], NT)
        dup_ref[:, n : n + step] = (da * grad).astype(bf16)
    branch = mm(act_ref[...], dw_ref[...], NN) + db_ref[...].astype(f32)
    out_ref[...] = (mid + gate2 * branch).astype(bf16)
    dgate2 = jnp.sum(cot * branch, axis=0, keepdims=True)
    dh2 = mm(dup_ref[...], uw_ref[...], NT)
    dscale2 = jnp.sum(dh2 * n2, axis=0, keepdims=True)
    dshift2 = jnp.sum(dh2, axis=0, keepdims=True)
    dn2 = dh2 * (1.0 + scale2)
    dmid = cot + r2 * (
        dn2 - jnp.mean(dn2, axis=1, keepdims=True) - n2 * jnp.mean(dn2 * n2, axis=1, keepdims=True)
    )
    dmid_ref[...] = dmid
    dgate1 = jnp.sum(dmid * attn, axis=0, keepdims=True)
    dat = jnp.where(valid, gate1 * dmid, 0.0).astype(bf16)
    dat_ref[...] = dat
    dmix_ref[...] = (mm(dat, ow_ref[...], NT) * linv_ref[...]).astype(bf16)
    part = jnp.concatenate([dgate1, dshift2, dscale2, dgate2], axis=1)

    @pl.when(i == 0)
    def _():
        dmod_ref[...] = part

    @pl.when(i > 0)
    def _():
        dmod_ref[...] += part


def middle_part(length, mixed, x, cot, mod, linv, ow, ob, uw, ub, dw, db, tile=256):
    slots, d = x.shape
    ff = uw.shape[1]
    row = lambda n: pl.BlockSpec((tile, n), lambda i, n_: (i, 0))
    S = jax.ShapeDtypeStruct
    return pl.pallas_call(
        middle_kernel,
        grid_spec=pltpu.PrefetchScalarGridSpec(
            num_scalar_prefetch=1,
            grid=(slots // tile,),
            in_specs=[row(d), row(d), row(d), full(mod.shape), row(d), full(ow.shape), full(ob.shape),
                      full(uw.shape), full(ub.shape), full(dw.shape), full(db.shape)],
            out_specs=[row(d), row(d), row(ff), row(d), row(ff), row(d), row(d), row(d),
                       pl.BlockSpec((1, 4 * d), lambda i, n_: (0, 0))],
        ),
        out_shape=[S((slots, d), bf16), S((slots, d), bf16), S((slots, ff), bf16), S((slots, d), bf16),
                   S((slots, ff), bf16), S((slots, d), bf16), S((slots, d), bf16), S((slots, d), f32),
                   S((1, 4 * d), f32)],
        compiler_params=params(),
        name="middle_part",
    )(length, mixed, x, cot, mod, linv, ow, ob, uw, ub, dw, db)


MESH = pl.DeviceIdType.MESH
STRIP = 512
RING = 4


class Exchange:
    def __init__(self, groups, batch, own, s, sems, chunks):
        self.G, self.B, self.H, self.chunks = groups, batch, groups // 4, chunks
        self.own = own
        self.s = s
        self.send, self.recv = sems
        g, c = lax.axis_index("groups"), lax.axis_index("batch")
        self.c, self.x, self.y, self.z = c, g % 2, (g // 2) % 2, g // 4
        x, y, z, H, B = self.x, self.y, self.z, self.H, self.B
        pos = lambda z_, y_, x_: z_ * 4 + y_ * 2 + x_
        self.cores = [(g, (c + k) % B) for k in range(1, B)]
        self.across_x = (pos(z, y, 1 - x), c)
        self.across_y = (pos(z, 1 - y, x), c)
        self.across_z = [(pos((z + k) % H, y, x), c) for k in range(1, H)]

    @staticmethod
    def sems_per_chunk(groups, batch):
        return 2 * (batch - 1) + 4 + (groups // 4 - 1)

    def barrier(self):
        sem = pltpu.get_barrier_semaphore()
        peers = self.cores + [self.across_x, self.across_y] + self.across_z
        for p in peers:
            pl.semaphore_signal(sem, inc=1, device_id=p, device_id_type=MESH)
        pl.semaphore_wait(sem, len(peers))

    def copy(self, j, n, src, dst, peer):
        return pltpu.make_async_remote_copy(
            src_ref=src, dst_ref=dst, send_sem=self.send.at[j, n], recv_sem=self.recv.at[j, n],
            device_id=peer, device_id_type=MESH,
        )

    def copies(self, j, phase):
        B, H, x, y = self.B, self.H, self.x, self.y
        s = self.s
        rows, width = s["r0"].shape[-2:]
        half = rows // 2
        q = j % RING
        if phase == 0:
            out = []
            for k, p in enumerate(self.cores):
                cols = pl.ds(pl.multiple_of(p[1] * width, width), width)
                out.append(self.copy(j, k, self.own(j).at[:, :, :, :, cols], s["r0"].at[q, k], p))
            return out
        n = B - 1
        if phase == 1:
            total = s["r0"].at[q, 0]
            return [
                self.copy(j, n, total.at[:, :, 1 - x, :half], s["r1"].at[q, 0], self.across_x),
                self.copy(j, n + 1, total.at[:, 1 - y, :, half:], s["r1"].at[q, 1], self.across_y),
            ]
        if phase == 2:
            return [
                self.copy(j, n + 2, s["r1"].at[q, 0, :, 1 - y], s["r2"].at[q, :, :half], self.across_y),
                self.copy(j, n + 3, s["r1"].at[q, 1, :, 1 - x], s["r2"].at[q, :, half:], self.across_x),
            ]
        n += 4
        if phase == 3:
            return [
                self.copy(j, n + k, s["r2"].at[q, p[0] // 4], s["r3"].at[q, k], p)
                for k, p in enumerate(self.across_z)
            ]
        n += H - 1
        cols = pl.ds(pl.multiple_of(self.c * width, width), width)
        place = s["out"].at[j, :, cols]
        return [self.copy(j, n + k, place, place, p) for k, p in enumerate(self.cores)]

    def start(self, j, phase):
        for d in self.copies(j, phase):
            d.start()

    def finish(self, j, phase):
        for d in self.copies(j, phase):
            d.wait()
        s, x, y, z, H = self.s, self.x, self.y, self.z, self.H
        rows, width = s["r0"].shape[-2:]
        half = rows // 2
        q = j % RING
        cols = pl.ds(pl.multiple_of(self.c * width, width), width)
        if phase == 0:
            own = self.own(j)

            def add(i, _):
                h, b = i // 4, i % 4
                t = own[h, b // 2, b % 2, :, cols].astype(f32)
                for k in range(self.B - 1):
                    t = t + s["r0"][q, k, h, b // 2, b % 2].astype(f32)
                s["r0"][q, 0, h, b // 2, b % 2] = t.astype(bf16)
                return _

            lax.fori_loop(0, 4 * H, add, 0)
        elif phase == 1:

            def add(h, _):
                for i in range(2):
                    a = s["r1"][q, 0, h, i].astype(f32) + s["r0"][q, 0, h, i, x, :half].astype(f32)
                    s["r1"][q, 0, h, i] = a.astype(bf16)
                    b = s["r1"][q, 1, h, i].astype(f32) + s["r0"][q, 0, h, y, i, half:].astype(f32)
                    s["r1"][q, 1, h, i] = b.astype(bf16)
                return _

            lax.fori_loop(0, H, add, 0)
        elif phase == 2:

            def add(h, _):
                a = s["r2"][q, h, :half].astype(f32) + s["r1"][q, 0, h, y].astype(f32)
                s["r2"][q, h, :half] = a.astype(bf16)
                b = s["r2"][q, h, half:].astype(f32) + s["r1"][q, 1, h, x].astype(f32)
                s["r2"][q, h, half:] = b.astype(bf16)
                return _

            lax.fori_loop(0, H, add, 0)
        elif phase == 3:
            t = s["r2"][q, z].astype(f32)
            for k in range(H - 1):
                t = t + s["r3"][q, k].astype(f32)
            s["out"][j, :, cols] = t

    @staticmethod
    def scratch(groups, batch, chunks, rows, cols):
        H, w = groups // 4, cols // batch
        return dict(
            r0=pltpu.VMEM((RING, batch - 1, H, 2, 2, rows, w), bf16),
            r1=pltpu.VMEM((RING, 2, H, 2, rows // 2, w), bf16),
            r2=pltpu.VMEM((RING, H, rows, w), bf16),
            r3=pltpu.VMEM((RING, H - 1, rows, w), bf16),
            out=pltpu.VMEM((chunks, rows, cols), f32),
        )

    def advance(self, step):
        static = isinstance(step, int)
        for phase in range(5, -1, -1):
            j = step - phase
            if static and not 0 <= j < self.chunks:
                continue
            if phase > 0:
                self.finish(j, phase - 1)
            if phase < 5:
                self.start(j, phase)


class Small:
    def __init__(self, ex, sems, total=None, mine=None, seen=None):
        self.ex, self.total, self.mine, self.seen = ex, total, mine, seen
        self.send, self.recv = sems

    @staticmethod
    def count(groups, batch):
        return batch - 1 + 2 + groups // 4 - 1

    def copies(self, phase):
        ex = self.ex
        peers = [ex.cores, [ex.across_x], [ex.across_y], ex.across_z][phase]
        first = [0, ex.B - 1, ex.B, ex.B + 1][phase]
        out = []
        for k, p in enumerate(peers):
            n = first + k
            if self.seen is None:
                src, dst = self.mine.at[phase], self.total.at[n]
            else:
                at = (ex.z, ex.y, ex.x, ex.c)[: 4 - phase]
                src = dst = self.seen.at[at]
            out.append(pltpu.make_async_remote_copy(
                src_ref=src, dst_ref=dst, send_sem=self.send.at[n], recv_sem=self.recv.at[n],
                device_id=p, device_id_type=MESH))
        return out

    def start(self, phase):
        for d in self.copies(phase):
            d.start()

    def finish(self, phase):
        for d in self.copies(phase):
            d.wait()
        if self.seen is None:
            ex = self.ex
            n = [ex.B - 1, 1, 1, ex.H - 1][phase]
            first = [0, ex.B - 1, ex.B, ex.B + 1][phase]
            t = self.mine[phase]
            for k in range(n):
                t = t + self.total[first + k]
            self.mine[phase + 1] = t


def back_kernel(groups, batch, per, n_chunks, *refs):
    (act_hbm, dbr_hbm, h2_hbm, dup_hbm, mixed_hbm, dat_hbm, dmix_hbm, qkv_hbm, e_hbm, h1_hbm, w_hbm, x_hbm, dmid_hbm,
     cos_ref, sin_ref, mod_ref, dmodb_ref, te_ref,
     dwo, uwo, owo, qwo, bias_out, early_out, late_out, fg_hbm, dmoda_ref,
     own, r0, r1, r2, r3, out, total, mine, early, late, etmp, ltmp,
     ebuf, dsb, qkv, mixed, dmix, dbr, h2, dat, dmid, fg,
     send, recv, ssum, rsum, sear, rear, slat, rlat, ld, eld, dld, fst, ost) = refs
    slots, d = mixed.shape
    H, rows = groups // 4, d // groups
    chunk = lambda strip: strip // per
    n_own = own.shape[0]
    ex = Exchange(groups, batch, lambda j: own.at[j % n_own], dict(r0=r0, r1=r1, r2=r2, r3=r3, out=out), (send, recv), n_chunks)
    sums = Small(ex, (ssum, rsum), total=total, mine=mine)
    gather_early = Small(ex, (sear, rear), seen=early)
    gather_late = Small(ex, (slat, rlat), seen=late)

    load = lambda k, src, dst: pltpu.make_async_copy(src, dst, ld.at[k])
    half = lambda ref, k: ref.at[:, k * d : (k + 1) * d]
    loads = [
        load(0, half(act_hbm, 0), ebuf.at[1, 0]), load(1, half(act_hbm, 1), ebuf.at[1, 1]), load(2, dbr_hbm, dbr),
        load(3, h2_hbm, h2), load(4, half(dup_hbm, 0), dsb.at[0]), load(5, half(dup_hbm, 1), dsb.at[1]),
        load(6, mixed_hbm, mixed), load(7, dat_hbm, dat), load(8, qkv_hbm, qkv), load(9, dmix_hbm, dmix),
    ]
    load_h1 = load(10, h1_hbm, h2)
    load_w = [load(11 + k, half(w_hbm, k), ebuf.at[k // 2, k % 2]) for k in range(3)]
    load_x = load(14, x_hbm, dat)
    load_e = lambda p, slot: pltpu.make_async_copy(e_hbm.at[pl.ds(2 * p, 2)], ebuf.at[slot], eld.at[slot])
    for t in loads:
        t.start()
    load_e(0, 0).start()

    for k in range(4 * d // STRIP):
        etmp[k : k + 1, :] = dmodb_ref[:, k * STRIP : (k + 1) * STRIP]
    t = te_ref[...].astype(f32)
    t = t * jax.nn.sigmoid(t)
    at = 4 * d // STRIP
    for k in range(d // STRIP):
        etmp[at + k : at + k + 1, :] = t[:, k * STRIP : (k + 1) * STRIP]
    at += d // STRIP
    etmp[at:, :] = jnp.zeros((etmp.shape[0] - at, STRIP), f32)
    early[ex.z, ex.y, ex.x, ex.c] = etmp[...].astype(bf16)
    mine[0] = jnp.zeros(mine.shape[1:], f32)
    ex.barrier()
    gather_early.start(0)

    done = [0]

    def service(ready, most):
        n = max(0, min(ready - done[0], most))
        for _ in range(n):
            ex.advance(done[0])
            done[0] += 1

    def column_sums(value, row, k):
        mine[0, row + k : row + k + 1, :] = jnp.sum(value.astype(f32), axis=0, keepdims=True)

    def wgrad_into(left, block_rows, rights, place, zs):
        parts = block_rows // rows

        def body(i, _):
            n = zs * 4 * block_rows
            lt = left(i * n, n).T
            for k, right in enumerate(rights):
                r = mm(lt, right(), NN).astype(bf16)
                for b in range(4 * zs):
                    for part in range(parts):
                        strip = place(k, part)
                        lo = b * block_rows + part * rows
                        off = (strip % per) * STRIP
                        own[chunk(strip) % n_own, i * zs + b // 4, (b // 2) % 2, b % 2, :, off : off + STRIP] = r[lo : lo + rows]
            return _

        lax.fori_loop(0, H // zs, body, 0)

    for k in (0, 1, 2):
        loads[k].wait()
    wide = lambda ref: lambda lo, n: ref[lo // d, :, pl.ds(pl.multiple_of(lo % d, 128), n)]
    flat = lambda ref: lambda lo, n: ref[:, pl.ds(pl.multiple_of(lo, 128), n)]
    cut = lambda ref, k: lambda: ref[:, k * STRIP : (k + 1) * STRIP]
    wgrad_into(wide(ebuf.at[1]), 2 * rows, [cut(dbr, k) for k in range(2)], lambda k, part: 2 * k + part, 2)
    for k in range(2):
        column_sums(cut(dbr, k)(), 12, k)
    gather_early.finish(0)
    gather_early.start(1)
    service(4 // per, 1)
    for k in (3, 4, 5):
        loads[k].wait()
    for h in range(2):
        wgrad_into(flat(h2), rows, [cut(dsb.at[h], k) for k in range(2)], lambda k, part: 4 + 2 * h + k, 2)
        for k in range(2):
            column_sums(cut(dsb.at[h], k)(), 8 + 2 * h, k)
        if h == 0:
            gather_early.finish(1)
            gather_early.start(2)
        service((6 + 2 * h) // per, 1)
    load_h1.start()
    for k in (6, 7):
        loads[k].wait()
    wgrad_into(flat(mixed), rows, [cut(dat, k) for k in range(2)], lambda k, part: 8 + k, 2)
    for k in range(2):
        column_sums(cut(dat, k)(), 6, k)
    gather_early.finish(2)
    gather_early.start(3)
    load_x.start()
    service(10 // per, 2)
    for k in (8, 9):
        loads[k].wait()
    gather_early.finish(3)
    lane = lax.broadcasted_iota(jnp.int32, (1, 128), 1)
    even = even_lanes(slots)
    pairs = d // 128
    at_once = 256

    def attention(p, slot):
        col = lambda off: pl.ds(pl.multiple_of(off + p * 128, 128), 128)
        qc, kc, vc = col(0), col(d), col(2 * d)
        q, k, v, do = qkv[:, qc], qkv[:, kc], qkv[:, vc], dmix[:, qc]
        dqs = []
        for h in range(2):
            own_lanes = lane < 64 if h == 0 else lane >= 64
            parts = []
            for a in range(0, slots, at_once):
                rws = pl.ds(a, at_once)
                t = dmix[rws, qc]
                t = jnp.where(own_lanes, t, jnp.zeros_like(t))
                inner = jnp.sum(t.astype(f32) * mixed[rws, qc].astype(f32), axis=1, keepdims=True)
                ds = (ebuf[slot, h, rws, :].astype(f32) * (mm(t, v, NT) - inner)).astype(bf16)
                dsb[h, rws, :] = ds
                parts.append(mm(ds, k, NN))
            dqs.append(jnp.concatenate(parts, axis=0))
        do_t, q_t = do.T, q.T
        dv = jnp.concatenate([mm(do_t[h * 64 : h * 64 + 64], ebuf[slot, h], NN) for h in range(2)], axis=0)
        dk = jnp.concatenate([mm(q_t[h * 64 : h * 64 + 64], dsb[h], NN) for h in range(2)], axis=0)
        cos, sin = cos_ref[...], -sin_ref[...]
        dq = jnp.where(lane < 64, dqs[0], dqs[1]) * 0.125
        qkv[:, qc] = turn(dq, cos, sin, even).astype(bf16)
        qkv[:, kc] = turn(dk.T, cos, sin, even).astype(bf16)
        qkv[:, vc] = dv.T.astype(bf16)

    for part in range(2):
        base = done[0]
        assert base >= 5
        ready = (10 if part == 0 else 13) // per
        n_half = pairs // 2
        n_serve = max(0, min(ready - base, n_half))

        def body(i, carry):
            p = part * n_half + i
            slot = p % 2
            load_e(p, slot).wait()

            @pl.when(p + 1 < pairs)
            def _():
                load_e(p + 1, 1 - slot).start()

            attention(p, slot)
            if n_serve:

                @pl.when(i < n_serve)
                def _():
                    ex.advance(base + i)

            return carry

        lax.fori_loop(0, n_half, body, 0)
        done[0] += n_serve
        if part == 0:
            load_h1.wait()
        else:
            for t in load_w:
                t.start()
        order = (0, 1, 2) if part == 0 else (2, 0, 1)
        rights = [cut(qkv, 2 * k + part) for k in order]
        wgrad_into(flat(h2), rows, rights, lambda k, _: 10 + 3 * part + k, 2)
        for k, r in zip(order, rights):
            column_sums(r(), 2 * k + part, 0)
        service((13 if part == 0 else 16) // per, 1)
    sums.start(0)
    tile = dmid.shape[1]
    tiles = slots // tile
    load_d = lambda i, slot: pltpu.make_async_copy(dmid_hbm.at[pl.ds(i * tile, tile)], dmid.at[slot], dld.at[slot])
    store_f = lambda i, slot: pltpu.make_async_copy(fg.at[slot], fg_hbm.at[pl.ds(i * tile, tile)], fst.at[slot])
    load_d(0, 0).start()
    load_x.wait()
    for t in load_w:
        t.wait()
    for i in range(tiles):
        slot = i % 2
        if i + 1 < tiles:
            load_d(i + 1, 1 - slot).start()
        rws = pl.ds(i * tile, tile)
        dh = (
            mm(qkv[rws, :d], ebuf[0, 0], NT) + mm(qkv[rws, d : 2 * d], ebuf[0, 1], NT) + mm(qkv[rws, 2 * d :], ebuf[1, 0], NT)
        )
        x = dat[rws, :].astype(f32)
        cen = x - jnp.mean(x, axis=1, keepdims=True)
        r = lax.rsqrt(jnp.mean(cen * cen, axis=1, keepdims=True) + EPS)
        n1 = cen * r
        psc = jnp.sum(dh * n1, axis=0, keepdims=True)
        psh = jnp.sum(dh, axis=0, keepdims=True)
        if i == 0:
            dmoda_ref[:, :d] = psh
            dmoda_ref[:, d:] = psc
        else:
            dmoda_ref[:, :d] += psh
            dmoda_ref[:, d:] += psc
        dn = dh * (1.0 + mod_ref[:, d : 2 * d])
        load_d(i, slot).wait()
        if i >= 2:
            store_f(i - 2, slot).wait()
        fg[slot] = dmid[slot] + r * (
            dn - jnp.mean(dn, axis=1, keepdims=True) - n1 * jnp.mean(dn * n1, axis=1, keepdims=True)
        )
        store_f(i, slot).start()
        if i < 3:
            sums.finish(i)
            sums.start(i + 1)
        service(n_chunks + 5, 1)
    for k in range(2 * d // 128):
        ltmp[k : k + 1, :] = dmoda_ref[:, k * 128 : (k + 1) * 128]
    late[ex.z, ex.y, ex.x, ex.c] = ltmp[...].astype(bf16)
    gather_late.start(0)
    sums.finish(3)
    for phase in range(4):
        service(n_chunks + 5, 1)
        gather_late.finish(phase)
        if phase < 3:
            gather_late.start(phase + 1)
    bias_out[...] = mine[4]
    for i in range(max(0, tiles - 2), tiles):
        store_f(i, i % 2).wait()
    service(n_chunks + 5, n_chunks + 5)
    dst = [dwo.at[part, :, k * STRIP : (k + 1) * STRIP] for k in range(2) for part in range(2)]
    dst += [uwo.at[:, k * STRIP : (k + 1) * STRIP] for k in range(4)]
    dst += [owo.at[:, k * STRIP : (k + 1) * STRIP] for k in range(2)]
    dst += [qwo.at[:, k * STRIP : (k + 1) * STRIP] for k in (0, 2, 4, 5, 1, 3)]
    stores = []
    for strip, a in enumerate(dst):
        off = (strip % per) * STRIP
        stores.append(pltpu.make_async_copy(out.at[chunk(strip), :, off : off + STRIP], a, ost.at[strip]))
    stores.append(pltpu.make_async_copy(early, early_out, ost.at[16]))
    stores.append(pltpu.make_async_copy(late, late_out, ost.at[17]))
    for t in stores:
        t.start()
    for t in stores:
        t.wait()


def backward(groups, batch, act, dbr, h2, dup, mixed, dat, dmix, qkv, e, h1, w, x, dmid, cos, sin, mod, dmodb, te):
    slots, d = mixed.shape
    H, rows = groups // 4, d // groups
    per = max(1, 128 * batch // STRIP)
    n_chunks = 16 // per
    S = jax.ShapeDtypeStruct
    hbm = pl.BlockSpec(memory_space=pl.ANY)
    vm = pl.BlockSpec(memory_space=pltpu.VMEM)
    V = pltpu.VMEM
    sc = Exchange.scratch(groups, batch, n_chunks, rows, per * STRIP)
    ns, nsm = Exchange.sems_per_chunk(groups, batch), Small.count(groups, batch)
    dma = pltpu.SemaphoreType.DMA
    tile = 256
    seen = (H, 2, 2, batch)
    return pl.pallas_call(
        lambda *a: back_kernel(groups, batch, per, n_chunks, *a),
        in_specs=[hbm] * 13 + [vm] * 5,
        out_specs=[hbm] * 4 + [vm, hbm, hbm, hbm, vm],
        out_shape=[S((2, rows, d), f32), S((rows, 2 * d), f32), S((rows, d), f32), S((rows, 3 * d), f32),
                   S((16, STRIP), f32), S(seen + (16, STRIP), bf16), S(seen + (16, 128), bf16),
                   S((slots, d), f32), S((1, 2 * d), f32)],
        scratch_shapes=[V((-(-10 // per), H, 2, 2, rows, per * STRIP), bf16),
                        sc["r0"], sc["r1"], sc["r2"], sc["r3"], sc["out"],
                        V((nsm, 16, STRIP), f32), V((5, 16, STRIP), f32), V(seen + (16, STRIP), bf16), V(seen + (16, 128), bf16),
                        V((16, STRIP), f32), V((16, 128), f32),
                        V((2, 2, slots, slots), bf16), V((2, slots, slots), bf16), V((slots, 3 * d), bf16), V((slots, d), bf16),
                        V((slots, d), bf16), V((slots, d), bf16), V((slots, d), bf16), V((slots, d), bf16),
                        V((2, tile, d), f32), V((2, tile, d), f32),
                        dma((n_chunks, ns)), dma((n_chunks, ns)), dma((nsm,)), dma((nsm,)), dma((nsm,)), dma((nsm,)),
                        dma((nsm,)), dma((nsm,)), dma((15,)), dma((2,)), dma((2,)), dma((2,)), dma((18,))],
        compiler_params=pltpu.CompilerParams(vmem_limit_bytes=67_000_000, collective_id=0, has_side_effects=True),
        name="backward",
    )(act, dbr, h2, dup, mixed, dat, dmix, qkv, e, h1, w, x, dmid, cos, sin, mod, dmodb, te)


def mods_kernel(em_ref, dm_ref, own_ref, w_ref, te_ref, wg_ref, bg_ref, tg_ref):
    i = pl.program_id(0)
    dm = dm_ref[...]
    wg_ref[...] = mm(em_ref[...], dm, TN)
    bg_ref[...] = jnp.sum(dm.astype(f32), axis=0, keepdims=True)
    part = mm(jnp.broadcast_to(own_ref[...], (8, own_ref.shape[1])), w_ref[...], NT)[:1]

    @pl.when(i == 0)
    def _():
        tg_ref[...] = part

    @pl.when(i > 0)
    def _():
        tg_ref[...] += part

    @pl.when(i == pl.num_programs(0) - 1)
    def _():
        t = te_ref[...].astype(f32)
        s = jax.nn.sigmoid(t)
        tg_ref[...] = tg_ref[...] * (s * (1.0 + t * (1.0 - s)))


def mods(em, dm, own, w, te):
    n, rows = em.shape
    d, wide = w.shape
    col = lambda r: pl.BlockSpec((r, d), lambda i: (0, i))
    S = jax.ShapeDtypeStruct
    return pl.pallas_call(
        mods_kernel,
        grid=(wide // d,),
        in_specs=[full((n, rows)), col(n), col(1), col(d), full((1, d))],
        out_specs=[col(rows), col(1), pl.BlockSpec((1, d), lambda i: (0, 0))],
        out_shape=[S((rows, wide), f32), S((1, wide), f32), S((1, d), f32)],
        compiler_params=params(),
        name="mods",
    )(em, dm, own, w, te)


def solution(mesh):
    groups, batch = mesh.shape["groups"], mesh.shape["batch"]

    def body(frames, te, lengths, mod_w, mod_b, qkv_w, qkv_b, out_w, out_b, up_w, up_b, down_w, down_b, cot):
        x, ct = frames[0], cot[0]
        slots, d = x.shape
        cos, sin = rot_tables(slots, d // HEADS)
        row = lambda b: b.reshape(1, -1)
        mod = modulation(te, mod_w, row(mod_b))
        h1, qkv = project_qkv(x, mod, qkv_w, row(qkv_b), cos, sin)
        mixed, e, linv = attend(lengths, qkv)
        out, h2, act, dbr, dup, dat, dmix, dmid, dmod_b = middle_part(
            lengths, mixed, x, ct, mod, linv, out_w, row(out_b), up_w, row(up_b), down_w, row(down_b)
        )
        dws, uws, ows, qws, bs, early, late, fg, dmod_a = backward(
            groups, batch, act, dbr, h2, dup, mixed, dat, dmix, qkv, e, h1, qkv_w, x, dmid, cos, sin, mod, dmod_b, te
        )
        rows, n = d // groups, groups * batch
        early, late = early.reshape(n, 16 * STRIP), late.reshape(n, 2 * d)
        g = lax.axis_index("groups")
        em = lax.dynamic_slice_in_dim(early, 4 * d + g * rows, rows, 1)
        dm = jnp.concatenate([late, early[:, : 4 * d]], axis=1)
        own = jnp.concatenate([dmod_a, dmod_b], axis=1).astype(bf16)
        mod_wg, mod_bg, time_grad = mods(em, dm, own, mod_w, te)
        bs = bs.reshape(16 * STRIP)
        cut = lambda v, off, n: lax.dynamic_slice_in_dim(v, off + g * n, n)
        return (out[None], fg[None], time_grad, mod_wg, cut(mod_bg[0], 0, 6 * rows), qws, cut(bs, 0, 3 * rows),
                ows, cut(bs, 3 * d, rows), uws, cut(bs, 4 * d, 2 * rows), dws.reshape(2 * rows, d), cut(bs, 6 * d, rows))

    split = P(("groups", "batch"))
    own = P("groups")
    return jax.shard_map(
        body, mesh=mesh,
        in_specs=(split,) * 3 + (P(),) * 10 + (split,),
        out_specs=(split,) * 3 + (own,) * 10,
        check_vma=False,
    )
```

```python
import jax, jax.numpy as jnp
import numpy as np
from jax import lax
from jax.experimental import pallas as pl
from jax.experimental.pallas import tpu as pltpu
from jax.sharding import PartitionSpec as P

f32 = jnp.float32
bf16 = jnp.bfloat16
HEADS = 16
LOG2E = 1.4426950408889634
EPS = 1e-6
NN = ((1,), (0,))
NT = ((1,), (1,))
TN = ((0,), (0,))
VMEM_LIMIT = 62 * 2**20


def mm(a, b, dims):
    return lax.dot_general(a, b, (dims, ((), ())), preferred_element_type=f32)


def params(**kw):
    return pltpu.CompilerParams(vmem_limit_bytes=VMEM_LIMIT, **kw)


BLOCK = 32


def rot_tables(slots, size):
    pair = np.arange(size // 2, dtype=np.float64)[None, :]
    sign = np.where(np.arange(size) % 2 == 0, -1.0, 1.0)
    out = []
    for pos in (np.arange(0, slots, BLOCK), np.arange(BLOCK)):
        ang = pos.astype(np.float64)[:, None] * np.power(10000.0, -2.0 * pair / size)
        cos = np.repeat(np.cos(ang), 2, axis=1)
        sin = np.repeat(np.sin(ang), 2, axis=1) * sign
        out += [np.tile(cos, (1, 2)).astype(np.float32), np.tile(sin, (1, 2)).astype(np.float32)]
    return out


def turn(x, cos, sin, even):
    swapped = jnp.where(even, pltpu.roll(x, 127, 1), pltpu.roll(x, 1, 1))
    return x * cos + swapped * sin


def even_lanes(rows):
    return lax.broadcasted_iota(jnp.int32, (rows, 128), 1) % 2 == 0


def full(shape):
    return pl.BlockSpec(shape, lambda *_: (0,) * len(shape), pipeline_mode=pl.Buffered(1))


def mod_kernel(te_ref, w_ref, b_ref, out_ref):
    t = te_ref[...].astype(f32)
    embed = (t * jax.nn.sigmoid(t)).astype(bf16)
    embed = jnp.broadcast_to(embed, (8, embed.shape[1]))
    out_ref[...] = mm(embed, w_ref[...], NN)[:1] + b_ref[...].astype(f32)


def modulation(te, w, b):
    d, n = w.shape
    blk = d
    return pl.pallas_call(
        mod_kernel,
        grid=(n // blk,),
        in_specs=[full((1, d)), pl.BlockSpec((d, blk), lambda i: (0, i)), pl.BlockSpec((1, blk), lambda i: (0, i))],
        out_specs=pl.BlockSpec((1, blk), lambda i: (0, i)),
        out_shape=jax.ShapeDtypeStruct((1, n), f32),
        compiler_params=params(),
        name="modulation",
    )(te, w, b)


def qkv_kernel(x_ref, mod_ref, w_ref, b_ref, cosa_ref, sina_ref, cosb_ref, sinb_ref, h_ref, qkv_ref, cos_ref, sin_ref):
    d = x_ref.shape[1]
    x = x_ref[...].astype(f32)
    c = x - jnp.mean(x, axis=1, keepdims=True)
    r = lax.rsqrt(jnp.mean(c * c, axis=1, keepdims=True) + EPS)
    h = (c * r * (1.0 + mod_ref[:, d : 2 * d]) + mod_ref[:, :d]).astype(bf16)
    h_ref[...] = h
    cosb, sinb = cosb_ref[...], sinb_ref[...]
    for k in range(x.shape[0] // BLOCK):
        cosa, sina = cosa_ref[k : k + 1, :], sina_ref[k : k + 1, :]
        cos_ref[k * BLOCK : (k + 1) * BLOCK, :] = cosa * cosb - sina * sinb
        sin_ref[k * BLOCK : (k + 1) * BLOCK, :] = sina * cosb + cosa * sinb
    cos, sin = cos_ref[...], sin_ref[...]
    even = even_lanes(x.shape[0])
    step = 512
    for n in range(0, 3 * d, step):
        y = mm(h, w_ref[:, n : n + step], NN) + b_ref[:, n : n + step].astype(f32)
        for t in range(0, step, 128):
            col = n + t
            z = y[:, t : t + 128]
            if col < 2 * d:
                z = turn(z, cos, sin, even)
            if col < d:
                z = z * 0.125
            qkv_ref[:, col : col + 128] = z.astype(bf16)


def project_qkv(x, mod, w, b, tables, tile=256):
    slots, d = x.shape
    row = lambda n: pl.BlockSpec((tile, n), lambda i: (i, 0))
    return pl.pallas_call(
        qkv_kernel,
        grid=(slots // tile,),
        in_specs=[row(d), full(mod.shape), full(w.shape), full(b.shape)]
        + [pl.BlockSpec((tile // BLOCK, 128), lambda i: (i, 0))] * 2 + [full((BLOCK, 128))] * 2,
        out_specs=[row(d), row(3 * d), row(128), row(128)],
        out_shape=[jax.ShapeDtypeStruct((slots, d), bf16), jax.ShapeDtypeStruct((slots, 3 * d), bf16),
                   jax.ShapeDtypeStruct((slots, 128), f32), jax.ShapeDtypeStruct((slots, 128), f32)],
        compiler_params=params(),
        name="project_qkv",
    )(x, mod, w, b, *tables)


def attend_kernel(len_ref, q_ref, k_ref, v_ref, o_ref, e_ref, linv_ref, *, rows_at_once):
    slots = q_ref.shape[0]
    lane = lax.broadcasted_iota(jnp.int32, (1, 128), 1)
    ones = jnp.where(lax.broadcasted_iota(jnp.int32, (slots, 128), 1) == 0, 1.0, 0.0).astype(bf16)
    k = k_ref[...]
    v = jnp.concatenate([v_ref[...], ones], axis=1)
    valid = lax.broadcasted_iota(jnp.int32, (1, slots), 1) < len_ref[0]
    for at in range(0, slots, rows_at_once):
        rows = pl.ds(at, rows_at_once)
        q = q_ref[rows, :]
        outs, invs = [], []
        for h in range(2):
            qh = jnp.where(lane < 64 if h == 0 else lane >= 64, q, jnp.zeros_like(q))
            s = jnp.where(valid, mm(qh, k, NT), -1e30)
            m = jnp.max(s, axis=1, keepdims=True)
            e = jnp.exp2((s - m) * LOG2E).astype(bf16)
            e_ref[h, rows, :] = e
            r = mm(e, v, NN)
            inv = 1.0 / r[:, 128:129]
            outs.append(r[:, :128] * inv)
            invs.append(inv)
        o_ref[rows, :] = jnp.where(lane < 64, outs[0], outs[1]).astype(bf16)
        linv_ref[rows, :] = jnp.where(lane < 64, invs[0], invs[1])


def attend(length, qkv, rows_at_once=128):
    slots, d = qkv.shape[0], qkv.shape[1] // 3
    pairs = d // 128
    col = lambda off: pl.BlockSpec((slots, 128), lambda i, n: (0, off + i))
    return pl.pallas_call(
        lambda *a: attend_kernel(*a, rows_at_once=rows_at_once),
        grid_spec=pltpu.PrefetchScalarGridSpec(
            num_scalar_prefetch=1,
            grid=(pairs,),
            in_specs=[col(0), col(pairs), col(2 * pairs)],
            out_specs=[col(0), pl.BlockSpec((2, slots, slots), lambda i, n: (i, 0, 0)), col(0)],
        ),
        out_shape=[
            jax.ShapeDtypeStruct((slots, d), bf16),
            jax.ShapeDtypeStruct((2 * pairs, slots, slots), bf16),
            jax.ShapeDtypeStruct((slots, d), f32),
        ],
        compiler_params=params(),
        name="attend",
    )(length, qkv, qkv, qkv)


def middle_kernel(
    len_ref, mixed_ref, x_ref, cot_ref, mod_ref, linv_ref, ow_ref, ob_ref, uw_ref, ub_ref, dw_ref, db_ref,
    out_ref, h2_ref, act_ref, dbr_ref, dup_ref, dat_ref, dmix_ref, dmid_ref, dmod_ref,
):
    i = pl.program_id(0)
    tile, d = x_ref.shape
    mod = lambda k: mod_ref[:, k * d : (k + 1) * d]
    gate1, shift2, scale2, gate2 = mod(2), mod(3), mod(4), mod(5)
    slot = lax.broadcasted_iota(jnp.int32, (tile, 1), 0) + i * tile
    valid = slot < len_ref[0]
    attn = jnp.where(valid, mm(mixed_ref[...], ow_ref[...], NN) + ob_ref[...].astype(f32), 0.0)
    mid = x_ref[...].astype(f32) + gate1 * attn
    c = mid - jnp.mean(mid, axis=1, keepdims=True)
    r2 = lax.rsqrt(jnp.mean(c * c, axis=1, keepdims=True) + EPS)
    n2 = c * r2
    h2 = (n2 * (1.0 + scale2) + shift2).astype(bf16)
    h2_ref[...] = h2
    cot = cot_ref[...].astype(f32)
    dbr = (gate2 * cot).astype(bf16)
    dbr_ref[...] = dbr
    ff = uw_ref.shape[1]
    step = 512
    for n in range(0, ff, step):
        u = mm(h2, uw_ref[:, n : n + step], NN) + ub_ref[:, n : n + step].astype(f32)
        c0 = 0.7978845608028654
        th = jnp.tanh(c0 * (u + 0.044715 * u * u * u))
        half = 0.5 * (1.0 + th)
        act_ref[:, n : n + step] = (u * half).astype(bf16)
        grad = half + 0.5 * u * (1.0 - th * th) * (c0 * (1.0 + 3.0 * 0.044715 * u * u))
        da = mm(dbr, dw_ref[n : n + step, :], NT)
        dup_ref[:, n : n + step] = (da * grad).astype(bf16)
    branch = mm(act_ref[...], dw_ref[...], NN) + db_ref[...].astype(f32)
    out_ref[...] = (mid + gate2 * branch).astype(bf16)
    dgate2 = jnp.sum(cot * branch, axis=0, keepdims=True)
    dh2 = mm(dup_ref[...], uw_ref[...], NT)
    dscale2 = jnp.sum(dh2 * n2, axis=0, keepdims=True)
    dshift2 = jnp.sum(dh2, axis=0, keepdims=True)
    dn2 = dh2 * (1.0 + scale2)
    dmid = cot + r2 * (
        dn2 - jnp.mean(dn2, axis=1, keepdims=True) - n2 * jnp.mean(dn2 * n2, axis=1, keepdims=True)
    )
    dmid_ref[...] = dmid
    dgate1 = jnp.sum(dmid * attn, axis=0, keepdims=True)
    dat = jnp.where(valid, gate1 * dmid, 0.0).astype(bf16)
    dat_ref[...] = dat
    dmix_ref[...] = (mm(dat, ow_ref[...], NT) * linv_ref[...]).astype(bf16)
    part = jnp.concatenate([dgate1, dshift2, dscale2, dgate2], axis=1)

    @pl.when(i == 0)
    def _():
        dmod_ref[...] = part

    @pl.when(i > 0)
    def _():
        dmod_ref[...] += part


def middle_part(length, mixed, x, cot, mod, linv, ow, ob, uw, ub, dw, db, tile=256):
    slots, d = x.shape
    ff = uw.shape[1]
    row = lambda n: pl.BlockSpec((tile, n), lambda i, n_: (i, 0))
    S = jax.ShapeDtypeStruct
    return pl.pallas_call(
        middle_kernel,
        grid_spec=pltpu.PrefetchScalarGridSpec(
            num_scalar_prefetch=1,
            grid=(slots // tile,),
            in_specs=[row(d), row(d), row(d), full(mod.shape), row(d), full(ow.shape), full(ob.shape),
                      full(uw.shape), full(ub.shape), full(dw.shape), full(db.shape)],
            out_specs=[row(d), row(d), row(ff), row(d), row(ff), row(d), row(d), row(d),
                       pl.BlockSpec((1, 4 * d), lambda i, n_: (0, 0))],
        ),
        out_shape=[S((slots, d), bf16), S((slots, d), bf16), S((slots, ff), bf16), S((slots, d), bf16),
                   S((slots, ff), bf16), S((slots, d), bf16), S((slots, d), bf16), S((slots, d), f32),
                   S((1, 4 * d), f32)],
        compiler_params=params(),
        name="middle_part",
    )(length, mixed, x, cot, mod, linv, ow, ob, uw, ub, dw, db)


MESH = pl.DeviceIdType.MESH
STRIP = 512
RINGS = dict(r0=4, r1=6, r2=6, r3=4)
DELAYS = (0, 1, 3, 5, 7, 8)


class Exchange:
    def __init__(self, groups, batch, own, s, sems, ready, chunks):
        self.G, self.B, self.H, self.chunks = groups, batch, groups // 4, chunks
        self.plan = []
        while len(self.plan) - self.plan.count(None) < chunks:
            n = len(self.plan) - self.plan.count(None)
            self.plan.append(n if len(self.plan) >= len(ready) or n < ready[len(self.plan)] else None)
        self.gaps = [t for t, c in enumerate(self.plan) if c is None]
        self.last = len(self.plan) - 1 + DELAYS[-1]
        self.own = own
        self.s = s
        self.send, self.recv = sems
        g, c = lax.axis_index("groups"), lax.axis_index("batch")
        self.c, self.x, self.y, self.z = c, g % 2, (g // 2) % 2, g // 4
        x, y, z, H, B = self.x, self.y, self.z, self.H, self.B
        pos = lambda z_, y_, x_: z_ * 4 + y_ * 2 + x_
        self.cores = [(g, (c + k) % B) for k in range(1, B)]
        self.across_x = (pos(z, y, 1 - x), c)
        self.across_y = (pos(z, 1 - y, x), c)
        self.across_z = [(pos((z + k) % H, y, x), c) for k in range(1, H)]

    @staticmethod
    def sems_per_chunk(groups, batch):
        return 2 * (batch - 1) + 4 + (groups // 4 - 1)

    def barrier(self):
        sem = pltpu.get_barrier_semaphore()
        peers = self.cores + [self.across_x, self.across_y] + self.across_z
        for p in peers:
            pl.semaphore_signal(sem, inc=1, device_id=p, device_id_type=MESH)
        pl.semaphore_wait(sem, len(peers))

    def copy(self, j, n, src, dst, peer):
        return pltpu.make_async_remote_copy(
            src_ref=src, dst_ref=dst, send_sem=self.send.at[j, n], recv_sem=self.recv.at[j, n],
            device_id=peer, device_id_type=MESH,
        )

    def copies(self, j, phase):
        B, H, x, y = self.B, self.H, self.x, self.y
        s = self.s
        rows, width = s["r0"].shape[-2:]
        half = rows // 2
        q0, q1, q2, q3 = (j % RINGS[k] for k in ("r0", "r1", "r2", "r3"))
        if phase == 0:
            out = []
            for k, p in enumerate(self.cores):
                cols = pl.ds(pl.multiple_of(p[1] * width, width), width)
                out.append(self.copy(j, k, self.own(j).at[:, :, :, :, cols], s["r0"].at[q0, k], p))
            return out
        n = B - 1
        if phase == 1:
            total = s["r0"].at[q0, 0]
            return [
                self.copy(j, n, total.at[:, :, 1 - x, :half], s["r1"].at[q1, 0], self.across_x),
                self.copy(j, n + 1, total.at[:, 1 - y, :, half:], s["r1"].at[q1, 1], self.across_y),
            ]
        if phase == 2:
            return [
                self.copy(j, n + 2, s["r1"].at[q1, 0, :, 1 - y], s["r2"].at[q2, :, :half], self.across_y),
                self.copy(j, n + 3, s["r1"].at[q1, 1, :, 1 - x], s["r2"].at[q2, :, half:], self.across_x),
            ]
        n += 4
        if phase == 3:
            return [
                self.copy(j, n + k, s["r2"].at[q2, p[0] // 4], s["r3"].at[q3, k], p)
                for k, p in enumerate(self.across_z)
            ]
        n += H - 1
        cols = pl.ds(pl.multiple_of(self.c * width, width), width)
        place = s["out"].at[j, :, cols]
        return [self.copy(j, n + k, place, place, p) for k, p in enumerate(self.cores)]

    def start(self, j, phase):
        for d in self.copies(j, phase):
            d.start()

    def finish(self, j, phase):
        for d in self.copies(j, phase):
            d.wait()
        s, x, y, z, H = self.s, self.x, self.y, self.z, self.H
        rows, width = s["r0"].shape[-2:]
        half = rows // 2
        q0, q1, q2, q3 = (j % RINGS[k] for k in ("r0", "r1", "r2", "r3"))
        cols = pl.ds(pl.multiple_of(self.c * width, width), width)
        if phase == 0:
            own = self.own(j)

            def add(h, _):
                t = own[h, :, :, :, cols]
                if self.B == 2:
                    t = t + s["r0"][q0, 0, h]
                else:
                    t = t.astype(f32)
                    for k in range(self.B - 1):
                        t = t + s["r0"][q0, k, h].astype(f32)
                s["r0"][q0, 0, h] = t.astype(bf16)
                return _

            lax.fori_loop(0, H, add, 0)
        elif phase == 1:

            def add(h, _):
                s["r1"][q1, 0, h] = s["r1"][q1, 0, h] + s["r0"][q0, 0, h, :, x, :half]
                s["r1"][q1, 1, h] = s["r1"][q1, 1, h] + s["r0"][q0, 0, h, y, :, half:]
                return _

            lax.fori_loop(0, H, add, 0)
        elif phase == 2:
            s["r2"][q2, :, :half] = s["r2"][q2, :, :half] + s["r1"][q1, 0, :, y]
            s["r2"][q2, :, half:] = s["r2"][q2, :, half:] + s["r1"][q1, 1, :, x]
        elif phase == 3:
            t = s["r2"][q2, z].astype(f32)
            for k in range(H - 1):
                t = t + s["r3"][q3, k].astype(f32)
            s["out"][j, :, cols] = t

    @staticmethod
    def scratch(groups, batch, chunks, rows, cols):
        H, w = groups // 4, cols // batch
        return dict(
            r0=pltpu.VMEM((RINGS["r0"], batch - 1, H, 2, 2, rows, w), bf16),
            r1=pltpu.VMEM((RINGS["r1"], 2, H, 2, rows // 2, w), bf16),
            r2=pltpu.VMEM((RINGS["r2"], H, rows, w), bf16),
            r3=pltpu.VMEM((RINGS["r3"], H - 1, rows, w), bf16),
            out=pltpu.VMEM((chunks, rows, cols), f32),
        )

    def tick(self, t, first=None, final=None):
        static = isinstance(t, int)
        if static:
            first = final = t
        n = len(self.plan)
        for phase in range(5, -1, -1):
            lo, hi = first - DELAYS[phase], final - DELAYS[phase]
            j = t - DELAYS[phase]
            if hi < 0 or lo >= n or (static and self.plan[j] is None):
                continue

            def act(phase=phase, j=j):
                c = self.plan[j] if static else j
                if not static:
                    for g in self.gaps:
                        if g < lo:
                            c = c - 1
                        elif g <= hi:
                            c = c - jnp.where(j > g, 1, 0)
                if phase > 0:
                    self.finish(c, phase - 1)
                if phase < 5:
                    self.start(c, phase)

            conds = []
            if lo < 0:
                conds.append(j >= 0)
            if hi >= n:
                conds.append(j < n)
            conds += [j != g for g in self.gaps if lo <= g <= hi]
            if static or not conds:
                act()
            else:
                ok = conds[0]
                for c in conds[1:]:
                    ok = jnp.logical_and(ok, c)
                pl.when(ok)(act)


class Small:
    def __init__(self, ex, sems, total=None, mine=None, seen=None):
        self.ex, self.total, self.mine, self.seen = ex, total, mine, seen
        self.send, self.recv = sems

    @staticmethod
    def count(groups, batch):
        return batch - 1 + 2 + groups // 4 - 1

    def copies(self, phase):
        ex = self.ex
        peers = [ex.cores, [ex.across_x], [ex.across_y], ex.across_z][phase]
        first = [0, ex.B - 1, ex.B, ex.B + 1][phase]
        out = []
        for k, p in enumerate(peers):
            n = first + k
            if self.seen is None:
                src, dst = self.mine.at[phase], self.total.at[n]
            else:
                at = (ex.z, ex.y, ex.x, ex.c)[: 4 - phase]
                src = dst = self.seen.at[at]
            out.append(pltpu.make_async_remote_copy(
                src_ref=src, dst_ref=dst, send_sem=self.send.at[n], recv_sem=self.recv.at[n],
                device_id=p, device_id_type=MESH))
        return out

    def start(self, phase):
        for d in self.copies(phase):
            d.start()

    def finish(self, phase):
        for d in self.copies(phase):
            d.wait()
        if self.seen is None:
            ex = self.ex
            n = [ex.B - 1, 1, 1, ex.H - 1][phase]
            first = [0, ex.B - 1, ex.B, ex.B + 1][phase]
            t = self.mine[phase]
            for k in range(n):
                t = t + self.total[first + k]
            self.mine[phase + 1] = t


def back_kernel(groups, batch, per, n_chunks, *refs):
    (act_hbm, dbr_hbm, h2_hbm, dup_hbm, mixed_hbm, dat_hbm, dmix_hbm, qkv_hbm, e_hbm, h1_hbm, w_hbm, x_hbm, dmid_hbm,
     cos_ref, sin_ref, mod_ref, dmodb_ref, te_ref,
     dwo, uwo, owo, qwo, bias_out, early_out, late_out, fg_hbm, dmoda_ref,
     own, r0, r1, r2, r3, out, total, mine, early, late, etmp, ltmp,
     ebuf, dsb, qkv, mixed, dmix, dbr, h2, dat, dmid, fg,
     send, recv, ssum, rsum, sear, rear, slat, rlat, ld, eld, dld, fst, ost) = refs
    slots, d = mixed.shape
    H, rows = groups // 4, d // groups
    chunk = lambda strip: strip // per
    n_own = own.shape[0]
    pairs = d // 128
    n_half = pairs // 2
    ready = [4, 6, 8, 10, 10] + [10] * n_half + [13] * (1 + n_half) + [16]
    ex = Exchange(groups, batch, lambda j: own.at[j % n_own], dict(r0=r0, r1=r1, r2=r2, r3=r3, out=out), (send, recv),
                  [n // per for n in ready], n_chunks)
    sums = Small(ex, (ssum, rsum), total=total, mine=mine)
    gather_early = Small(ex, (sear, rear), seen=early)
    gather_late = Small(ex, (slat, rlat), seen=late)

    load = lambda k, src, dst: pltpu.make_async_copy(src, dst, ld.at[k])
    half = lambda ref, k: ref.at[:, k * d : (k + 1) * d]
    loads = [
        load(0, half(act_hbm, 0), ebuf.at[1, 0]), load(1, half(act_hbm, 1), ebuf.at[1, 1]), load(2, dbr_hbm, dbr),
        load(3, h2_hbm, h2), load(4, half(dup_hbm, 0), dsb.at[0]), load(5, half(dup_hbm, 1), dsb.at[1]),
        load(6, mixed_hbm, mixed), load(7, dat_hbm, dat), load(8, qkv_hbm, qkv), load(9, dmix_hbm, dmix),
    ]
    load_h1 = load(10, h1_hbm, h2)
    load_w = [load(11 + k, half(w_hbm, k), ebuf.at[k // 2, k % 2]) for k in range(3)]
    load_x = load(14, x_hbm, dat)
    load_e = lambda p, slot: pltpu.make_async_copy(e_hbm.at[pl.ds(2 * p, 2)], ebuf.at[slot], eld.at[slot])
    for t in loads[:3]:
        t.start()

    for k in range(4 * d // STRIP):
        etmp[k : k + 1, :] = dmodb_ref[:, k * STRIP : (k + 1) * STRIP]
    t = te_ref[...].astype(f32)
    t = t * jax.nn.sigmoid(t)
    at = 4 * d // STRIP
    for k in range(d // STRIP):
        etmp[at + k : at + k + 1, :] = t[:, k * STRIP : (k + 1) * STRIP]
    at += d // STRIP
    etmp[at:, :] = jnp.zeros((etmp.shape[0] - at, STRIP), f32)
    early[ex.z, ex.y, ex.x, ex.c] = etmp[...].astype(bf16)
    mine[0] = jnp.zeros(mine.shape[1:], f32)
    ex.barrier()
    gather_early.start(0)

    def column_sums(value, row, k):
        mine[0, pl.ds(row + k, 1), :] = jnp.sum(value.astype(f32), axis=0, keepdims=True)

    def wgrad_into(left, block_rows, rights, place, zs):
        parts = block_rows // rows

        def body(i, _):
            n = zs * 4 * block_rows
            lt = left(i * n, n).T
            for k, right in enumerate(rights):
                r = mm(lt, right(), NN).astype(bf16)
                for b in range(4 * zs):
                    for part in range(parts):
                        strip = place(k, part)
                        lo = b * block_rows + part * rows
                        off = (strip % per) * STRIP
                        cols = pl.ds(off if isinstance(off, int) else pl.multiple_of(off, STRIP), STRIP)
                        own[chunk(strip) % n_own, i * zs + b // 4, (b // 2) % 2, b % 2, :, cols] = r[lo : lo + rows]
            return _

        lax.fori_loop(0, H // zs, body, 0)

    for k in (0, 1, 2):
        loads[k].wait()
    for k in (3, 4, 5, 6, 7):
        loads[k].start()
    wide = lambda ref: lambda lo, n: ref[lo // d, :, pl.ds(pl.multiple_of(lo % d, 128), n)]
    flat = lambda ref: lambda lo, n: ref[:, pl.ds(pl.multiple_of(lo, 128), n)]
    strip_at = lambda k: pl.ds(k * STRIP if isinstance(k, int) else pl.multiple_of(k * STRIP, STRIP), STRIP)
    cut = lambda ref, k: lambda: ref[:, strip_at(k)]
    wgrad_into(wide(ebuf.at[1]), 2 * rows, [cut(dbr, k) for k in range(2)], lambda k, part: 2 * k + part, 2)
    for k in range(2):
        column_sums(cut(dbr, k)(), 12, k)
    gather_early.finish(0)
    gather_early.start(1)
    ex.tick(0)
    for k in (3, 4, 5):
        loads[k].wait()
    for k in (8, 9):
        loads[k].start()
    load_e(0, 0).start()
    for h in range(2):
        wgrad_into(flat(h2), rows, [cut(dsb.at[h], k) for k in range(2)], lambda k, part: 4 + 2 * h + k, 2)
        for k in range(2):
            column_sums(cut(dsb.at[h], k)(), 8 + 2 * h, k)
        if h == 0:
            gather_early.finish(1)
            gather_early.start(2)
        ex.tick(1 + h)
    load_h1.start()
    for k in (6, 7):
        loads[k].wait()
    wgrad_into(flat(mixed), rows, [cut(dat, k) for k in range(2)], lambda k, part: 8 + k, 2)
    for k in range(2):
        column_sums(cut(dat, k)(), 6, k)
    gather_early.finish(2)
    gather_early.start(3)
    load_x.start()
    ex.tick(3)
    ex.tick(4)
    for k in (8, 9):
        loads[k].wait()
    gather_early.finish(3)
    lane = lax.broadcasted_iota(jnp.int32, (1, 128), 1)
    even = even_lanes(slots)
    at_once = 256

    def attention(p, slot):
        col = lambda off: pl.ds(pl.multiple_of(off + p * 128, 128), 128)
        qc, kc, vc = col(0), col(d), col(2 * d)
        q, k, v, do = qkv[:, qc], qkv[:, kc], qkv[:, vc], dmix[:, qc]
        dqs = []
        for h in range(2):
            own_lanes = lane < 64 if h == 0 else lane >= 64
            parts = []
            for a in range(0, slots, at_once):
                rws = pl.ds(a, at_once)
                t = dmix[rws, qc]
                t = jnp.where(own_lanes, t, jnp.zeros_like(t))
                inner = jnp.sum(t.astype(f32) * mixed[rws, qc].astype(f32), axis=1, keepdims=True)
                ds = (ebuf[slot, h, rws, :].astype(f32) * (mm(t, v, NT) - inner)).astype(bf16)
                dsb[h, rws, :] = ds
                parts.append(mm(ds, k, NN))
            dqs.append(jnp.concatenate(parts, axis=0))
        do_t, q_t = do.T, q.T
        dv = jnp.concatenate([mm(do_t[h * 64 : h * 64 + 64], ebuf[slot, h], NN) for h in range(2)], axis=0)
        dk = jnp.concatenate([mm(q_t[h * 64 : h * 64 + 64], dsb[h], NN) for h in range(2)], axis=0)
        cos, sin = cos_ref[...], -sin_ref[...]
        dq = jnp.where(lane < 64, dqs[0], dqs[1]) * 0.125
        qkv[:, qc] = turn(dq, cos, sin, even).astype(bf16)
        qkv[:, kc] = turn(dk.T, cos, sin, even).astype(bf16)
        qkv[:, vc] = dv.T.astype(bf16)

    def half_of_heads(part, carry):
        base = 5 + part * (n_half + 1)

        def body(i, carry):
            p = part * n_half + i
            slot = p % 2
            load_e(p, slot).wait()

            @pl.when(p + 1 < pairs)
            def _():
                load_e(p + 1, 1 - slot).start()

            attention(p, slot)
            ex.tick(base + i, 5, 5 + 2 * n_half)
            return carry

        lax.fori_loop(0, n_half, body, 0)

        @pl.when(part == 0)
        def _():
            load_h1.wait()

        @pl.when(part == 1)
        def _():
            for t in load_w:
                t.start()

        rights = [cut(qkv, 2 * k + part) for k in range(3)]
        wgrad_into(flat(h2), rows, rights, lambda k, _: 10 + 3 * part + k, 2)
        for k, r in enumerate(rights):
            column_sums(r(), 2 * k + part, 0)
        ex.tick(base + n_half, 5 + n_half, 6 + 2 * n_half)
        return carry

    lax.fori_loop(0, 2, half_of_heads, 0)
    sums.start(0)
    tile = dmid.shape[1]
    tiles = slots // tile
    row_tile = lambda i: pl.ds(pl.multiple_of(i * tile, tile), tile)
    load_d = lambda i, slot: pltpu.make_async_copy(dmid_hbm.at[row_tile(i)], dmid.at[slot], dld.at[slot])
    store_f = lambda i, slot: pltpu.make_async_copy(fg.at[slot], fg_hbm.at[row_tile(i)], fst.at[slot])
    load_d(0, 0).start()
    load_x.wait()
    for t in load_w:
        t.wait()
    dmoda_ref[...] = jnp.zeros_like(dmoda_ref)
    t0 = 7 + 2 * n_half

    def front(i, carry):
        slot = i % 2

        @pl.when(i + 1 < tiles)
        def _():
            load_d(i + 1, 1 - slot).start()

        ex.tick(t0 + 2 * i, t0, t0 + 2 * tiles - 2)
        rws = row_tile(i)
        dh = (
            mm(qkv[rws, :d], ebuf[0, 0], NT) + mm(qkv[rws, d : 2 * d], ebuf[0, 1], NT) + mm(qkv[rws, 2 * d :], ebuf[1, 0], NT)
        )
        x = dat[rws, :].astype(f32)
        cen = x - jnp.mean(x, axis=1, keepdims=True)
        r = lax.rsqrt(jnp.mean(cen * cen, axis=1, keepdims=True) + EPS)
        n1 = cen * r
        dmoda_ref[:, :d] += jnp.sum(dh, axis=0, keepdims=True)
        dmoda_ref[:, d:] += jnp.sum(dh * n1, axis=0, keepdims=True)
        dn = dh * (1.0 + mod_ref[:, d : 2 * d])
        load_d(i, slot).wait()

        @pl.when(i >= 2)
        def _():
            store_f(i - 2, slot).wait()

        fg[slot] = dmid[slot] + r * (
            dn - jnp.mean(dn, axis=1, keepdims=True) - n1 * jnp.mean(dn * n1, axis=1, keepdims=True)
        )
        store_f(i, slot).start()
        for phase in range(3):

            @pl.when(i == phase)
            def _():
                sums.finish(phase)
                sums.start(phase + 1)

        ex.tick(t0 + 2 * i + 1, t0 + 1, t0 + 2 * tiles - 1)
        return carry

    lax.fori_loop(0, tiles, front, 0)
    for k in range(2 * d // 128):
        ltmp[k : k + 1, :] = dmoda_ref[:, k * 128 : (k + 1) * 128]
    late[ex.z, ex.y, ex.x, ex.c] = ltmp[...].astype(bf16)
    gather_late.start(0)
    sums.finish(3)
    t = t0 + 2 * tiles
    for phase in range(4):
        if t <= ex.last:
            ex.tick(t)
            t += 1
        gather_late.finish(phase)
        if phase < 3:
            gather_late.start(phase + 1)
    bias_out[...] = mine[4]
    for i in range(max(0, tiles - 2), tiles):
        store_f(i, i % 2).wait()
    while t <= ex.last:
        ex.tick(t)
        t += 1
    dst = [dwo.at[part, :, k * STRIP : (k + 1) * STRIP] for k in range(2) for part in range(2)]
    dst += [uwo.at[:, k * STRIP : (k + 1) * STRIP] for k in range(4)]
    dst += [owo.at[:, k * STRIP : (k + 1) * STRIP] for k in range(2)]
    dst += [qwo.at[:, k * STRIP : (k + 1) * STRIP] for k in (0, 2, 4, 1, 3, 5)]
    stores = []
    for strip, a in enumerate(dst):
        off = (strip % per) * STRIP
        stores.append(pltpu.make_async_copy(out.at[chunk(strip), :, off : off + STRIP], a, ost.at[strip]))
    stores.append(pltpu.make_async_copy(early, early_out, ost.at[16]))
    stores.append(pltpu.make_async_copy(late, late_out, ost.at[17]))
    for t in stores:
        t.start()
    for t in stores:
        t.wait()


def backward(groups, batch, act, dbr, h2, dup, mixed, dat, dmix, qkv, e, h1, w, x, dmid, cos, sin, mod, dmodb, te):
    slots, d = mixed.shape
    H, rows = groups // 4, d // groups
    per = max(1, 128 * batch // STRIP)
    n_chunks = 16 // per
    S = jax.ShapeDtypeStruct
    hbm = pl.BlockSpec(memory_space=pl.ANY)
    vm = pl.BlockSpec(memory_space=pltpu.VMEM)
    V = pltpu.VMEM
    sc = Exchange.scratch(groups, batch, n_chunks, rows, per * STRIP)
    ns, nsm = Exchange.sems_per_chunk(groups, batch), Small.count(groups, batch)
    dma = pltpu.SemaphoreType.DMA
    tile = 256
    seen = (H, 2, 2, batch)
    return pl.pallas_call(
        lambda *a: back_kernel(groups, batch, per, n_chunks, *a),
        in_specs=[hbm] * 13 + [vm] * 5,
        out_specs=[hbm] * 4 + [vm, hbm, hbm, hbm, vm],
        out_shape=[S((2, rows, d), f32), S((rows, 2 * d), f32), S((rows, d), f32), S((rows, 3 * d), f32),
                   S((16, STRIP), f32), S(seen + (16, STRIP), bf16), S(seen + (16, 128), bf16),
                   S((slots, d), f32), S((1, 2 * d), f32)],
        scratch_shapes=[V((-(-10 // per), H, 2, 2, rows, per * STRIP), bf16),
                        sc["r0"], sc["r1"], sc["r2"], sc["r3"], sc["out"],
                        V((nsm, 16, STRIP), f32), V((5, 16, STRIP), f32), V(seen + (16, STRIP), bf16), V(seen + (16, 128), bf16),
                        V((16, STRIP), f32), V((16, 128), f32),
                        V((2, 2, slots, slots), bf16), V((2, slots, slots), bf16), V((slots, 3 * d), bf16), V((slots, d), bf16),
                        V((slots, d), bf16), V((slots, d), bf16), V((slots, d), bf16), V((slots, d), bf16),
                        V((2, tile, d), f32), V((2, tile, d), f32),
                        dma((n_chunks, ns)), dma((n_chunks, ns)), dma((nsm,)), dma((nsm,)), dma((nsm,)), dma((nsm,)),
                        dma((nsm,)), dma((nsm,)), dma((15,)), dma((2,)), dma((2,)), dma((2,)), dma((18,))],
        compiler_params=pltpu.CompilerParams(vmem_limit_bytes=67_000_000, collective_id=0, has_side_effects=True),
        name="backward",
    )(act, dbr, h2, dup, mixed, dat, dmix, qkv, e, h1, w, x, dmid, cos, sin, mod, dmodb, te)


def mods_kernel(em_ref, dm_ref, own_ref, w_ref, te_ref, wg_ref, bg_ref, tg_ref):
    i = pl.program_id(0)
    dm = dm_ref[...]
    wg_ref[...] = mm(em_ref[...], dm, TN)
    bg_ref[...] = jnp.sum(dm.astype(f32), axis=0, keepdims=True)
    part = mm(jnp.broadcast_to(own_ref[...], (8, own_ref.shape[1])), w_ref[...], NT)[:1]

    @pl.when(i == 0)
    def _():
        tg_ref[...] = part

    @pl.when(i > 0)
    def _():
        tg_ref[...] += part

    @pl.when(i == pl.num_programs(0) - 1)
    def _():
        t = te_ref[...].astype(f32)
        s = jax.nn.sigmoid(t)
        tg_ref[...] = tg_ref[...] * (s * (1.0 + t * (1.0 - s)))


def mods(em, dm, own, w, te):
    n, rows = em.shape
    d, wide = w.shape
    col = lambda r: pl.BlockSpec((r, d), lambda i: (0, i))
    S = jax.ShapeDtypeStruct
    return pl.pallas_call(
        mods_kernel,
        grid=(wide // d,),
        in_specs=[full((n, rows)), col(n), col(1), col(d), full((1, d))],
        out_specs=[col(rows), col(1), pl.BlockSpec((1, d), lambda i: (0, 0))],
        out_shape=[S((rows, wide), f32), S((1, wide), f32), S((1, d), f32)],
        compiler_params=params(),
        name="mods",
    )(em, dm, own, w, te)


def solution(mesh):
    groups, batch = mesh.shape["groups"], mesh.shape["batch"]

    def body(frames, te, lengths, mod_w, mod_b, qkv_w, qkv_b, out_w, out_b, up_w, up_b, down_w, down_b, cot):
        x, ct = frames[0], cot[0]
        slots, d = x.shape
        row = lambda b: b.reshape(1, -1)
        mod = modulation(te, mod_w, row(mod_b))
        h1, qkv, cos, sin = project_qkv(x, mod, qkv_w, row(qkv_b), rot_tables(slots, d // HEADS))
        mixed, e, linv = attend(lengths, qkv)
        out, h2, act, dbr, dup, dat, dmix, dmid, dmod_b = middle_part(
            lengths, mixed, x, ct, mod, linv, out_w, row(out_b), up_w, row(up_b), down_w, row(down_b)
        )
        dws, uws, ows, qws, bs, early, late, fg, dmod_a = backward(
            groups, batch, act, dbr, h2, dup, mixed, dat, dmix, qkv, e, h1, qkv_w, x, dmid, cos, sin, mod, dmod_b, te
        )
        rows, n = d // groups, groups * batch
        early, late = early.reshape(n, 16 * STRIP), late.reshape(n, 2 * d)
        g = lax.axis_index("groups")
        em = lax.dynamic_slice_in_dim(early, 4 * d + g * rows, rows, 1)
        dm = jnp.concatenate([late, early[:, : 4 * d]], axis=1)
        own = jnp.concatenate([dmod_a, dmod_b], axis=1).astype(bf16)
        mod_wg, mod_bg, time_grad = mods(em, dm, own, mod_w, te)
        bs = bs.reshape(16 * STRIP)
        cut = lambda v, off, n: lax.dynamic_slice_in_dim(v, off + g * n, n)
        return (out[None], fg[None], time_grad, mod_wg, cut(mod_bg[0], 0, 6 * rows), qws, cut(bs, 0, 3 * rows),
                ows, cut(bs, 3 * d, rows), uws, cut(bs, 4 * d, 2 * rows), dws.reshape(2 * rows, d), cut(bs, 6 * d, rows))

    split = P(("groups", "batch"))
    own = P("groups")
    return jax.shard_map(
        body, mesh=mesh,
        in_specs=(split,) * 3 + (P(),) * 10 + (split,),
        out_specs=(split,) * 3 + (own,) * 10,
        check_vma=False,
    )
```

```python
import jax, jax.numpy as jnp
import numpy as np
from jax import lax
from jax.experimental import pallas as pl
from jax.experimental.pallas import tpu as pltpu
from jax.sharding import PartitionSpec as P

f32 = jnp.float32
bf16 = jnp.bfloat16
HEADS = 16
LOG2E = 1.4426950408889634
EPS = 1e-6
NN = ((1,), (0,))
NT = ((1,), (1,))
TN = ((0,), (0,))
VMEM_LIMIT = 62 * 2**20


def mm(a, b, dims):
    return lax.dot_general(a, b, (dims, ((), ())), preferred_element_type=f32)


def params(**kw):
    return pltpu.CompilerParams(vmem_limit_bytes=VMEM_LIMIT, **kw)


BLOCK = 32


def rot_tables(slots, size):
    pair = np.arange(size // 2, dtype=np.float64)[None, :]
    sign = np.where(np.arange(size) % 2 == 0, -1.0, 1.0)
    out = []
    for pos in (np.arange(0, slots, BLOCK), np.arange(BLOCK)):
        ang = pos.astype(np.float64)[:, None] * np.power(10000.0, -2.0 * pair / size)
        cos = np.repeat(np.cos(ang), 2, axis=1)
        sin = np.repeat(np.sin(ang), 2, axis=1) * sign
        out += [np.tile(cos, (1, 2)).astype(np.float32), np.tile(sin, (1, 2)).astype(np.float32)]
    return out


def turn(x, cos, sin, even):
    swapped = jnp.where(even, pltpu.roll(x, 127, 1), pltpu.roll(x, 1, 1))
    return x * cos + swapped * sin


def even_lanes(rows):
    return lax.broadcasted_iota(jnp.int32, (rows, 128), 1) % 2 == 0


def full(shape):
    return pl.BlockSpec(shape, lambda *_: (0,) * len(shape), pipeline_mode=pl.Buffered(1))


def mod_kernel(te_ref, w_ref, b_ref, out_ref):
    t = te_ref[...].astype(f32)
    embed = (t * jax.nn.sigmoid(t)).astype(bf16)
    embed = jnp.broadcast_to(embed, (8, embed.shape[1]))
    out_ref[...] = mm(embed, w_ref[...], NN)[:1] + b_ref[...].astype(f32)


def modulation(te, w, b):
    d, n = w.shape
    blk = d
    return pl.pallas_call(
        mod_kernel,
        grid=(n // blk,),
        in_specs=[full((1, d)), pl.BlockSpec((d, blk), lambda i: (0, i)), pl.BlockSpec((1, blk), lambda i: (0, i))],
        out_specs=pl.BlockSpec((1, blk), lambda i: (0, i)),
        out_shape=jax.ShapeDtypeStruct((1, n), f32),
        compiler_params=params(),
        name="modulation",
    )(te, w, b)


def qkv_kernel(x_ref, mod_ref, w_ref, b_ref, cosa_ref, sina_ref, cosb_ref, sinb_ref, h_ref, qkv_ref, cos_ref, sin_ref):
    d = x_ref.shape[1]
    x = x_ref[...].astype(f32)
    c = x - jnp.mean(x, axis=1, keepdims=True)
    r = lax.rsqrt(jnp.mean(c * c, axis=1, keepdims=True) + EPS)
    h = (c * r * (1.0 + mod_ref[:, d : 2 * d]) + mod_ref[:, :d]).astype(bf16)
    h_ref[...] = h
    cosb, sinb = cosb_ref[...], sinb_ref[...]
    for k in range(x.shape[0] // BLOCK):
        cosa, sina = cosa_ref[k : k + 1, :], sina_ref[k : k + 1, :]
        cos_ref[k * BLOCK : (k + 1) * BLOCK, :] = cosa * cosb - sina * sinb
        sin_ref[k * BLOCK : (k + 1) * BLOCK, :] = sina * cosb + cosa * sinb
    cos, sin = cos_ref[...], sin_ref[...]
    even = even_lanes(x.shape[0])
    step = 512
    for n in range(0, 3 * d, step):
        y = mm(h, w_ref[:, n : n + step], NN) + b_ref[:, n : n + step].astype(f32)
        for t in range(0, step, 128):
            col = n + t
            z = y[:, t : t + 128]
            if col < 2 * d:
                z = turn(z, cos, sin, even)
            if col < d:
                z = z * 0.125
            qkv_ref[:, col : col + 128] = z.astype(bf16)


def project_qkv(x, mod, w, b, tables, tile=256):
    slots, d = x.shape
    row = lambda n: pl.BlockSpec((tile, n), lambda i: (i, 0))
    return pl.pallas_call(
        qkv_kernel,
        grid=(slots // tile,),
        in_specs=[row(d), full(mod.shape), full(w.shape), full(b.shape)]
        + [pl.BlockSpec((tile // BLOCK, 128), lambda i: (i, 0))] * 2 + [full((BLOCK, 128))] * 2,
        out_specs=[row(d), row(3 * d), row(128), row(128)],
        out_shape=[jax.ShapeDtypeStruct((slots, d), bf16), jax.ShapeDtypeStruct((slots, 3 * d), bf16),
                   jax.ShapeDtypeStruct((slots, 128), f32), jax.ShapeDtypeStruct((slots, 128), f32)],
        compiler_params=params(),
        name="project_qkv",
    )(x, mod, w, b, *tables)


def attend_kernel(len_ref, q_ref, k_ref, v_ref, o_ref, e_ref, linv_ref, *, rows_at_once):
    slots = q_ref.shape[0]
    lane = lax.broadcasted_iota(jnp.int32, (1, 128), 1)
    ones = jnp.where(lax.broadcasted_iota(jnp.int32, (slots, 128), 1) == 0, 1.0, 0.0).astype(bf16)
    k = k_ref[...]
    v = jnp.concatenate([v_ref[...], ones], axis=1)
    valid = lax.broadcasted_iota(jnp.int32, (1, slots), 1) < len_ref[0]
    for at in range(0, slots, rows_at_once):
        rows = pl.ds(at, rows_at_once)
        q = q_ref[rows, :]
        outs, invs = [], []
        for h in range(2):
            qh = jnp.where(lane < 64 if h == 0 else lane >= 64, q, jnp.zeros_like(q))
            s = jnp.where(valid, mm(qh, k, NT), -1e30)
            m = jnp.max(s, axis=1, keepdims=True)
            e = jnp.exp2((s - m) * LOG2E).astype(bf16)
            e_ref[h, rows, :] = e
            r = mm(e, v, NN)
            inv = 1.0 / r[:, 128:129]
            outs.append(r[:, :128] * inv)
            invs.append(inv)
        o_ref[rows, :] = jnp.where(lane < 64, outs[0], outs[1]).astype(bf16)
        linv_ref[rows, :] = jnp.where(lane < 64, invs[0], invs[1])


def attend(length, qkv, rows_at_once=128):
    slots, d = qkv.shape[0], qkv.shape[1] // 3
    pairs = d // 128
    col = lambda off: pl.BlockSpec((slots, 128), lambda i, n: (0, off + i))
    return pl.pallas_call(
        lambda *a: attend_kernel(*a, rows_at_once=rows_at_once),
        grid_spec=pltpu.PrefetchScalarGridSpec(
            num_scalar_prefetch=1,
            grid=(pairs,),
            in_specs=[col(0), col(pairs), col(2 * pairs)],
            out_specs=[col(0), pl.BlockSpec((2, slots, slots), lambda i, n: (i, 0, 0)), col(0)],
        ),
        out_shape=[
            jax.ShapeDtypeStruct((slots, d), bf16),
            jax.ShapeDtypeStruct((2 * pairs, slots, slots), bf16),
            jax.ShapeDtypeStruct((slots, d), f32),
        ],
        compiler_params=params(),
        name="attend",
    )(length, qkv, qkv, qkv)


def middle_kernel(
    len_ref, mixed_ref, x_ref, cot_ref, mod_ref, linv_ref, ow_ref, ob_ref, uw_ref, ub_ref, dw_ref, db_ref,
    out_ref, h2_ref, act_ref, dbr_ref, dup_ref, dat_ref, dmix_ref, dmid_ref, dmod_ref,
):
    i = pl.program_id(0)
    tile, d = x_ref.shape
    mod = lambda k: mod_ref[:, k * d : (k + 1) * d]
    gate1, shift2, scale2, gate2 = mod(2), mod(3), mod(4), mod(5)
    slot = lax.broadcasted_iota(jnp.int32, (tile, 1), 0) + i * tile
    valid = slot < len_ref[0]
    attn = jnp.where(valid, mm(mixed_ref[...], ow_ref[...], NN) + ob_ref[...].astype(f32), 0.0)
    mid = x_ref[...].astype(f32) + gate1 * attn
    c = mid - jnp.mean(mid, axis=1, keepdims=True)
    r2 = lax.rsqrt(jnp.mean(c * c, axis=1, keepdims=True) + EPS)
    n2 = c * r2
    h2 = (n2 * (1.0 + scale2) + shift2).astype(bf16)
    h2_ref[...] = h2
    cot = cot_ref[...].astype(f32)
    dbr = (gate2 * cot).astype(bf16)
    dbr_ref[...] = dbr
    ff = uw_ref.shape[1]
    step = 512
    for n in range(0, ff, step):
        u = mm(h2, uw_ref[:, n : n + step], NN) + ub_ref[:, n : n + step].astype(f32)
        c0 = 0.7978845608028654
        th = jnp.tanh(c0 * (u + 0.044715 * u * u * u))
        half = 0.5 * (1.0 + th)
        act_ref[:, n : n + step] = (u * half).astype(bf16)
        grad = half + 0.5 * u * (1.0 - th * th) * (c0 * (1.0 + 3.0 * 0.044715 * u * u))
        da = mm(dbr, dw_ref[n : n + step, :], NT)
        dup_ref[:, n : n + step] = (da * grad).astype(bf16)
    branch = mm(act_ref[...], dw_ref[...], NN) + db_ref[...].astype(f32)
    out_ref[...] = (mid + gate2 * branch).astype(bf16)
    dgate2 = jnp.sum(cot * branch, axis=0, keepdims=True)
    dh2 = mm(dup_ref[...], uw_ref[...], NT)
    dscale2 = jnp.sum(dh2 * n2, axis=0, keepdims=True)
    dshift2 = jnp.sum(dh2, axis=0, keepdims=True)
    dn2 = dh2 * (1.0 + scale2)
    dmid = cot + r2 * (
        dn2 - jnp.mean(dn2, axis=1, keepdims=True) - n2 * jnp.mean(dn2 * n2, axis=1, keepdims=True)
    )
    dmid_ref[...] = dmid
    dgate1 = jnp.sum(dmid * attn, axis=0, keepdims=True)
    dat = jnp.where(valid, gate1 * dmid, 0.0).astype(bf16)
    dat_ref[...] = dat
    dmix_ref[...] = (mm(dat, ow_ref[...], NT) * linv_ref[...]).astype(bf16)
    part = jnp.concatenate([dgate1, dshift2, dscale2, dgate2], axis=1)

    @pl.when(i == 0)
    def _():
        dmod_ref[...] = part

    @pl.when(i > 0)
    def _():
        dmod_ref[...] += part


def middle_part(length, mixed, x, cot, mod, linv, ow, ob, uw, ub, dw, db, tile=256):
    slots, d = x.shape
    ff = uw.shape[1]
    row = lambda n: pl.BlockSpec((tile, n), lambda i, n_: (i, 0))
    S = jax.ShapeDtypeStruct
    return pl.pallas_call(
        middle_kernel,
        grid_spec=pltpu.PrefetchScalarGridSpec(
            num_scalar_prefetch=1,
            grid=(slots // tile,),
            in_specs=[row(d), row(d), row(d), full(mod.shape), row(d), full(ow.shape), full(ob.shape),
                      full(uw.shape), full(ub.shape), full(dw.shape), full(db.shape)],
            out_specs=[row(d), row(d), row(ff), row(d), row(ff), row(d), row(d), row(d),
                       pl.BlockSpec((1, 4 * d), lambda i, n_: (0, 0))],
        ),
        out_shape=[S((slots, d), bf16), S((slots, d), bf16), S((slots, ff), bf16), S((slots, d), bf16),
                   S((slots, ff), bf16), S((slots, d), bf16), S((slots, d), bf16), S((slots, d), f32),
                   S((1, 4 * d), f32)],
        compiler_params=params(),
        name="middle_part",
    )(length, mixed, x, cot, mod, linv, ow, ob, uw, ub, dw, db)


MESH = pl.DeviceIdType.MESH
STRIP = 512
RINGS = dict(r0=4, r1=6, r2=6, r3=4)
DELAYS = (0, 1, 3, 5, 7, 8)


class Exchange:
    def __init__(self, groups, batch, own, s, sems, ready, chunks):
        self.G, self.B, self.H, self.chunks = groups, batch, groups // 4, chunks
        self.plan = []
        while len(self.plan) - self.plan.count(None) < chunks:
            n = len(self.plan) - self.plan.count(None)
            self.plan.append(n if len(self.plan) >= len(ready) or n < ready[len(self.plan)] else None)
        self.gaps = [t for t, c in enumerate(self.plan) if c is None]
        self.last = len(self.plan) - 1 + DELAYS[-1]
        self.own = own
        self.s = s
        self.send, self.recv = sems
        g, c = lax.axis_index("groups"), lax.axis_index("batch")
        self.c, self.x, self.y, self.z = c, g % 2, (g // 2) % 2, g // 4
        x, y, z, H, B = self.x, self.y, self.z, self.H, self.B
        pos = lambda z_, y_, x_: z_ * 4 + y_ * 2 + x_
        self.cores = [(g, (c + k) % B) for k in range(1, B)]
        self.across_x = (pos(z, y, 1 - x), c)
        self.across_y = (pos(z, 1 - y, x), c)
        self.across_z = [(pos((z + k) % H, y, x), c) for k in range(1, H)]

    @staticmethod
    def sems_per_chunk(groups, batch):
        return 2 * (batch - 1) + 4 + (groups // 4 - 1)

    def barrier(self):
        sem = pltpu.get_barrier_semaphore()
        peers = self.cores + [self.across_x, self.across_y] + self.across_z
        for p in peers:
            pl.semaphore_signal(sem, inc=1, device_id=p, device_id_type=MESH)
        pl.semaphore_wait(sem, len(peers))

    def copy(self, j, n, src, dst, peer):
        return pltpu.make_async_remote_copy(
            src_ref=src, dst_ref=dst, send_sem=self.send.at[j, n], recv_sem=self.recv.at[j, n],
            device_id=peer, device_id_type=MESH,
        )

    def copies(self, j, phase):
        B, H, x, y = self.B, self.H, self.x, self.y
        s = self.s
        rows, width = s["r0"].shape[-2:]
        half = rows // 2
        q0, q1, q2, q3 = (j % RINGS[k] for k in ("r0", "r1", "r2", "r3"))
        if phase == 0:
            out = []
            for k, p in enumerate(self.cores):
                cols = pl.ds(pl.multiple_of(p[1] * width, width), width)
                out.append(self.copy(j, k, self.own(j).at[:, :, :, :, cols], s["r0"].at[q0, k], p))
            return out
        n = B - 1
        if phase == 1:
            total = s["r0"].at[q0, 0]
            return [
                self.copy(j, n, total.at[:, :, 1 - x, :half], s["r1"].at[q1, 0], self.across_x),
                self.copy(j, n + 1, total.at[:, 1 - y, :, half:], s["r1"].at[q1, 1], self.across_y),
            ]
        if phase == 2:
            return [
                self.copy(j, n + 2, s["r1"].at[q1, 0, :, 1 - y], s["r2"].at[q2, :, :half], self.across_y),
                self.copy(j, n + 3, s["r1"].at[q1, 1, :, 1 - x], s["r2"].at[q2, :, half:], self.across_x),
            ]
        n += 4
        if phase == 3:
            return [
                self.copy(j, n + k, s["r2"].at[q2, p[0] // 4], s["r3"].at[q3, k], p)
                for k, p in enumerate(self.across_z)
            ]
        n += H - 1
        cols = pl.ds(pl.multiple_of(self.c * width, width), width)
        place = s["out"].at[j, :, cols]
        return [self.copy(j, n + k, place, place, p) for k, p in enumerate(self.cores)]

    def start(self, j, phase):
        for d in self.copies(j, phase):
            d.start()

    def finish(self, j, phase):
        for d in self.copies(j, phase):
            d.wait()
        s, x, y, z, H = self.s, self.x, self.y, self.z, self.H
        rows, width = s["r0"].shape[-2:]
        half = rows // 2
        q0, q1, q2, q3 = (j % RINGS[k] for k in ("r0", "r1", "r2", "r3"))
        cols = pl.ds(pl.multiple_of(self.c * width, width), width)
        if phase == 0:
            own = self.own(j)

            def add(h, _):
                t = own[h, :, :, :, cols]
                if self.B == 2:
                    t = t + s["r0"][q0, 0, h]
                else:
                    t = t.astype(f32)
                    for k in range(self.B - 1):
                        t = t + s["r0"][q0, k, h].astype(f32)
                s["r0"][q0, 0, h] = t.astype(bf16)
                return _

            lax.fori_loop(0, H, add, 0)
        elif phase == 1:

            def add(h, _):
                s["r1"][q1, 0, h] = s["r1"][q1, 0, h] + s["r0"][q0, 0, h, :, x, :half]
                s["r1"][q1, 1, h] = s["r1"][q1, 1, h] + s["r0"][q0, 0, h, y, :, half:]
                return _

            lax.fori_loop(0, H, add, 0)
        elif phase == 2:
            s["r2"][q2, :, :half] = s["r2"][q2, :, :half] + s["r1"][q1, 0, :, y]
            s["r2"][q2, :, half:] = s["r2"][q2, :, half:] + s["r1"][q1, 1, :, x]
        elif phase == 3:
            t = s["r2"][q2, z].astype(f32)
            for k in range(H - 1):
                t = t + s["r3"][q3, k].astype(f32)
            s["out"][j, :, cols] = t

    @staticmethod
    def scratch(groups, batch, chunks, rows, cols):
        H, w = groups // 4, cols // batch
        return dict(
            r0=pltpu.VMEM((RINGS["r0"], batch - 1, H, 2, 2, rows, w), bf16),
            r1=pltpu.VMEM((RINGS["r1"], 2, H, 2, rows // 2, w), bf16),
            r2=pltpu.VMEM((RINGS["r2"], H, rows, w), bf16),
            r3=pltpu.VMEM((RINGS["r3"], H - 1, rows, w), bf16),
            out=pltpu.VMEM((chunks, rows, cols), f32),
        )

    def tick(self, t, first=None, final=None):
        static = isinstance(t, int)
        if static:
            first = final = t
        n = len(self.plan)
        for phase in range(5, -1, -1):
            lo, hi = first - DELAYS[phase], final - DELAYS[phase]
            j = t - DELAYS[phase]
            if hi < 0 or lo >= n or (static and self.plan[j] is None):
                continue

            def act(phase=phase, j=j):
                c = self.plan[j] if static else j
                if not static:
                    for g in self.gaps:
                        if g < lo:
                            c = c - 1
                        elif g <= hi:
                            c = c - jnp.where(j > g, 1, 0)
                if phase > 0:
                    self.finish(c, phase - 1)
                if phase < 5:
                    self.start(c, phase)

            conds = []
            if lo < 0:
                conds.append(j >= 0)
            if hi >= n:
                conds.append(j < n)
            conds += [j != g for g in self.gaps if lo <= g <= hi]
            if static or not conds:
                act()
            else:
                ok = conds[0]
                for c in conds[1:]:
                    ok = jnp.logical_and(ok, c)
                pl.when(ok)(act)


class Small:
    def __init__(self, ex, sems, total=None, mine=None, seen=None):
        self.ex, self.total, self.mine, self.seen = ex, total, mine, seen
        self.send, self.recv = sems

    @staticmethod
    def count(groups, batch):
        return batch - 1 + 2 + groups // 4 - 1

    def copies(self, phase):
        ex = self.ex
        peers = [ex.cores, [ex.across_x], [ex.across_y], ex.across_z][phase]
        first = [0, ex.B - 1, ex.B, ex.B + 1][phase]
        out = []
        for k, p in enumerate(peers):
            n = first + k
            if self.seen is None:
                src, dst = self.mine.at[phase], self.total.at[n]
            else:
                at = (ex.z, ex.y, ex.x, ex.c)[: 4 - phase]
                src = dst = self.seen.at[at]
            out.append(pltpu.make_async_remote_copy(
                src_ref=src, dst_ref=dst, send_sem=self.send.at[n], recv_sem=self.recv.at[n],
                device_id=p, device_id_type=MESH))
        return out

    def start(self, phase):
        for d in self.copies(phase):
            d.start()

    def finish(self, phase):
        for d in self.copies(phase):
            d.wait()
        if self.seen is None:
            ex = self.ex
            n = [ex.B - 1, 1, 1, ex.H - 1][phase]
            first = [0, ex.B - 1, ex.B, ex.B + 1][phase]
            t = self.mine[phase]
            for k in range(n):
                t = t + self.total[first + k]
            self.mine[phase + 1] = t


def back_kernel(groups, batch, per, n_chunks, *refs):
    (act_hbm, dbr_hbm, h2_hbm, dup_hbm, mixed_hbm, dat_hbm, dmix_hbm, qkv_hbm, e_hbm, h1_hbm, w_hbm, x_hbm, dmid_hbm, mw_hbm,
     cos_ref, sin_ref, mod_ref, dmodb_ref, te_ref,
     dwo, uwo, owo, qwo, bias_out, early_out, late_out, fg_hbm, tg_ref,
     own, r0, r1, r2, r3, out, total, mine, early, late, etmp, ltmp,
     ebuf, dsb, qkv, mixed, dmix, dbr, h2, dat, dmid, fg, dmoda_ref,
     send, recv, ssum, rsum, sear, rear, slat, rlat, ld, eld, dld, fst, ost, mld) = refs
    slots, d = mixed.shape
    H, rows = groups // 4, d // groups
    chunk = lambda strip: strip // per
    n_own = own.shape[0]
    pairs = d // 128
    first, second = pairs // 2, pairs - 1
    ready = [4, 6, 8, 10, 10] + [10] * first + [13] * (second - first + 1) + [15] * (1 + pairs - second) + [16]
    ex = Exchange(groups, batch, lambda j: own.at[j % n_own], dict(r0=r0, r1=r1, r2=r2, r3=r3, out=out), (send, recv),
                  [n // per for n in ready], n_chunks)
    sums = Small(ex, (ssum, rsum), total=total, mine=mine)
    gather_early = Small(ex, (sear, rear), seen=early)
    gather_late = Small(ex, (slat, rlat), seen=late)

    load = lambda k, src, dst: pltpu.make_async_copy(src, dst, ld.at[k])
    half = lambda ref, k: ref.at[:, k * d : (k + 1) * d]
    loads = [
        load(0, half(act_hbm, 0), ebuf.at[1, 0]), load(1, half(act_hbm, 1), ebuf.at[1, 1]), load(2, dbr_hbm, dbr),
        load(3, h2_hbm, h2), load(4, half(dup_hbm, 0), dsb.at[0]), load(5, half(dup_hbm, 1), dsb.at[1]),
        load(6, mixed_hbm, mixed), load(7, dat_hbm, dat), load(8, qkv_hbm, qkv), load(9, dmix_hbm, dmix),
    ]
    load_h1 = load(10, h1_hbm, h2)
    load_w = [load(11 + k, half(w_hbm, k), ebuf.at[k // 2, k % 2]) for k in range(3)]
    load_x = load(14, x_hbm, dat)
    free = [mixed, dmix, dbr, dsb.at[0], dsb.at[1], ebuf.at[1, 1]]
    load_m = [pltpu.make_async_copy(half(mw_hbm, k), free[k], mld.at[k]) for k in range(6)]
    load_e = lambda p, slot: pltpu.make_async_copy(e_hbm.at[pl.ds(2 * p, 2)], ebuf.at[slot], eld.at[slot])
    for t in loads[:3]:
        t.start()

    for k in range(4 * d // STRIP):
        etmp[k : k + 1, :] = dmodb_ref[:, k * STRIP : (k + 1) * STRIP]
    t = te_ref[...].astype(f32)
    t = t * jax.nn.sigmoid(t)
    at = 4 * d // STRIP
    for k in range(d // STRIP):
        etmp[at + k : at + k + 1, :] = t[:, k * STRIP : (k + 1) * STRIP]
    at += d // STRIP
    etmp[at:, :] = jnp.zeros((etmp.shape[0] - at, STRIP), f32)
    early[ex.z, ex.y, ex.x, ex.c] = etmp[...].astype(bf16)
    mine[0] = jnp.zeros(mine.shape[1:], f32)
    ex.barrier()
    gather_early.start(0)

    def column_sums(value, row, k):
        mine[0, pl.ds(row + k, 1), :] = jnp.sum(value.astype(f32), axis=0, keepdims=True)

    def wgrad_into(left, block_rows, rights, place, zs):
        parts = block_rows // rows

        def body(i, _):
            n = zs * 4 * block_rows
            lt = left(i * n, n).T
            for k, right in enumerate(rights):
                r = mm(lt, right(), NN).astype(bf16)
                for b in range(4 * zs):
                    for part in range(parts):
                        strip = place(k, part)
                        lo = b * block_rows + part * rows
                        off = (strip % per) * STRIP
                        cols = pl.ds(off if isinstance(off, int) else pl.multiple_of(off, STRIP), STRIP)
                        own[chunk(strip) % n_own, i * zs + b // 4, (b // 2) % 2, b % 2, :, cols] = r[lo : lo + rows]
            return _

        lax.fori_loop(0, H // zs, body, 0)

    for k in (0, 1, 2):
        loads[k].wait()
    for k in (3, 4, 5, 6, 7):
        loads[k].start()
    wide = lambda ref: lambda lo, n: ref[lo // d, :, pl.ds(pl.multiple_of(lo % d, 128), n)]
    flat = lambda ref: lambda lo, n: ref[:, pl.ds(pl.multiple_of(lo, 128), n)]
    strip_at = lambda k: pl.ds(k * STRIP if isinstance(k, int) else pl.multiple_of(k * STRIP, STRIP), STRIP)
    cut = lambda ref, k: lambda: ref[:, strip_at(k)]
    wgrad_into(wide(ebuf.at[1]), 2 * rows, [cut(dbr, k) for k in range(2)], lambda k, part: 2 * k + part, 2)
    for k in range(2):
        column_sums(cut(dbr, k)(), 12, k)
    gather_early.finish(0)
    gather_early.start(1)
    ex.tick(0)
    for k in (3, 4, 5):
        loads[k].wait()
    for k in (8, 9):
        loads[k].start()
    load_e(0, 0).start()
    for h in range(2):
        wgrad_into(flat(h2), rows, [cut(dsb.at[h], k) for k in range(2)], lambda k, part: 4 + 2 * h + k, 2)
        for k in range(2):
            column_sums(cut(dsb.at[h], k)(), 8 + 2 * h, k)
        if h == 0:
            gather_early.finish(1)
            gather_early.start(2)
        ex.tick(1 + h)
    load_h1.start()
    for k in (6, 7):
        loads[k].wait()
    wgrad_into(flat(mixed), rows, [cut(dat, k) for k in range(2)], lambda k, part: 8 + k, 2)
    for k in range(2):
        column_sums(cut(dat, k)(), 6, k)
    gather_early.finish(2)
    gather_early.start(3)
    load_x.start()
    ex.tick(3)
    ex.tick(4)
    for k in (8, 9):
        loads[k].wait()
    gather_early.finish(3)
    lane = lax.broadcasted_iota(jnp.int32, (1, 128), 1)
    even = even_lanes(slots)
    at_once = 256

    def attention(p, slot):
        col = lambda off: pl.ds(pl.multiple_of(off + p * 128, 128), 128)
        qc, kc, vc = col(0), col(d), col(2 * d)
        q, k, v, do = qkv[:, qc], qkv[:, kc], qkv[:, vc], dmix[:, qc]
        dqs = []
        for h in range(2):
            own_lanes = lane < 64 if h == 0 else lane >= 64
            parts = []
            for a in range(0, slots, at_once):
                rws = pl.ds(a, at_once)
                t = dmix[rws, qc]
                t = jnp.where(own_lanes, t, jnp.zeros_like(t))
                inner = jnp.sum(t.astype(f32) * mixed[rws, qc].astype(f32), axis=1, keepdims=True)
                ds = ebuf[slot, h, rws, :] * (mm(t, v, NT) - inner).astype(bf16)
                dsb[h, rws, :] = ds
                parts.append(mm(ds, k, NN))
            dqs.append(jnp.concatenate(parts, axis=0))
        do_t, q_t = do.T, q.T
        dv = jnp.concatenate([mm(do_t[h * 64 : h * 64 + 64], ebuf[slot, h], NN) for h in range(2)], axis=0)
        dk = jnp.concatenate([mm(q_t[h * 64 : h * 64 + 64], dsb[h], NN) for h in range(2)], axis=0)
        cos, sin = cos_ref[...], -sin_ref[...]
        dq = jnp.where(lane < 64, dqs[0], dqs[1]) * 0.125
        qkv[:, qc] = turn(dq, cos, sin, even).astype(bf16)
        qkv[:, kc] = turn(dk.T, cos, sin, even).astype(bf16)
        qkv[:, vc] = dv.T.astype(bf16)

    def qkv_grad(rights, places):
        zs = 2

        def body(i, carry):
            n = zs * 4 * rows
            lt = h2[:, pl.ds(pl.multiple_of(i * n, 128), n)].T
            for right, where in zip(rights, places):
                r = mm(lt, right(), NN).astype(bf16)
                for c, (strip, at) in enumerate(where):
                    lo = (strip % per) * STRIP + at * 128
                    for b in range(4 * zs):
                        own[chunk(strip) % n_own, i * zs + b // 4, (b // 2) % 2, b % 2, :, lo : lo + 128] = (
                            r[b * rows : (b + 1) * rows, c * 128 : (c + 1) * 128]
                        )
            return carry

        lax.fori_loop(0, H // zs, body, 0)

    span = lambda k, lo, hi: lambda: qkv[:, k * d + lo * 128 : k * d + hi * 128]
    late_cols = [(k, p) for k in range(3) for p in range(first, second)] + [(k, p) for k in range(3) for p in range(second, pairs)]
    late_place = {kp: (13 + n // 4, n % 4) for n, kp in enumerate(late_cols)}
    t1 = 5 + first

    def heads(p, carry):
        slot = p % 2
        load_e(p, slot).wait()

        @pl.when(p + 1 < pairs)
        def _():
            load_e(p + 1, 1 - slot).start()

        attention(p, slot)
        ex.tick(5 + p + jnp.where(p >= first, 1, 0) + jnp.where(p >= second, 1, 0), 5, 6 + pairs)

        @pl.when(p == first - 1)
        def _():
            load_h1.wait()
            qkv_grad([cut(qkv, 2 * k) for k in range(3)], [[(10 + k, c) for c in range(4)] for k in range(3)])
            for k in range(3):
                column_sums(cut(qkv, 2 * k)(), 2 * k, 0)
            ex.tick(t1)

        @pl.when(p == second - 1)
        def _():
            qkv_grad([span(k, first, second) for k in range(3)],
                     [[late_place[k, q] for q in range(first, second)] for k in range(3)])
            ex.tick(1 + 5 + second)

        return carry

    lax.fori_loop(0, pairs, heads, 0)
    for t in load_w:
        t.start()
    qkv_grad([lambda: jnp.concatenate([span(k, second, pairs)() for k in range(3)], axis=1)],
             [[late_place[k, q] for k in range(3) for q in range(second, pairs)]])
    t0 = 8 + pairs
    ex.tick(t0 - 1)
    for k in range(3):
        column_sums(cut(qkv, 2 * k + 1)(), 2 * k + 1, 0)
    sums.start(0)
    tile = dmid.shape[1]
    tiles = slots // tile
    row_tile = lambda i: pl.ds(pl.multiple_of(i * tile, tile), tile)
    load_d = lambda i, slot: pltpu.make_async_copy(dmid_hbm.at[row_tile(i)], dmid.at[slot], dld.at[slot])
    store_f = lambda i, slot: pltpu.make_async_copy(fg.at[slot], fg_hbm.at[row_tile(i)], fst.at[slot])
    load_d(0, 0).start()
    load_x.wait()
    for t in load_w:
        t.wait()
    for t in load_m:
        t.start()
    dmoda_ref[...] = jnp.zeros_like(dmoda_ref)
    def front(i, carry):
        slot = i % 2

        @pl.when(i + 1 < tiles)
        def _():
            load_d(i + 1, 1 - slot).start()

        rws = row_tile(i)
        dh = (
            mm(qkv[rws, :d], ebuf[0, 0], NT) + mm(qkv[rws, d : 2 * d], ebuf[0, 1], NT) + mm(qkv[rws, 2 * d :], ebuf[1, 0], NT)
        )
        ex.tick(t0 + 2 * i, t0, t0 + 2 * tiles - 2)
        x = dat[rws, :].astype(f32)
        cen = x - jnp.mean(x, axis=1, keepdims=True)
        r = lax.rsqrt(jnp.mean(cen * cen, axis=1, keepdims=True) + EPS)
        n1 = cen * r
        dmoda_ref[:, :d] += jnp.sum(dh, axis=0, keepdims=True)
        dmoda_ref[:, d:] += jnp.sum(dh * n1, axis=0, keepdims=True)
        dn = dh * (1.0 + mod_ref[:, d : 2 * d])
        load_d(i, slot).wait()

        @pl.when(i >= 2)
        def _():
            store_f(i - 2, slot).wait()

        fg[slot] = dmid[slot] + r * (
            dn - jnp.mean(dn, axis=1, keepdims=True) - n1 * jnp.mean(dn * n1, axis=1, keepdims=True)
        )
        store_f(i, slot).start()
        for phase in range(3):

            @pl.when(i == phase)
            def _():
                sums.finish(phase)
                sums.start(phase + 1)

        ex.tick(t0 + 2 * i + 1, t0 + 1, t0 + 2 * tiles - 1)
        return carry

    lax.fori_loop(0, tiles, front, 0)
    for k in range(2 * d // 128):
        ltmp[k : k + 1, :] = dmoda_ref[:, k * 128 : (k + 1) * 128]
    late[ex.z, ex.y, ex.x, ex.c] = ltmp[...].astype(bf16)
    gather_late.start(0)
    sums.finish(3)

    def through_mod(k):
        load_m[k].wait()
        v = dmoda_ref[:, k * d : (k + 1) * d] if k < 2 else dmodb_ref[:, (k - 2) * d : (k - 1) * d]
        v = jnp.broadcast_to(v, (8, d)).astype(bf16)
        tg_ref[...] += mm(v, free[k][...], NT)[:1]

    pieces = [(2 * k + part, 0, dwo.at[part, :, k * STRIP : (k + 1) * STRIP]) for k in range(2) for part in range(2)]
    pieces += [(4 + k, 0, uwo.at[:, k * STRIP : (k + 1) * STRIP]) for k in range(4)]
    pieces += [(8 + k, 0, owo.at[:, k * STRIP : (k + 1) * STRIP]) for k in range(2)]
    pieces += [(10 + k, 0, qwo.at[:, k * d : k * d + STRIP]) for k in range(3)]
    for (k, p), (strip, at) in late_place.items():
        pieces.append((strip, at * 128, qwo.at[:, k * d + p * 128 : k * d + (p + 1) * 128]))
    stores = [pltpu.make_async_copy(early, early_out, ost.at[0])]
    for n, (strip, off, dst) in enumerate(pieces):
        off += (strip % per) * STRIP
        stores.append(pltpu.make_async_copy(out.at[chunk(strip), :, off : off + dst.shape[1]], dst, ost.at[n + 1]))

    def start_stores():
        for c in stores:
            c.start()

    tg_ref[...] = jnp.zeros_like(tg_ref)
    t = t0 + 2 * tiles
    stored = t > ex.last
    if stored:
        start_stores()
    for phase in range(4):
        through_mod(phase)
        if t <= ex.last:
            ex.tick(t)
            t += 1
        gather_late.finish(phase)
        if phase < 3:
            gather_late.start(phase + 1)
    through_mod(4)
    through_mod(5)
    for k in range(mine.shape[1]):
        for c in range(STRIP // 128):
            at = k * (STRIP // 128) + c
            bias_out[at : at + 1, :] = mine[4, k : k + 1, c * 128 : (c + 1) * 128]
    for i in range(max(0, tiles - 2), tiles):
        store_f(i, i % 2).wait()
    while t <= ex.last:
        ex.tick(t)
        t += 1
    if not stored:
        start_stores()
    late_store = pltpu.make_async_copy(late, late_out, ost.at[len(stores)])
    late_store.start()
    for c in stores:
        c.wait()
    late_store.wait()


def backward(groups, batch, act, dbr, h2, dup, mixed, dat, dmix, qkv, e, h1, w, x, dmid, mw, cos, sin, mod, dmodb, te):
    slots, d = mixed.shape
    H, rows = groups // 4, d // groups
    per = max(1, 128 * batch // STRIP)
    n_chunks = 16 // per
    S = jax.ShapeDtypeStruct
    hbm = pl.BlockSpec(memory_space=pl.ANY)
    vm = pl.BlockSpec(memory_space=pltpu.VMEM)
    V = pltpu.VMEM
    sc = Exchange.scratch(groups, batch, n_chunks, rows, per * STRIP)
    ns, nsm = Exchange.sems_per_chunk(groups, batch), Small.count(groups, batch)
    dma = pltpu.SemaphoreType.DMA
    tile = 256
    seen = (H, 2, 2, batch)
    return pl.pallas_call(
        lambda *a: back_kernel(groups, batch, per, n_chunks, *a),
        in_specs=[hbm] * 14 + [vm] * 5,
        out_specs=[hbm] * 4 + [vm, hbm, hbm, hbm, vm],
        out_shape=[S((2, rows, d), f32), S((rows, 2 * d), f32), S((rows, d), f32), S((rows, 3 * d), f32),
                   S((16 * STRIP // 128, 128), f32), S(seen + (16, STRIP), bf16), S(seen + (16, 128), bf16),
                   S((slots, d), f32), S((1, d), f32)],
        scratch_shapes=[V((-(-10 // per), H, 2, 2, rows, per * STRIP), bf16),
                        sc["r0"], sc["r1"], sc["r2"], sc["r3"], sc["out"],
                        V((nsm, 16, STRIP), f32), V((5, 16, STRIP), f32), V(seen + (16, STRIP), bf16), V(seen + (16, 128), bf16),
                        V((16, STRIP), f32), V((16, 128), f32),
                        V((2, 2, slots, slots), bf16), V((2, slots, slots), bf16), V((slots, 3 * d), bf16), V((slots, d), bf16),
                        V((slots, d), bf16), V((slots, d), bf16), V((slots, d), bf16), V((slots, d), bf16),
                        V((2, tile, d), f32), V((2, tile, d), f32), V((1, 2 * d), f32),
                        dma((n_chunks, ns)), dma((n_chunks, ns)), dma((nsm,)), dma((nsm,)), dma((nsm,)), dma((nsm,)),
                        dma((nsm,)), dma((nsm,)), dma((15,)), dma((2,)), dma((2,)), dma((2,)), dma((27,)), dma((6,))],
        compiler_params=pltpu.CompilerParams(vmem_limit_bytes=67_000_000, collective_id=0, has_side_effects=True),
        name="backward",
    )(act, dbr, h2, dup, mixed, dat, dmix, qkv, e, h1, w, x, dmid, mw, cos, sin, mod, dmodb, te)


def finish_kernel(early_ref, late_ref, bias_ref, tg_ref, te_ref, wg_ref, tout_ref, mb_ref, qb_ref, ob_ref, ub_ref, db_ref, flat):
    rows, d = wg_ref.shape[0], wg_ref.shape[1] // 6
    g = lax.axis_index("groups")
    e, late = early_ref[...], late_ref[...]
    n = e.shape[0] // 16
    at, off = 4 * d // STRIP + (g * rows) // STRIP, (g * rows) % STRIP
    pick = lax.broadcasted_iota(jnp.int32, (STRIP, 128), 0) - lax.broadcasted_iota(jnp.int32, (STRIP, 128), 1) == off
    em = mm(e, jnp.where(pick, 1.0, 0.0).astype(bf16), NN).reshape(n, 16, 128)
    em = jnp.where(lax.broadcasted_iota(jnp.int32, em.shape, 1) == at, em, 0.0)
    em = jnp.broadcast_to(jnp.sum(em, axis=1, keepdims=True), em.shape).reshape(n * 16, 128).T[:rows]
    row = lax.broadcasted_iota(jnp.int32, em.shape, 1) % 16
    for r in range(16):
        left = jnp.where(row == r, em, 0.0).astype(bf16)
        wg_ref[:, r * 128 : (r + 1) * 128] = mm(left, late, NN)
        if r < 4 * d // STRIP:
            lo = 2 * d + r * STRIP
            wg_ref[:, lo : lo + STRIP] = mm(left, e, NN)
    flat[:16, :] = jnp.sum(late.astype(f32).reshape(n, 16, 128), axis=0)
    es = jnp.sum(e.astype(f32).reshape(n, 16, STRIP), axis=0)
    for r in range(4 * d // STRIP):
        for c in range(STRIP // 128):
            k = 16 + r * (STRIP // 128) + c
            flat[k : k + 1, :] = es[r : r + 1, c * 128 : (c + 1) * 128]
    flat[48:, :] = jnp.zeros((flat.shape[0] - 48, 128), f32)
    lane = lax.broadcasted_iota(jnp.int32, (1, 128), 1)
    for ref, src, first in ((mb_ref, flat, 0), (qb_ref, bias_ref, 0), (ob_ref, bias_ref, 3 * d), (ub_ref, bias_ref, 4 * d), (db_ref, bias_ref, 6 * d)):
        width = ref.shape[1]
        at, off = first // 128 + (g * width) // 128, (g * width) % 128
        for k in range(-(-width // 128)):
            turned = [pltpu.roll(src[pl.ds(at + k + i, 1), :], (128 - off) % 128, 1) for i in range(2)]
            v = jnp.where(lane < 128 - off, turned[0], turned[1])
            w = min(128, width - k * 128)
            ref[:, k * 128 : k * 128 + w] = v[:, :w]
    t = te_ref[...].astype(f32)
    s = jax.nn.sigmoid(t)
    tout_ref[...] = tg_ref[...] * (s * (1.0 + t * (1.0 - s)))


def finish(early, late, bias, tg, te, rows):
    d = te.shape[1]
    S = jax.ShapeDtypeStruct
    return pl.pallas_call(
        finish_kernel,
        out_shape=[S((rows, 6 * d), f32), S((1, d), f32)] + [S((1, k * rows), f32) for k in (6, 3, 1, 2, 1)],
        scratch_shapes=[pltpu.VMEM((56, 128), f32)],
        compiler_params=params(),
        name="finish",
    )(early, late, bias, tg, te)


def solution(mesh):
    groups, batch = mesh.shape["groups"], mesh.shape["batch"]

    def body(frames, te, lengths, mod_w, mod_b, qkv_w, qkv_b, out_w, out_b, up_w, up_b, down_w, down_b, cot):
        x, ct = frames[0], cot[0]
        slots, d = x.shape
        row = lambda b: b.reshape(1, -1)
        mod = modulation(te, mod_w, row(mod_b))
        h1, qkv, cos, sin = project_qkv(x, mod, qkv_w, row(qkv_b), rot_tables(slots, d // HEADS))
        mixed, e, linv = attend(lengths, qkv)
        out, h2, act, dbr, dup, dat, dmix, dmid, dmod_b = middle_part(
            lengths, mixed, x, ct, mod, linv, out_w, row(out_b), up_w, row(up_b), down_w, row(down_b)
        )
        dws, uws, ows, qws, bs, early, late, fg, tg = backward(
            groups, batch, act, dbr, h2, dup, mixed, dat, dmix, qkv, e, h1, qkv_w, x, dmid, mod_w, cos, sin, mod, dmod_b, te
        )
        rows, n = d // groups, groups * batch
        mod_wg, time_grad, mb, qb, ob, ub, db = finish(early.reshape(n * 16, STRIP), late.reshape(n * 16, 128), bs, tg, te, rows)
        return (out[None], fg[None], time_grad, mod_wg, mb[0], qws, qb[0], ows, ob[0], uws, ub[0], dws.reshape(2 * rows, d), db[0])

    split = P(("groups", "batch"))
    own = P("groups")
    return jax.shard_map(
        body, mesh=mesh,
        in_specs=(split,) * 3 + (P(),) * 10 + (split,),
        out_specs=(split,) * 3 + (own,) * 10,
        check_vma=False,
    )
```

```python
import jax, jax.numpy as jnp
import numpy as np
from jax import lax
from jax.experimental import pallas as pl
from jax.experimental.pallas import tpu as pltpu
from jax.sharding import PartitionSpec as P

f32 = jnp.float32
bf16 = jnp.bfloat16
HEADS = 16
LOG2E = 1.4426950408889634
EPS = 1e-6
NN = ((1,), (0,))
NT = ((1,), (1,))
TN = ((0,), (0,))
VMEM_LIMIT = 62 * 2**20


def mm(a, b, dims):
    return lax.dot_general(a, b, (dims, ((), ())), preferred_element_type=f32)


def params(**kw):
    return pltpu.CompilerParams(vmem_limit_bytes=VMEM_LIMIT, **kw)


BLOCK = 32


def rot_tables(slots, size):
    pair = np.arange(size // 2, dtype=np.float64)[None, :]
    sign = np.where(np.arange(size) % 2 == 0, -1.0, 1.0)
    out = []
    for pos in (np.arange(0, slots, BLOCK), np.arange(BLOCK)):
        ang = pos.astype(np.float64)[:, None] * np.power(10000.0, -2.0 * pair / size)
        cos = np.repeat(np.cos(ang), 2, axis=1)
        sin = np.repeat(np.sin(ang), 2, axis=1) * sign
        out += [np.tile(cos, (1, 2)).astype(np.float32), np.tile(sin, (1, 2)).astype(np.float32)]
    return out


def turn(x, cos, sin, even):
    swapped = jnp.where(even, pltpu.roll(x, 127, 1), pltpu.roll(x, 1, 1))
    return x * cos + swapped * sin


def even_lanes(rows):
    return lax.broadcasted_iota(jnp.int32, (rows, 128), 1) % 2 == 0


def full(shape):
    return pl.BlockSpec(shape, lambda *_: (0,) * len(shape), pipeline_mode=pl.Buffered(1))


def mod_kernel(te_ref, w_ref, b_ref, out_ref):
    t = te_ref[...].astype(f32)
    embed = (t * jax.nn.sigmoid(t)).astype(bf16)
    embed = jnp.broadcast_to(embed, (8, embed.shape[1]))
    out_ref[...] = mm(embed, w_ref[...], NN)[:1] + b_ref[...].astype(f32)


def modulation(te, w, b):
    d, n = w.shape
    blk = d
    return pl.pallas_call(
        mod_kernel,
        grid=(n // blk,),
        in_specs=[full((1, d)), pl.BlockSpec((d, blk), lambda i: (0, i)), pl.BlockSpec((1, blk), lambda i: (0, i))],
        out_specs=pl.BlockSpec((1, blk), lambda i: (0, i)),
        out_shape=jax.ShapeDtypeStruct((1, n), f32),
        compiler_params=params(),
        name="modulation",
    )(te, w, b)


def qkv_kernel(x_ref, mod_ref, w_ref, b_ref, cosa_ref, sina_ref, cosb_ref, sinb_ref, h_ref, qkv_ref, cos_ref, sin_ref):
    d = x_ref.shape[1]
    x = x_ref[...].astype(f32)
    c = x - jnp.mean(x, axis=1, keepdims=True)
    r = lax.rsqrt(jnp.mean(c * c, axis=1, keepdims=True) + EPS)
    h = (c * r * (1.0 + mod_ref[:, d : 2 * d]) + mod_ref[:, :d]).astype(bf16)
    h_ref[...] = h
    cosb, sinb = cosb_ref[...], sinb_ref[...]
    for k in range(x.shape[0] // BLOCK):
        cosa, sina = cosa_ref[k : k + 1, :], sina_ref[k : k + 1, :]
        cos_ref[k * BLOCK : (k + 1) * BLOCK, :] = cosa * cosb - sina * sinb
        sin_ref[k * BLOCK : (k + 1) * BLOCK, :] = sina * cosb + cosa * sinb
    cos, sin = cos_ref[...], sin_ref[...]
    even = even_lanes(x.shape[0])
    step = 512
    for n in range(0, 3 * d, step):
        y = mm(h, w_ref[:, n : n + step], NN) + b_ref[:, n : n + step].astype(f32)
        for t in range(0, step, 128):
            col = n + t
            z = y[:, t : t + 128]
            if col < 2 * d:
                z = turn(z, cos, sin, even)
            if col < d:
                z = z * 0.125
            qkv_ref[:, col : col + 128] = z.astype(bf16)


def project_qkv(x, mod, w, b, tables, tile=256):
    slots, d = x.shape
    row = lambda n: pl.BlockSpec((tile, n), lambda i: (i, 0))
    return pl.pallas_call(
        qkv_kernel,
        grid=(slots // tile,),
        in_specs=[row(d), full(mod.shape), full(w.shape), full(b.shape)]
        + [pl.BlockSpec((tile // BLOCK, 128), lambda i: (i, 0))] * 2 + [full((BLOCK, 128))] * 2,
        out_specs=[row(d), row(3 * d), row(128), row(128)],
        out_shape=[jax.ShapeDtypeStruct((slots, d), bf16), jax.ShapeDtypeStruct((slots, 3 * d), bf16),
                   jax.ShapeDtypeStruct((slots, 128), f32), jax.ShapeDtypeStruct((slots, 128), f32)],
        compiler_params=params(),
        name="project_qkv",
    )(x, mod, w, b, *tables)


def attend_kernel(len_ref, q_ref, k_ref, v_ref, o_ref, e_ref, linv_ref, *, rows_at_once):
    slots = q_ref.shape[0]
    lane = lax.broadcasted_iota(jnp.int32, (1, 128), 1)
    ones = jnp.where(lax.broadcasted_iota(jnp.int32, (slots, 128), 1) == 0, 1.0, 0.0).astype(bf16)
    k = k_ref[...]
    v = jnp.concatenate([v_ref[...], ones], axis=1)
    valid = lax.broadcasted_iota(jnp.int32, (1, slots), 1) < len_ref[0]
    for at in range(0, slots, rows_at_once):
        rows = pl.ds(at, rows_at_once)
        q = q_ref[rows, :]
        outs, invs = [], []
        for h in range(2):
            qh = jnp.where(lane < 64 if h == 0 else lane >= 64, q, jnp.zeros_like(q))
            s = jnp.where(valid, mm(qh, k, NT), -1e30)
            m = jnp.max(s, axis=1, keepdims=True)
            e = jnp.exp2((s - m) * LOG2E).astype(bf16)
            e_ref[h, rows, :] = e
            r = mm(e, v, NN)
            inv = 1.0 / r[:, 128:129]
            outs.append(r[:, :128] * inv)
            invs.append(inv)
        o_ref[rows, :] = jnp.where(lane < 64, outs[0], outs[1]).astype(bf16)
        linv_ref[rows, :] = jnp.where(lane < 64, invs[0], invs[1])


def attend(length, qkv, rows_at_once=128):
    slots, d = qkv.shape[0], qkv.shape[1] // 3
    pairs = d // 128
    col = lambda off: pl.BlockSpec((slots, 128), lambda i, n: (0, off + i))
    return pl.pallas_call(
        lambda *a: attend_kernel(*a, rows_at_once=rows_at_once),
        grid_spec=pltpu.PrefetchScalarGridSpec(
            num_scalar_prefetch=1,
            grid=(pairs,),
            in_specs=[col(0), col(pairs), col(2 * pairs)],
            out_specs=[col(0), pl.BlockSpec((2, slots, slots), lambda i, n: (i, 0, 0)), col(0)],
        ),
        out_shape=[
            jax.ShapeDtypeStruct((slots, d), bf16),
            jax.ShapeDtypeStruct((2 * pairs, slots, slots), bf16),
            jax.ShapeDtypeStruct((slots, d), f32),
        ],
        compiler_params=params(),
        name="attend",
    )(length, qkv, qkv, qkv)


def middle_kernel(
    len_ref, mixed_ref, x_ref, cot_ref, mod_ref, linv_ref, ow_ref, ob_ref, uw_ref, ub_ref, dw_ref, db_ref,
    out_ref, h2_ref, act_ref, dbr_ref, dup_ref, dat_ref, dmix_ref, dmid_ref, dmod_ref,
):
    i = pl.program_id(0)
    tile, d = x_ref.shape
    mod = lambda k: mod_ref[:, k * d : (k + 1) * d]
    gate1, shift2, scale2, gate2 = mod(2), mod(3), mod(4), mod(5)
    slot = lax.broadcasted_iota(jnp.int32, (tile, 1), 0) + i * tile
    valid = slot < len_ref[0]
    attn = jnp.where(valid, mm(mixed_ref[...], ow_ref[...], NN) + ob_ref[...].astype(f32), 0.0)
    mid = x_ref[...].astype(f32) + gate1 * attn
    c = mid - jnp.mean(mid, axis=1, keepdims=True)
    r2 = lax.rsqrt(jnp.mean(c * c, axis=1, keepdims=True) + EPS)
    n2 = c * r2
    h2 = (n2 * (1.0 + scale2) + shift2).astype(bf16)
    h2_ref[...] = h2
    cot = cot_ref[...].astype(f32)
    dbr = (gate2 * cot).astype(bf16)
    dbr_ref[...] = dbr
    ff = uw_ref.shape[1]
    step = 512
    for n in range(0, ff, step):
        u = mm(h2, uw_ref[:, n : n + step], NN) + ub_ref[:, n : n + step].astype(f32)
        c0 = 0.7978845608028654
        th = jnp.tanh(c0 * (u + 0.044715 * u * u * u))
        half = 0.5 * (1.0 + th)
        act_ref[:, n : n + step] = (u * half).astype(bf16)
        grad = half + 0.5 * u * (1.0 - th * th) * (c0 * (1.0 + 3.0 * 0.044715 * u * u))
        da = mm(dbr, dw_ref[n : n + step, :], NT)
        dup_ref[:, n : n + step] = (da * grad).astype(bf16)
    branch = mm(act_ref[...], dw_ref[...], NN) + db_ref[...].astype(f32)
    out_ref[...] = (mid + gate2 * branch).astype(bf16)
    dgate2 = jnp.sum(cot * branch, axis=0, keepdims=True)
    dh2 = mm(dup_ref[...], uw_ref[...], NT)
    dscale2 = jnp.sum(dh2 * n2, axis=0, keepdims=True)
    dshift2 = jnp.sum(dh2, axis=0, keepdims=True)
    dn2 = dh2 * (1.0 + scale2)
    dmid = cot + r2 * (
        dn2 - jnp.mean(dn2, axis=1, keepdims=True) - n2 * jnp.mean(dn2 * n2, axis=1, keepdims=True)
    )
    dmid_ref[...] = dmid
    dgate1 = jnp.sum(dmid * attn, axis=0, keepdims=True)
    dat = jnp.where(valid, gate1 * dmid, 0.0).astype(bf16)
    dat_ref[...] = dat
    dmix_ref[...] = (mm(dat, ow_ref[...], NT) * linv_ref[...]).astype(bf16)
    part = jnp.concatenate([dgate1, dshift2, dscale2, dgate2], axis=1)

    @pl.when(i == 0)
    def _():
        dmod_ref[...] = part

    @pl.when(i > 0)
    def _():
        dmod_ref[...] += part


def middle_part(length, mixed, x, cot, mod, linv, ow, ob, uw, ub, dw, db, tile=256):
    slots, d = x.shape
    ff = uw.shape[1]
    row = lambda n: pl.BlockSpec((tile, n), lambda i, n_: (i, 0))
    S = jax.ShapeDtypeStruct
    return pl.pallas_call(
        middle_kernel,
        grid_spec=pltpu.PrefetchScalarGridSpec(
            num_scalar_prefetch=1,
            grid=(slots // tile,),
            in_specs=[row(d), row(d), row(d), full(mod.shape), row(d), full(ow.shape), full(ob.shape),
                      full(uw.shape), full(ub.shape), full(dw.shape), full(db.shape)],
            out_specs=[row(d), row(d), row(ff), row(d), row(ff), row(d), row(d), row(d),
                       pl.BlockSpec((1, 4 * d), lambda i, n_: (0, 0))],
        ),
        out_shape=[S((slots, d), bf16), S((slots, d), bf16), S((slots, ff), bf16), S((slots, d), bf16),
                   S((slots, ff), bf16), S((slots, d), bf16), S((slots, d), bf16), S((slots, d), f32),
                   S((1, 4 * d), f32)],
        compiler_params=params(),
        name="middle_part",
    )(length, mixed, x, cot, mod, linv, ow, ob, uw, ub, dw, db)


MESH = pl.DeviceIdType.MESH
STRIP = 512
RINGS = dict(r0=4, r1=6, r2=7, r3=6)
DELAYS = (0, 1, 3, 5, 8, 9)


class Exchange:
    def __init__(self, groups, batch, own, s, sems, ready, chunks):
        self.G, self.B, self.H, self.chunks = groups, batch, groups // 4, chunks
        self.plan = []
        while len(self.plan) - self.plan.count(None) < chunks:
            n = len(self.plan) - self.plan.count(None)
            self.plan.append(n if len(self.plan) >= len(ready) or n < ready[len(self.plan)] else None)
        self.gaps = [t for t, c in enumerate(self.plan) if c is None]
        self.last = len(self.plan) - 1 + DELAYS[-1]
        self.own = own
        self.s = s
        self.send, self.recv = sems
        g, c = lax.axis_index("groups"), lax.axis_index("batch")
        self.c, self.x, self.y, self.z = c, g % 2, (g // 2) % 2, g // 4
        x, y, z, H, B = self.x, self.y, self.z, self.H, self.B
        pos = lambda z_, y_, x_: z_ * 4 + y_ * 2 + x_
        self.cores = [(g, (c + k) % B) for k in range(1, B)]
        self.across_x = (pos(z, y, 1 - x), c)
        self.across_y = (pos(z, 1 - y, x), c)
        self.across_z = [(pos((z + k) % H, y, x), c) for k in range(1, H)]

    @staticmethod
    def sems_per_chunk(groups, batch):
        return 2 * (batch - 1) + 4 + (groups // 4 - 1)

    def barrier(self):
        sem = pltpu.get_barrier_semaphore()
        peers = self.cores + [self.across_x, self.across_y] + self.across_z
        for p in peers:
            pl.semaphore_signal(sem, inc=1, device_id=p, device_id_type=MESH)
        pl.semaphore_wait(sem, len(peers))

    def copy(self, j, n, src, dst, peer):
        return pltpu.make_async_remote_copy(
            src_ref=src, dst_ref=dst, send_sem=self.send.at[j, n], recv_sem=self.recv.at[j, n],
            device_id=peer, device_id_type=MESH,
        )

    def copies(self, j, phase):
        B, H, x, y = self.B, self.H, self.x, self.y
        s = self.s
        rows, width = s["r0"].shape[-2:]
        half = rows // 2
        q0, q1, q2, q3 = (j % RINGS[k] for k in ("r0", "r1", "r2", "r3"))
        if phase == 0:
            out = []
            for k, p in enumerate(self.cores):
                cols = pl.ds(pl.multiple_of(p[1] * width, width), width)
                out.append(self.copy(j, k, self.own(j).at[:, :, :, :, cols], s["r0"].at[q0, k], p))
            return out
        n = B - 1
        if phase == 1:
            total = s["r0"].at[q0, 0]
            return [
                self.copy(j, n, total.at[:, :, 1 - x, :half], s["r1"].at[q1, 0], self.across_x),
                self.copy(j, n + 1, total.at[:, 1 - y, :, half:], s["r1"].at[q1, 1], self.across_y),
            ]
        if phase == 2:
            return [
                self.copy(j, n + 2, s["r1"].at[q1, 0, :, 1 - y], s["r2"].at[q2, :, :half], self.across_y),
                self.copy(j, n + 3, s["r1"].at[q1, 1, :, 1 - x], s["r2"].at[q2, :, half:], self.across_x),
            ]
        n += 4
        if phase == 3:
            return [
                self.copy(j, n + k, s["r2"].at[q2, p[0] // 4], s["r3"].at[q3, k], p)
                for k, p in enumerate(self.across_z)
            ]
        n += H - 1
        cols = pl.ds(pl.multiple_of(self.c * width, width), width)
        place = s["out"].at[j, :, cols]
        return [self.copy(j, n + k, place, place, p) for k, p in enumerate(self.cores)]

    def start(self, j, phase):
        for d in self.copies(j, phase):
            d.start()

    def finish(self, j, phase):
        for d in self.copies(j, phase):
            d.wait()
        s, x, y, z, H = self.s, self.x, self.y, self.z, self.H
        rows, width = s["r0"].shape[-2:]
        half = rows // 2
        q0, q1, q2, q3 = (j % RINGS[k] for k in ("r0", "r1", "r2", "r3"))
        cols = pl.ds(pl.multiple_of(self.c * width, width), width)
        if phase == 0:
            own = self.own(j)

            def add(h, _):
                t = own[h, :, :, :, cols]
                if self.B == 2:
                    t = t + s["r0"][q0, 0, h]
                else:
                    t = t.astype(f32)
                    for k in range(self.B - 1):
                        t = t + s["r0"][q0, k, h].astype(f32)
                s["r0"][q0, 0, h] = t.astype(bf16)
                return _

            lax.fori_loop(0, H, add, 0)
        elif phase == 1:

            def add(h, _):
                s["r1"][q1, 0, h] = s["r1"][q1, 0, h] + s["r0"][q0, 0, h, :, x, :half]
                s["r1"][q1, 1, h] = s["r1"][q1, 1, h] + s["r0"][q0, 0, h, y, :, half:]
                return _

            lax.fori_loop(0, H, add, 0)
        elif phase == 2:
            s["r2"][q2, :, :half] = s["r2"][q2, :, :half] + s["r1"][q1, 0, :, y]
            s["r2"][q2, :, half:] = s["r2"][q2, :, half:] + s["r1"][q1, 1, :, x]
        elif phase == 3:
            t = s["r2"][q2, z].astype(f32)
            for k in range(H - 1):
                t = t + s["r3"][q3, k].astype(f32)
            s["out"][j, :, cols] = t

    @staticmethod
    def scratch(groups, batch, chunks, rows, cols):
        H, w = groups // 4, cols // batch
        return dict(
            r0=pltpu.VMEM((RINGS["r0"], batch - 1, H, 2, 2, rows, w), bf16),
            r1=pltpu.VMEM((RINGS["r1"], 2, H, 2, rows // 2, w), bf16),
            r2=pltpu.VMEM((RINGS["r2"], H, rows, w), bf16),
            r3=pltpu.VMEM((RINGS["r3"], H - 1, rows, w), bf16),
            out=pltpu.VMEM((chunks, rows, cols), f32),
        )

    def tick(self, t, first=None, final=None):
        static = isinstance(t, int)
        if static:
            first = final = t
        n = len(self.plan)
        for phase in range(5, -1, -1):
            lo, hi = first - DELAYS[phase], final - DELAYS[phase]
            j = t - DELAYS[phase]
            if hi < 0 or lo >= n or (static and self.plan[j] is None):
                continue

            def act(phase=phase, j=j):
                c = self.plan[j] if static else j
                if not static:
                    for g in self.gaps:
                        if g < lo:
                            c = c - 1
                        elif g <= hi:
                            c = c - jnp.where(j > g, 1, 0)
                if phase > 0:
                    self.finish(c, phase - 1)
                if phase < 5:
                    self.start(c, phase)

            conds = []
            if lo < 0:
                conds.append(j >= 0)
            if hi >= n:
                conds.append(j < n)
            conds += [j != g for g in self.gaps if lo <= g <= hi]
            if static or not conds:
                act()
            else:
                ok = conds[0]
                for c in conds[1:]:
                    ok = jnp.logical_and(ok, c)
                pl.when(ok)(act)


class Small:
    def __init__(self, ex, sems, total=None, mine=None, seen=None):
        self.ex, self.total, self.mine, self.seen = ex, total, mine, seen
        self.send, self.recv = sems

    @staticmethod
    def count(groups, batch):
        return batch - 1 + 2 + groups // 4 - 1

    def copies(self, phase):
        ex = self.ex
        peers = [ex.cores, [ex.across_x], [ex.across_y], ex.across_z][phase]
        first = [0, ex.B - 1, ex.B, ex.B + 1][phase]
        out = []
        for k, p in enumerate(peers):
            n = first + k
            if self.seen is None:
                src, dst = self.mine.at[phase], self.total.at[n]
            else:
                at = (ex.z, ex.y, ex.x, ex.c)[: 4 - phase]
                src = dst = self.seen.at[at]
            out.append(pltpu.make_async_remote_copy(
                src_ref=src, dst_ref=dst, send_sem=self.send.at[n], recv_sem=self.recv.at[n],
                device_id=p, device_id_type=MESH))
        return out

    def start(self, phase):
        for d in self.copies(phase):
            d.start()

    def finish(self, phase):
        for d in self.copies(phase):
            d.wait()
        if self.seen is None:
            ex = self.ex
            n = [ex.B - 1, 1, 1, ex.H - 1][phase]
            first = [0, ex.B - 1, ex.B, ex.B + 1][phase]
            t = self.mine[phase]
            for k in range(n):
                t = t + self.total[first + k]
            self.mine[phase + 1] = t


def back_kernel(groups, batch, per, n_chunks, *refs):
    (act_hbm, dbr_hbm, h2_hbm, dup_hbm, mixed_hbm, dat_hbm, dmix_hbm, qkv_hbm, e_hbm, h1_hbm, w_hbm, x_hbm, dmid_hbm, mw_hbm,
     cos_ref, sin_ref, mod_ref, dmodb_ref, te_ref,
     dwo, uwo, owo, qwo, bias_out, early_out, late_out, fg_hbm, tg_ref,
     own, r0, r1, r2, r3, out, total, mine, early, late, etmp, ltmp,
     ebuf, dsb, qkv, mixed, dmix, dbr, h2, dat, dmid, fg, dmoda_ref,
     send, recv, ssum, rsum, sear, rear, slat, rlat, ld, eld, dld, fst, ost, mld) = refs
    slots, d = mixed.shape
    H, rows = groups // 4, d // groups
    chunk = lambda strip: strip // per
    n_own = own.shape[0]
    pairs = d // 128
    first, second = pairs // 2, pairs - 1
    ready = [4, 6, 8, 10, 10] + [10] * first + [13] * (second - first + 1) + [15] * (1 + pairs - second) + [16]
    ex = Exchange(groups, batch, lambda j: own.at[j % n_own], dict(r0=r0, r1=r1, r2=r2, r3=r3, out=out), (send, recv),
                  [n // per for n in ready], n_chunks)
    sums = Small(ex, (ssum, rsum), total=total, mine=mine)
    gather_early = Small(ex, (sear, rear), seen=early)
    gather_late = Small(ex, (slat, rlat), seen=late)

    load = lambda k, src, dst: pltpu.make_async_copy(src, dst, ld.at[k])
    half = lambda ref, k: ref.at[:, k * d : (k + 1) * d]
    loads = [
        load(0, half(act_hbm, 0), ebuf.at[1, 0]), load(1, half(act_hbm, 1), ebuf.at[1, 1]), load(2, dbr_hbm, dbr),
        load(3, h2_hbm, h2), load(4, half(dup_hbm, 0), dsb.at[0]), load(5, half(dup_hbm, 1), dsb.at[1]),
        load(6, mixed_hbm, mixed), load(7, dat_hbm, dat), load(8, qkv_hbm, qkv), load(9, dmix_hbm, dmix),
    ]
    load_h1 = load(10, h1_hbm, h2)
    load_w = [load(11 + k, half(w_hbm, k), (ebuf.at[0, 0], ebuf.at[0, 1], dbr)[k]) for k in range(3)]
    load_x = load(14, x_hbm, dat)
    free = [mixed, dmix, ebuf.at[1, 0], dsb.at[0], dsb.at[1], ebuf.at[1, 1]]
    load_m = [pltpu.make_async_copy(half(mw_hbm, k), free[k], mld.at[k]) for k in range(6)]
    load_e = lambda p, slot: pltpu.make_async_copy(e_hbm.at[pl.ds(2 * p, 2)], ebuf.at[slot], eld.at[slot])
    for k in (0, 2, 1):
        loads[k].start()

    for k in range(4 * d // STRIP):
        etmp[k : k + 1, :] = dmodb_ref[:, k * STRIP : (k + 1) * STRIP]
    t = te_ref[...].astype(f32)
    t = t * jax.nn.sigmoid(t)
    at = 4 * d // STRIP
    for k in range(d // STRIP):
        etmp[at + k : at + k + 1, :] = t[:, k * STRIP : (k + 1) * STRIP]
    at += d // STRIP
    etmp[at:, :] = jnp.zeros((etmp.shape[0] - at, STRIP), f32)
    early[ex.z, ex.y, ex.x, ex.c] = etmp[...].astype(bf16)
    mine[0] = jnp.zeros(mine.shape[1:], f32)
    ex.barrier()
    gather_early.start(0)

    def column_sums(value, row, k):
        mine[0, pl.ds(row + k, 1), :] = jnp.sum(value.astype(f32), axis=0, keepdims=True)

    def wgrad_into(left, block_rows, rights, place, zs, before=None):
        parts = block_rows // rows

        def body(i, _):
            n = zs * 4 * block_rows
            if before is not None:
                before(i, n)
            lt = left(i * n, n).T
            for k, right in enumerate(rights):
                r = mm(lt, right(), NN).astype(bf16)
                for b in range(4 * zs):
                    for part in range(parts):
                        strip = place(k, part)
                        lo = b * block_rows + part * rows
                        off = (strip % per) * STRIP
                        cols = pl.ds(off if isinstance(off, int) else pl.multiple_of(off, STRIP), STRIP)
                        own[chunk(strip) % n_own, i * zs + b // 4, (b // 2) % 2, b % 2, :, cols] = r[lo : lo + rows]
            return _

        lax.fori_loop(0, H // zs, body, 0)

    for k in (0, 2):
        loads[k].wait()
    for k in (3, 4, 5, 6, 7):
        loads[k].start()
    wide = lambda ref: lambda lo, n: ref[lo // d, :, pl.ds(pl.multiple_of(lo % d, 128), n)]
    flat = lambda ref: lambda lo, n: ref[:, pl.ds(pl.multiple_of(lo, 128), n)]
    strip_at = lambda k: pl.ds(k * STRIP if isinstance(k, int) else pl.multiple_of(k * STRIP, STRIP), STRIP)
    cut = lambda ref, k: lambda: ref[:, strip_at(k)]

    def second_half(i, n):
        @pl.when(i * n == d)
        def _():
            loads[1].wait()

    wgrad_into(wide(ebuf.at[1]), 2 * rows, [cut(dbr, k) for k in range(2)], lambda k, part: 2 * k + part, 2, second_half)
    for k in range(2):
        column_sums(cut(dbr, k)(), 12, k)
    gather_early.finish(0)
    gather_early.start(1)
    ex.tick(0)
    for k in (3, 4, 5):
        loads[k].wait()
    for k in (8, 9):
        loads[k].start()
    load_e(0, 0).start()
    for h in range(2):
        wgrad_into(flat(h2), rows, [cut(dsb.at[h], k) for k in range(2)], lambda k, part: 4 + 2 * h + k, 2)
        for k in range(2):
            column_sums(cut(dsb.at[h], k)(), 8 + 2 * h, k)
        if h == 0:
            gather_early.finish(1)
            gather_early.start(2)
        ex.tick(1 + h)
    load_h1.start()
    for k in (6, 7):
        loads[k].wait()
    wgrad_into(flat(mixed), rows, [cut(dat, k) for k in range(2)], lambda k, part: 8 + k, 2)
    for k in range(2):
        column_sums(cut(dat, k)(), 6, k)
    gather_early.finish(2)
    gather_early.start(3)
    load_x.start()
    ex.tick(3)
    ex.tick(4)
    for k in (8, 9):
        loads[k].wait()
    gather_early.finish(3)
    lane = lax.broadcasted_iota(jnp.int32, (1, 128), 1)
    even = even_lanes(slots)
    at_once = 256

    def attention(p, slot):
        col = lambda off: pl.ds(pl.multiple_of(off + p * 128, 128), 128)
        qc, kc, vc = col(0), col(d), col(2 * d)
        q, k, v, do = qkv[:, qc], qkv[:, kc], qkv[:, vc], dmix[:, qc]
        dqs = []
        for h in range(2):
            own_lanes = lane < 64 if h == 0 else lane >= 64
            parts = []
            for a in range(0, slots, at_once):
                rws = pl.ds(a, at_once)
                t = dmix[rws, qc]
                t = jnp.where(own_lanes, t, jnp.zeros_like(t))
                inner = jnp.sum(t.astype(f32) * mixed[rws, qc].astype(f32), axis=1, keepdims=True)
                ds = ebuf[slot, h, rws, :] * (mm(t, v, NT) - inner).astype(bf16)
                dsb[h, rws, :] = ds
                parts.append(mm(ds, k, NN))
            dqs.append(jnp.concatenate(parts, axis=0))
        do_t, q_t = do.T, q.T
        dv = jnp.concatenate([mm(do_t[h * 64 : h * 64 + 64], ebuf[slot, h], NN) for h in range(2)], axis=0)
        dk = jnp.concatenate([mm(q_t[h * 64 : h * 64 + 64], dsb[h], NN) for h in range(2)], axis=0)
        cos, sin = cos_ref[...], -sin_ref[...]
        dq = jnp.where(lane < 64, dqs[0], dqs[1]) * 0.125
        qkv[:, qc] = turn(dq, cos, sin, even).astype(bf16)
        qkv[:, kc] = turn(dk.T, cos, sin, even).astype(bf16)
        qkv[:, vc] = dv.T.astype(bf16)

    def qkv_grad(rights, places):
        zs = 2

        def body(i, carry):
            n = zs * 4 * rows
            lt = h2[:, pl.ds(pl.multiple_of(i * n, 128), n)].T
            for right, where in zip(rights, places):
                r = mm(lt, right(), NN).astype(bf16)
                for c, (strip, at) in enumerate(where):
                    lo = (strip % per) * STRIP + at * 128
                    for b in range(4 * zs):
                        own[chunk(strip) % n_own, i * zs + b // 4, (b // 2) % 2, b % 2, :, lo : lo + 128] = (
                            r[b * rows : (b + 1) * rows, c * 128 : (c + 1) * 128]
                        )
            return carry

        lax.fori_loop(0, H // zs, body, 0)

    span = lambda k, lo, hi: lambda: qkv[:, k * d + lo * 128 : k * d + hi * 128]
    late_cols = [(k, p) for k in range(3) for p in range(first, second)] + [(k, p) for k in range(3) for p in range(second, pairs)]
    late_place = {kp: (13 + n // 4, n % 4) for n, kp in enumerate(late_cols)}
    t1 = 5 + first

    def heads(p, carry):
        slot = p % 2
        load_e(p, slot).wait()

        @pl.when(p + 1 < pairs)
        def _():
            load_e(p + 1, 1 - slot).start()

        attention(p, slot)
        ex.tick(5 + p + jnp.where(p >= first, 1, 0) + jnp.where(p >= second, 1, 0), 5, 6 + pairs)

        @pl.when(p == first - 1)
        def _():
            load_h1.wait()
            qkv_grad([cut(qkv, 2 * k) for k in range(3)], [[(10 + k, c) for c in range(4)] for k in range(3)])
            for k in range(3):
                column_sums(cut(qkv, 2 * k)(), 2 * k, 0)
            ex.tick(t1)

        @pl.when(p == second - 1)
        def _():
            for c in load_w:
                c.start()
            qkv_grad([span(k, first, second) for k in range(3)],
                     [[late_place[k, q] for q in range(first, second)] for k in range(3)])
            ex.tick(1 + 5 + second)

        return carry

    lax.fori_loop(0, pairs, heads, 0)
    assert second % 2 == 1
    for t in load_m:
        t.start()
    qkv_grad([lambda: jnp.concatenate([span(k, second, pairs)() for k in range(3)], axis=1)],
             [[late_place[k, q] for k in range(3) for q in range(second, pairs)]])
    t0 = 8 + pairs
    ex.tick(t0 - 1)
    for k in range(3):
        column_sums(cut(qkv, 2 * k + 1)(), 2 * k + 1, 0)
    sums.start(0)
    tile = dmid.shape[1]
    tiles = slots // tile
    row_tile = lambda i: pl.ds(pl.multiple_of(i * tile, tile), tile)
    load_d = lambda i, slot: pltpu.make_async_copy(dmid_hbm.at[row_tile(i)], dmid.at[slot], dld.at[slot])
    store_f = lambda i, slot: pltpu.make_async_copy(fg.at[slot], fg_hbm.at[row_tile(i)], fst.at[slot])
    load_d(0, 0).start()
    load_x.wait()
    for t in load_w:
        t.wait()
    dmoda_ref[...] = jnp.zeros_like(dmoda_ref)
    def front(i, carry):
        slot = i % 2

        @pl.when(i + 1 < tiles)
        def _():
            load_d(i + 1, 1 - slot).start()

        rws = row_tile(i)
        dh = (
            mm(qkv[rws, :d], ebuf[0, 0], NT) + mm(qkv[rws, d : 2 * d], ebuf[0, 1], NT) + mm(qkv[rws, 2 * d :], dbr[...], NT)
        )
        ex.tick(t0 + 2 * i, t0, t0 + 2 * tiles - 2)
        x = dat[rws, :].astype(f32)
        cen = x - jnp.mean(x, axis=1, keepdims=True)
        r = lax.rsqrt(jnp.mean(cen * cen, axis=1, keepdims=True) + EPS)
        n1 = cen * r
        dmoda_ref[:, :d] += jnp.sum(dh, axis=0, keepdims=True)
        dmoda_ref[:, d:] += jnp.sum(dh * n1, axis=0, keepdims=True)
        dn = dh * (1.0 + mod_ref[:, d : 2 * d])
        load_d(i, slot).wait()

        @pl.when(i >= 2)
        def _():
            store_f(i - 2, slot).wait()

        fg[slot] = dmid[slot] + r * (
            dn - jnp.mean(dn, axis=1, keepdims=True) - n1 * jnp.mean(dn * n1, axis=1, keepdims=True)
        )
        store_f(i, slot).start()
        for phase in range(3):

            @pl.when(i == phase)
            def _():
                sums.finish(phase)
                sums.start(phase + 1)

        ex.tick(t0 + 2 * i + 1, t0 + 1, t0 + 2 * tiles - 1)
        return carry

    lax.fori_loop(0, tiles, front, 0)
    for k in range(2 * d // 128):
        ltmp[k : k + 1, :] = dmoda_ref[:, k * 128 : (k + 1) * 128]
    late[ex.z, ex.y, ex.x, ex.c] = ltmp[...].astype(bf16)
    gather_late.start(0)
    sums.finish(3)

    def through_mod(k):
        load_m[k].wait()
        v = dmoda_ref[:, k * d : (k + 1) * d] if k < 2 else dmodb_ref[:, (k - 2) * d : (k - 1) * d]
        v = jnp.broadcast_to(v, (8, d)).astype(bf16)
        tg_ref[...] += mm(v, free[k][...], NT)[:1]

    pieces = [(2 * k + part, 0, dwo.at[part, :, k * STRIP : (k + 1) * STRIP]) for k in range(2) for part in range(2)]
    pieces += [(4 + k, 0, uwo.at[:, k * STRIP : (k + 1) * STRIP]) for k in range(4)]
    pieces += [(8 + k, 0, owo.at[:, k * STRIP : (k + 1) * STRIP]) for k in range(2)]
    pieces += [(10 + k, 0, qwo.at[:, k * d : k * d + STRIP]) for k in range(3)]
    for (k, p), (strip, at) in late_place.items():
        pieces.append((strip, at * 128, qwo.at[:, k * d + p * 128 : k * d + (p + 1) * 128]))
    stores = [pltpu.make_async_copy(early, early_out, ost.at[0])]
    for n, (strip, off, dst) in enumerate(pieces):
        off += (strip % per) * STRIP
        stores.append(pltpu.make_async_copy(out.at[chunk(strip), :, off : off + dst.shape[1]], dst, ost.at[n + 1]))

    def start_stores():
        for c in stores:
            c.start()

    tg_ref[...] = jnp.zeros_like(tg_ref)
    t = t0 + 2 * tiles
    stored = t > ex.last
    if stored:
        start_stores()
    for phase in range(4):
        through_mod(phase)
        if t <= ex.last:
            ex.tick(t)
            t += 1
            if t > ex.last:
                start_stores()
                stored = True
        gather_late.finish(phase)
        if phase < 3:
            gather_late.start(phase + 1)
    through_mod(4)
    through_mod(5)
    for k in range(mine.shape[1]):
        for c in range(STRIP // 128):
            at = k * (STRIP // 128) + c
            bias_out[at : at + 1, :] = mine[4, k : k + 1, c * 128 : (c + 1) * 128]
    for i in range(max(0, tiles - 2), tiles):
        store_f(i, i % 2).wait()
    while t <= ex.last:
        ex.tick(t)
        t += 1
    if not stored:
        start_stores()
    late_store = pltpu.make_async_copy(late, late_out, ost.at[len(stores)])
    late_store.start()
    for c in stores:
        c.wait()
    late_store.wait()


def backward(groups, batch, act, dbr, h2, dup, mixed, dat, dmix, qkv, e, h1, w, x, dmid, mw, cos, sin, mod, dmodb, te):
    slots, d = mixed.shape
    H, rows = groups // 4, d // groups
    per = max(1, 128 * batch // STRIP)
    n_chunks = 16 // per
    S = jax.ShapeDtypeStruct
    hbm = pl.BlockSpec(memory_space=pl.ANY)
    vm = pl.BlockSpec(memory_space=pltpu.VMEM)
    V = pltpu.VMEM
    sc = Exchange.scratch(groups, batch, n_chunks, rows, per * STRIP)
    ns, nsm = Exchange.sems_per_chunk(groups, batch), Small.count(groups, batch)
    dma = pltpu.SemaphoreType.DMA
    tile = 256
    seen = (H, 2, 2, batch)
    return pl.pallas_call(
        lambda *a: back_kernel(groups, batch, per, n_chunks, *a),
        in_specs=[hbm] * 14 + [vm] * 5,
        out_specs=[hbm] * 4 + [vm, hbm, hbm, hbm, vm],
        out_shape=[S((2, rows, d), f32), S((rows, 2 * d), f32), S((rows, d), f32), S((rows, 3 * d), f32),
                   S((16 * STRIP // 128, 128), f32), S(seen + (16, STRIP), bf16), S(seen + (16, 128), bf16),
                   S((slots, d), f32), S((1, d), f32)],
        scratch_shapes=[V((-(-10 // per), H, 2, 2, rows, per * STRIP), bf16),
                        sc["r0"], sc["r1"], sc["r2"], sc["r3"], sc["out"],
                        V((nsm, 16, STRIP), f32), V((5, 16, STRIP), f32), V(seen + (16, STRIP), bf16), V(seen + (16, 128), bf16),
                        V((16, STRIP), f32), V((16, 128), f32),
                        V((2, 2, slots, slots), bf16), V((2, slots, slots), bf16), V((slots, 3 * d), bf16), V((slots, d), bf16),
                        V((slots, d), bf16), V((slots, d), bf16), V((slots, d), bf16), V((slots, d), bf16),
                        V((2, tile, d), f32), V((2, tile, d), f32), V((1, 2 * d), f32),
                        dma((n_chunks, ns)), dma((n_chunks, ns)), dma((nsm,)), dma((nsm,)), dma((nsm,)), dma((nsm,)),
                        dma((nsm,)), dma((nsm,)), dma((15,)), dma((2,)), dma((2,)), dma((2,)), dma((27,)), dma((6,))],
        compiler_params=pltpu.CompilerParams(vmem_limit_bytes=67_000_000, collective_id=0, has_side_effects=True),
        name="backward",
    )(act, dbr, h2, dup, mixed, dat, dmix, qkv, e, h1, w, x, dmid, mw, cos, sin, mod, dmodb, te)


def finish_kernel(
    early_ref, late_ref, bias_ref, tg_ref, te_ref, dw_in, uw_in, ow_in, qw_in, fg_in,
    wg_hbm, tout_ref, mb_ref, qb_ref, ob_ref, ub_ref, db_ref, dw_out, uw_out, ow_out, qw_out, fg_out,
    flat, wg_ref, dw, uw, ow, qw, fg, isem, osem,
):
    rows, d = wg_ref.shape[0], wg_ref.shape[1] // 6
    tile = fg.shape[0] // 8
    cuts = [pl.ds(k * tile, tile) for k in range(8)]
    through = [(dw_in, dw, dw_out), (uw_in, uw, uw_out), (ow_in, ow, ow_out), (qw_in, qw, qw_out)]
    through += [(fg_in.at[c], fg.at[c], fg_out.at[c]) for c in cuts]
    ins = [pltpu.make_async_copy(a, v, isem.at[k]) for k, (a, v, _) in enumerate(through)]
    outs = [pltpu.make_async_copy(v, b, osem.at[k]) for k, (_, v, b) in enumerate(through)]
    for c in ins:
        c.start()
    g = lax.axis_index("groups")
    e, late = early_ref[...], late_ref[...]
    n = e.shape[0] // 16
    at, off = 4 * d // STRIP + (g * rows) // STRIP, (g * rows) % STRIP
    pick = lax.broadcasted_iota(jnp.int32, (STRIP, 128), 0) - lax.broadcasted_iota(jnp.int32, (STRIP, 128), 1) == off
    em = mm(e, jnp.where(pick, 1.0, 0.0).astype(bf16), NN).reshape(n, 16, 128)
    em = jnp.where(lax.broadcasted_iota(jnp.int32, em.shape, 1) == at, em, 0.0)
    em = jnp.broadcast_to(jnp.sum(em, axis=1, keepdims=True), em.shape).reshape(n * 16, 128).T[:rows]
    row = lax.broadcasted_iota(jnp.int32, em.shape, 1) % 16
    for r in range(16):
        left = jnp.where(row == r, em, 0.0).astype(bf16)
        wg_ref[:, r * 128 : (r + 1) * 128] = mm(left, late, NN)
        if r < 4 * d // STRIP:
            lo = 2 * d + r * STRIP
            wg_ref[:, lo : lo + STRIP] = mm(left, e, NN)
    store_wg = pltpu.make_async_copy(wg_ref, wg_hbm, osem.at[len(outs)])
    store_wg.start()
    for a, b in zip(ins, outs):
        a.wait()
        b.start()
    flat[:16, :] = jnp.sum(late.astype(f32).reshape(n, 16, 128), axis=0)
    es = jnp.sum(e.astype(f32).reshape(n, 16, STRIP), axis=0)
    for r in range(4 * d // STRIP):
        for c in range(STRIP // 128):
            k = 16 + r * (STRIP // 128) + c
            flat[k : k + 1, :] = es[r : r + 1, c * 128 : (c + 1) * 128]
    flat[48:, :] = jnp.zeros((flat.shape[0] - 48, 128), f32)
    lane = lax.broadcasted_iota(jnp.int32, (1, 128), 1)
    for ref, src, first in ((mb_ref, flat, 0), (qb_ref, bias_ref, 0), (ob_ref, bias_ref, 3 * d), (ub_ref, bias_ref, 4 * d), (db_ref, bias_ref, 6 * d)):
        width = ref.shape[1]
        at, off = first // 128 + (g * width) // 128, (g * width) % 128
        for k in range(-(-width // 128)):
            turned = [pltpu.roll(src[pl.ds(at + k + i, 1), :], (128 - off) % 128, 1) for i in range(2)]
            v = jnp.where(lane < 128 - off, turned[0], turned[1])
            w = min(128, width - k * 128)
            ref[:, k * 128 : k * 128 + w] = v[:, :w]
    t = te_ref[...].astype(f32)
    s = jax.nn.sigmoid(t)
    tout_ref[...] = tg_ref[...] * (s * (1.0 + t * (1.0 - s)))
    for c in outs:
        c.wait()
    store_wg.wait()


def finish(early, late, bias, tg, te, *results):
    rows, d = results[2].shape
    S = jax.ShapeDtypeStruct
    hbm, vm = pl.BlockSpec(memory_space=pl.ANY), pl.BlockSpec(memory_space=pltpu.VMEM)
    n = len(results)
    return pl.pallas_call(
        finish_kernel,
        in_specs=[vm] * 5 + [hbm] * n,
        out_specs=[hbm] + [vm] * 6 + [hbm] * n,
        out_shape=[S((rows, 6 * d), f32), S((1, d), f32)] + [S((1, k * rows), f32) for k in (6, 3, 1, 2, 1)]
        + [S(r.shape, f32) for r in results],
        scratch_shapes=[pltpu.VMEM((56, 128), f32), pltpu.VMEM((rows, 6 * d), f32)]
        + [pltpu.VMEM(r.shape, f32) for r in results]
        + [pltpu.SemaphoreType.DMA((n + 7,)), pltpu.SemaphoreType.DMA((n + 8,))],
        compiler_params=params(),
        name="finish",
    )(early, late, bias, tg, te, *results)


def solution(mesh):
    groups, batch = mesh.shape["groups"], mesh.shape["batch"]

    def body(frames, te, lengths, mod_w, mod_b, qkv_w, qkv_b, out_w, out_b, up_w, up_b, down_w, down_b, cot):
        x, ct = frames[0], cot[0]
        slots, d = x.shape
        row = lambda b: b.reshape(1, -1)
        mod = modulation(te, mod_w, row(mod_b))
        h1, qkv, cos, sin = project_qkv(x, mod, qkv_w, row(qkv_b), rot_tables(slots, d // HEADS))
        mixed, e, linv = attend(lengths, qkv)
        out, h2, act, dbr, dup, dat, dmix, dmid, dmod_b = middle_part(
            lengths, mixed, x, ct, mod, linv, out_w, row(out_b), up_w, row(up_b), down_w, row(down_b)
        )
        dws, uws, ows, qws, bs, early, late, fg, tg = backward(
            groups, batch, act, dbr, h2, dup, mixed, dat, dmix, qkv, e, h1, qkv_w, x, dmid, mod_w, cos, sin, mod, dmod_b, te
        )
        rows, n = d // groups, groups * batch
        mod_wg, time_grad, mb, qb, ob, ub, db, dws, uws, ows, qws, fg = finish(
            early.reshape(n * 16, STRIP), late.reshape(n * 16, 128), bs, tg, te, dws, uws, ows, qws, fg
        )
        return (out[None], fg[None], time_grad, mod_wg, mb[0], qws, qb[0], ows, ob[0], uws, ub[0], dws.reshape(2 * rows, d), db[0])

    split = P(("groups", "batch"))
    own = P("groups")
    return jax.shard_map(
        body, mesh=mesh,
        in_specs=(split,) * 3 + (P(),) * 10 + (split,),
        out_specs=(split,) * 3 + (own,) * 10,
        check_vma=False,
    )
```

```python
import jax, jax.numpy as jnp
import numpy as np
from jax import lax
from jax.experimental import pallas as pl
from jax.experimental.pallas import tpu as pltpu
from jax.sharding import PartitionSpec as P

f32 = jnp.float32
bf16 = jnp.bfloat16
HEADS = 16
LOG2E = 1.4426950408889634
EPS = 1e-6
NN = ((1,), (0,))
NT = ((1,), (1,))
TN = ((0,), (0,))
VMEM_LIMIT = 62 * 2**20


def mm(a, b, dims):
    return lax.dot_general(a, b, (dims, ((), ())), preferred_element_type=f32)


def params(**kw):
    return pltpu.CompilerParams(vmem_limit_bytes=VMEM_LIMIT, **kw)


BLOCK = 32


def rot_tables(slots, size):
    pair = np.arange(size // 2, dtype=np.float64)[None, :]
    sign = np.where(np.arange(size) % 2 == 0, -1.0, 1.0)
    out = []
    for pos in (np.arange(0, slots, BLOCK), np.arange(BLOCK)):
        ang = pos.astype(np.float64)[:, None] * np.power(10000.0, -2.0 * pair / size)
        cos = np.repeat(np.cos(ang), 2, axis=1)
        sin = np.repeat(np.sin(ang), 2, axis=1) * sign
        out += [np.tile(cos, (1, 2)).astype(np.float32), np.tile(sin, (1, 2)).astype(np.float32)]
    return out


def turn(x, cos, sin, even):
    swapped = jnp.where(even, pltpu.roll(x, 127, 1), pltpu.roll(x, 1, 1))
    return x * cos + swapped * sin


def even_lanes(rows):
    return lax.broadcasted_iota(jnp.int32, (rows, 128), 1) % 2 == 0


def full(shape):
    return pl.BlockSpec(shape, lambda *_: (0,) * len(shape), pipeline_mode=pl.Buffered(1))


def part(b, n, k):
    return pl.BlockSpec((1, n), lambda *_: (0, k), pipeline_mode=pl.Buffered(1))


def mod_kernel(te_ref, w_ref, b_ref, out_ref):
    t = te_ref[...].astype(f32)
    embed = (t * jax.nn.sigmoid(t)).astype(bf16)
    embed = jnp.broadcast_to(embed, (8, embed.shape[1]))
    out_ref[...] = mm(embed, w_ref[...], NN)[:1] + b_ref[...].astype(f32)


def modulation(te, w, b):
    d, n = w.shape
    blk = d
    return pl.pallas_call(
        mod_kernel,
        grid=(n // blk,),
        in_specs=[full((1, d)), pl.BlockSpec((d, blk), lambda i: (0, i)), pl.BlockSpec((1, blk), lambda i: (0, i))],
        out_specs=pl.BlockSpec((1, blk), lambda i: (0, i)),
        out_shape=jax.ShapeDtypeStruct((1, n), f32),
        compiler_params=params(),
        name="modulation",
    )(te, w, b)


def qkv_kernel(x_ref, mod_ref, w_ref, b_ref, cosa_ref, sina_ref, cosb_ref, sinb_ref, h_ref, qkv_ref, cos_ref, sin_ref):
    d = x_ref.shape[1]
    x = x_ref[...].astype(f32)
    c = x - jnp.mean(x, axis=1, keepdims=True)
    r = lax.rsqrt(jnp.mean(c * c, axis=1, keepdims=True) + EPS)
    h = (c * r * (1.0 + mod_ref[:, d : 2 * d]) + mod_ref[:, :d]).astype(bf16)
    h_ref[...] = h
    cosb, sinb = cosb_ref[...], sinb_ref[...]
    for k in range(x.shape[0] // BLOCK):
        cosa, sina = cosa_ref[k : k + 1, :], sina_ref[k : k + 1, :]
        cos_ref[k * BLOCK : (k + 1) * BLOCK, :] = cosa * cosb - sina * sinb
        sin_ref[k * BLOCK : (k + 1) * BLOCK, :] = sina * cosb + cosa * sinb
    cos, sin = cos_ref[...], sin_ref[...]
    even = even_lanes(x.shape[0])
    step = 512
    for n in range(0, 3 * d, step):
        y = mm(h, w_ref[:, n : n + step], NN) + b_ref[:, n : n + step].astype(f32)
        for t in range(0, step, 128):
            col = n + t
            z = y[:, t : t + 128]
            if col < 2 * d:
                z = turn(z, cos, sin, even)
            if col < d:
                z = z * 0.125
            qkv_ref[:, col : col + 128] = z.astype(bf16)


def project_qkv(x, mod, w, b, tables, tile=256):
    slots, d = x.shape
    row = lambda n: pl.BlockSpec((tile, n), lambda i: (i, 0))
    return pl.pallas_call(
        qkv_kernel,
        grid=(slots // tile,),
        in_specs=[row(d), full(mod.shape), full(w.shape), part(b, 3 * d, 0)]
        + [pl.BlockSpec((tile // BLOCK, 128), lambda i: (i, 0))] * 2 + [full((BLOCK, 128))] * 2,
        out_specs=[row(d), row(3 * d), row(128), row(128)],
        out_shape=[jax.ShapeDtypeStruct((slots, d), bf16), jax.ShapeDtypeStruct((slots, 3 * d), bf16),
                   jax.ShapeDtypeStruct((slots, 128), f32), jax.ShapeDtypeStruct((slots, 128), f32)],
        compiler_params=params(),
        name="project_qkv",
    )(x, mod, w, b, *tables)


def attend_kernel(len_ref, q_ref, k_ref, v_ref, o_ref, e_ref, linv_ref, *, rows_at_once):
    slots = q_ref.shape[0]
    lane = lax.broadcasted_iota(jnp.int32, (1, 128), 1)
    ones = jnp.where(lax.broadcasted_iota(jnp.int32, (slots, 128), 1) == 0, 1.0, 0.0).astype(bf16)
    k = k_ref[...]
    v = jnp.concatenate([v_ref[...], ones], axis=1)
    valid = lax.broadcasted_iota(jnp.int32, (1, slots), 1) < len_ref[0]
    for at in range(0, slots, rows_at_once):
        rows = pl.ds(at, rows_at_once)
        q = q_ref[rows, :]
        outs, invs = [], []
        for h in range(2):
            qh = jnp.where(lane < 64 if h == 0 else lane >= 64, q, jnp.zeros_like(q))
            s = jnp.where(valid, mm(qh, k, NT), -1e30)
            m = jnp.max(s, axis=1, keepdims=True)
            e = jnp.exp2((s - m) * LOG2E).astype(bf16)
            e_ref[h, rows, :] = e
            r = mm(e, v, NN)
            inv = 1.0 / r[:, 128:129]
            outs.append(r[:, :128] * inv)
            invs.append(inv)
        o_ref[rows, :] = jnp.where(lane < 64, outs[0], outs[1]).astype(bf16)
        linv_ref[rows, :] = jnp.where(lane < 64, invs[0], invs[1])


def attend(length, qkv, rows_at_once=128):
    slots, d = qkv.shape[0], qkv.shape[1] // 3
    pairs = d // 128
    col = lambda off: pl.BlockSpec((slots, 128), lambda i, n: (0, off + i))
    return pl.pallas_call(
        lambda *a: attend_kernel(*a, rows_at_once=rows_at_once),
        grid_spec=pltpu.PrefetchScalarGridSpec(
            num_scalar_prefetch=1,
            grid=(pairs,),
            in_specs=[col(0), col(pairs), col(2 * pairs)],
            out_specs=[col(0), pl.BlockSpec((2, slots, slots), lambda i, n: (i, 0, 0)), col(0)],
        ),
        out_shape=[
            jax.ShapeDtypeStruct((slots, d), bf16),
            jax.ShapeDtypeStruct((2 * pairs, slots, slots), bf16),
            jax.ShapeDtypeStruct((slots, d), f32),
        ],
        compiler_params=params(),
        name="attend",
    )(length, qkv, qkv, qkv)


def middle_kernel(
    len_ref, mixed_ref, x_ref, cot_ref, mod_ref, linv_ref, ow_ref, ob_ref, uw_ref, ub_ref, dw_ref, db_ref,
    out_ref, h2_ref, act_ref, dbr_ref, dup_ref, dat_ref, dmix_ref, dmid_ref, dmod_ref,
):
    i = pl.program_id(0)
    tile, d = x_ref.shape
    mod = lambda k: mod_ref[:, k * d : (k + 1) * d]
    gate1, shift2, scale2, gate2 = mod(2), mod(3), mod(4), mod(5)
    slot = lax.broadcasted_iota(jnp.int32, (tile, 1), 0) + i * tile
    valid = slot < len_ref[0]
    attn = jnp.where(valid, mm(mixed_ref[...], ow_ref[...], NN) + ob_ref[...].astype(f32), 0.0)
    mid = x_ref[...].astype(f32) + gate1 * attn
    c = mid - jnp.mean(mid, axis=1, keepdims=True)
    r2 = lax.rsqrt(jnp.mean(c * c, axis=1, keepdims=True) + EPS)
    n2 = c * r2
    h2 = (n2 * (1.0 + scale2) + shift2).astype(bf16)
    h2_ref[...] = h2
    cot = cot_ref[...].astype(f32)
    dbr = (gate2 * cot).astype(bf16)
    dbr_ref[...] = dbr
    ff = uw_ref.shape[1]
    step = 512
    for n in range(0, ff, step):
        u = mm(h2, uw_ref[:, n : n + step], NN) + ub_ref[:, n : n + step].astype(f32)
        c0 = 0.7978845608028654
        th = jnp.tanh(c0 * (u + 0.044715 * u * u * u))
        half = 0.5 * (1.0 + th)
        act_ref[:, n : n + step] = (u * half).astype(bf16)
        grad = half + 0.5 * u * (1.0 - th * th) * (c0 * (1.0 + 3.0 * 0.044715 * u * u))
        da = mm(dbr, dw_ref[n : n + step, :], NT)
        dup_ref[:, n : n + step] = (da * grad).astype(bf16)
    branch = mm(act_ref[...], dw_ref[...], NN) + db_ref[...].astype(f32)
    out_ref[...] = (mid + gate2 * branch).astype(bf16)
    dgate2 = jnp.sum(cot * branch, axis=0, keepdims=True)
    dh2 = mm(dup_ref[...], uw_ref[...], NT)
    dscale2 = jnp.sum(dh2 * n2, axis=0, keepdims=True)
    dshift2 = jnp.sum(dh2, axis=0, keepdims=True)
    dn2 = dh2 * (1.0 + scale2)
    dmid = cot + r2 * (
        dn2 - jnp.mean(dn2, axis=1, keepdims=True) - n2 * jnp.mean(dn2 * n2, axis=1, keepdims=True)
    )
    dmid_ref[...] = dmid
    dgate1 = jnp.sum(dmid * attn, axis=0, keepdims=True)
    dat = jnp.where(valid, gate1 * dmid, 0.0).astype(bf16)
    dat_ref[...] = dat
    dmix_ref[...] = (mm(dat, ow_ref[...], NT) * linv_ref[...]).astype(bf16)
    part = jnp.concatenate([dgate1, dshift2, dscale2, dgate2], axis=1)

    @pl.when(i == 0)
    def _():
        dmod_ref[...] = part

    @pl.when(i > 0)
    def _():
        dmod_ref[...] += part


def middle_part(length, mixed, x, cot, mod, linv, ow, uw, dw, b, tile=256):
    slots, d = x.shape
    ff = uw.shape[1]
    row = lambda n: pl.BlockSpec((tile, n), lambda i, n_: (i, 0))
    S = jax.ShapeDtypeStruct
    return pl.pallas_call(
        middle_kernel,
        grid_spec=pltpu.PrefetchScalarGridSpec(
            num_scalar_prefetch=1,
            grid=(slots // tile,),
            in_specs=[row(d), row(d), row(d), full(mod.shape), row(d), full(ow.shape), part(b, d, 3),
                      full(uw.shape), part(b, 2 * d, 2), full(dw.shape), part(b, d, 6)],
            out_specs=[row(d), row(d), row(ff), row(d), row(ff), row(d), row(d), row(d),
                       pl.BlockSpec((1, 4 * d), lambda i, n_: (0, 0))],
        ),
        out_shape=[S((slots, d), bf16), S((slots, d), bf16), S((slots, ff), bf16), S((slots, d), bf16),
                   S((slots, ff), bf16), S((slots, d), bf16), S((slots, d), bf16), S((slots, d), f32),
                   S((1, 4 * d), f32)],
        compiler_params=params(),
        name="middle_part",
    )(length, mixed, x, cot, mod, linv, ow, b, uw, b, dw, b)


MESH = pl.DeviceIdType.MESH
STRIP = 512
RINGS = dict(r0=4, r1=6, r2=7, r3=6)
DELAYS = (0, 1, 3, 5, 8, 9)


class Exchange:
    def __init__(self, groups, batch, own, s, sems, ready, chunks):
        self.G, self.B, self.H, self.chunks = groups, batch, groups // 4, chunks
        self.plan = []
        while len(self.plan) - self.plan.count(None) < chunks:
            n = len(self.plan) - self.plan.count(None)
            self.plan.append(n if len(self.plan) >= len(ready) or n < ready[len(self.plan)] else None)
        self.gaps = [t for t, c in enumerate(self.plan) if c is None]
        self.last = len(self.plan) - 1 + DELAYS[-1]
        self.own = own
        self.s = s
        self.send, self.recv = sems
        g, c = lax.axis_index("groups"), lax.axis_index("batch")
        self.c, self.x, self.y, self.z = c, g % 2, (g // 2) % 2, g // 4
        x, y, z, H, B = self.x, self.y, self.z, self.H, self.B
        pos = lambda z_, y_, x_: z_ * 4 + y_ * 2 + x_
        self.cores = [(g, (c + k) % B) for k in range(1, B)]
        self.across_x = (pos(z, y, 1 - x), c)
        self.across_y = (pos(z, 1 - y, x), c)
        self.across_z = [(pos((z + k) % H, y, x), c) for k in range(1, H)]

    @staticmethod
    def sems_per_chunk(groups, batch):
        return 2 * (batch - 1) + 4 + (groups // 4 - 1)

    def barrier(self):
        sem = pltpu.get_barrier_semaphore()
        peers = self.cores + [self.across_x, self.across_y] + self.across_z
        for p in peers:
            pl.semaphore_signal(sem, inc=1, device_id=p, device_id_type=MESH)
        pl.semaphore_wait(sem, len(peers))

    def copy(self, j, n, src, dst, peer):
        return pltpu.make_async_remote_copy(
            src_ref=src, dst_ref=dst, send_sem=self.send.at[j, n], recv_sem=self.recv.at[j, n],
            device_id=peer, device_id_type=MESH,
        )

    def copies(self, j, phase):
        B, H, x, y = self.B, self.H, self.x, self.y
        s = self.s
        rows, width = s["r0"].shape[-2:]
        half = rows // 2
        q0, q1, q2, q3 = (j % RINGS[k] for k in ("r0", "r1", "r2", "r3"))
        if phase == 0:
            out = []
            for k, p in enumerate(self.cores):
                cols = pl.ds(pl.multiple_of(p[1] * width, width), width)
                out.append(self.copy(j, k, self.own(j).at[:, :, :, :, cols], s["r0"].at[q0, k], p))
            return out
        n = B - 1
        if phase == 1:
            total = s["r0"].at[q0, 0]
            return [
                self.copy(j, n, total.at[:, :, 1 - x, :half], s["r1"].at[q1, 0], self.across_x),
                self.copy(j, n + 1, total.at[:, 1 - y, :, half:], s["r1"].at[q1, 1], self.across_y),
            ]
        if phase == 2:
            return [
                self.copy(j, n + 2, s["r1"].at[q1, 0, :, 1 - y], s["r2"].at[q2, :, :half], self.across_y),
                self.copy(j, n + 3, s["r1"].at[q1, 1, :, 1 - x], s["r2"].at[q2, :, half:], self.across_x),
            ]
        n += 4
        if phase == 3:
            return [
                self.copy(j, n + k, s["r2"].at[q2, p[0] // 4], s["r3"].at[q3, k], p)
                for k, p in enumerate(self.across_z)
            ]
        n += H - 1
        cols = pl.ds(pl.multiple_of(self.c * width, width), width)
        place = s["out"].at[j, :, cols]
        return [self.copy(j, n + k, place, place, p) for k, p in enumerate(self.cores)]

    def start(self, j, phase):
        for d in self.copies(j, phase):
            d.start()

    def finish(self, j, phase):
        for d in self.copies(j, phase):
            d.wait()
        s, x, y, z, H = self.s, self.x, self.y, self.z, self.H
        rows, width = s["r0"].shape[-2:]
        half = rows // 2
        q0, q1, q2, q3 = (j % RINGS[k] for k in ("r0", "r1", "r2", "r3"))
        cols = pl.ds(pl.multiple_of(self.c * width, width), width)
        if phase == 0:
            own = self.own(j)

            def add(h, _):
                t = own[h, :, :, :, cols]
                if self.B == 2:
                    t = t + s["r0"][q0, 0, h]
                else:
                    t = t.astype(f32)
                    for k in range(self.B - 1):
                        t = t + s["r0"][q0, k, h].astype(f32)
                s["r0"][q0, 0, h] = t.astype(bf16)
                return _

            lax.fori_loop(0, H, add, 0)
        elif phase == 1:

            def add(h, _):
                s["r1"][q1, 0, h] = s["r1"][q1, 0, h] + s["r0"][q0, 0, h, :, x, :half]
                s["r1"][q1, 1, h] = s["r1"][q1, 1, h] + s["r0"][q0, 0, h, y, :, half:]
                return _

            lax.fori_loop(0, H, add, 0)
        elif phase == 2:
            s["r2"][q2, :, :half] = s["r2"][q2, :, :half] + s["r1"][q1, 0, :, y]
            s["r2"][q2, :, half:] = s["r2"][q2, :, half:] + s["r1"][q1, 1, :, x]
        elif phase == 3:
            t = s["r2"][q2, z].astype(f32)
            for k in range(H - 1):
                t = t + s["r3"][q3, k].astype(f32)
            s["out"][j, :, cols] = t

    @staticmethod
    def scratch(groups, batch, chunks, rows, cols):
        H, w = groups // 4, cols // batch
        return dict(
            r0=pltpu.VMEM((RINGS["r0"], batch - 1, H, 2, 2, rows, w), bf16),
            r1=pltpu.VMEM((RINGS["r1"], 2, H, 2, rows // 2, w), bf16),
            r2=pltpu.VMEM((RINGS["r2"], H, rows, w), bf16),
            r3=pltpu.VMEM((RINGS["r3"], H - 1, rows, w), bf16),
            out=pltpu.VMEM((chunks, rows, cols), f32),
        )

    def tick(self, t, first=None, final=None):
        static = isinstance(t, int)
        if static:
            first = final = t
        n = len(self.plan)
        for phase in range(5, -1, -1):
            lo, hi = first - DELAYS[phase], final - DELAYS[phase]
            j = t - DELAYS[phase]
            if hi < 0 or lo >= n or (static and self.plan[j] is None):
                continue

            def act(phase=phase, j=j):
                c = self.plan[j] if static else j
                if not static:
                    for g in self.gaps:
                        if g < lo:
                            c = c - 1
                        elif g <= hi:
                            c = c - jnp.where(j > g, 1, 0)
                if phase > 0:
                    self.finish(c, phase - 1)
                if phase < 5:
                    self.start(c, phase)

            conds = []
            if lo < 0:
                conds.append(j >= 0)
            if hi >= n:
                conds.append(j < n)
            conds += [j != g for g in self.gaps if lo <= g <= hi]
            if static or not conds:
                act()
            else:
                ok = conds[0]
                for c in conds[1:]:
                    ok = jnp.logical_and(ok, c)
                pl.when(ok)(act)


class Small:
    def __init__(self, ex, sems, total=None, mine=None, seen=None):
        self.ex, self.total, self.mine, self.seen = ex, total, mine, seen
        self.send, self.recv = sems

    @staticmethod
    def count(groups, batch):
        return batch - 1 + 2 + groups // 4 - 1

    def copies(self, phase):
        ex = self.ex
        peers = [ex.cores, [ex.across_x], [ex.across_y], ex.across_z][phase]
        first = [0, ex.B - 1, ex.B, ex.B + 1][phase]
        out = []
        for k, p in enumerate(peers):
            n = first + k
            if self.seen is None:
                src, dst = self.mine.at[phase], self.total.at[n]
            else:
                at = (ex.z, ex.y, ex.x, ex.c)[: 4 - phase]
                src = dst = self.seen.at[at]
            out.append(pltpu.make_async_remote_copy(
                src_ref=src, dst_ref=dst, send_sem=self.send.at[n], recv_sem=self.recv.at[n],
                device_id=p, device_id_type=MESH))
        return out

    def start(self, phase):
        for d in self.copies(phase):
            d.start()

    def finish(self, phase):
        for d in self.copies(phase):
            d.wait()
        if self.seen is None:
            ex = self.ex
            n = [ex.B - 1, 1, 1, ex.H - 1][phase]
            first = [0, ex.B - 1, ex.B, ex.B + 1][phase]
            t = self.mine[phase]
            for k in range(n):
                t = t + self.total[first + k]
            self.mine[phase + 1] = t


def back_kernel(groups, batch, per, n_chunks, *refs):
    (act_hbm, dbr_hbm, h2_hbm, dup_hbm, mixed_hbm, dat_hbm, dmix_hbm, qkv_hbm, e_hbm, h1_hbm, w_hbm, x_hbm, dmid_hbm, mw_hbm,
     cos_ref, sin_ref, mod_ref, dmodb_ref, te_ref,
     dwo, uwo, owo, qwo, bias_out, early_out, late_out, fg_hbm, tg_ref,
     own, r0, r1, r2, r3, out, total, mine, early, late, etmp, ltmp,
     ebuf, dsb, qkv, mixed, dmix, dbr, h2, dat, dmid, fg, dmoda_ref,
     send, recv, ssum, rsum, sear, rear, slat, rlat, ld, eld, dld, fst, ost, mld) = refs
    slots, d = mixed.shape
    H, rows = groups // 4, d // groups
    chunk = lambda strip: strip // per
    n_own = own.shape[0]
    pairs = d // 128
    first, second = pairs // 2, pairs - 1
    ready = [4, 6, 8, 10, 10] + [10] * first + [13] * (second - first + 1) + [15] * (1 + pairs - second) + [16]
    ex = Exchange(groups, batch, lambda j: own.at[j % n_own], dict(r0=r0, r1=r1, r2=r2, r3=r3, out=out), (send, recv),
                  [n // per for n in ready], n_chunks)
    sums = Small(ex, (ssum, rsum), total=total, mine=mine)
    gather_early = Small(ex, (sear, rear), seen=early)
    gather_late = Small(ex, (slat, rlat), seen=late)

    load = lambda k, src, dst: pltpu.make_async_copy(src, dst, ld.at[k])
    half = lambda ref, k: ref.at[:, k * d : (k + 1) * d]
    loads = [
        load(0, half(act_hbm, 0), ebuf.at[1, 0]), load(1, half(act_hbm, 1), ebuf.at[1, 1]), load(2, dbr_hbm, dbr),
        load(3, h2_hbm, h2), load(4, half(dup_hbm, 0), dsb.at[0]), load(5, half(dup_hbm, 1), dsb.at[1]),
        load(6, mixed_hbm, mixed), load(7, dat_hbm, dat), load(8, qkv_hbm, qkv), load(9, dmix_hbm, dmix),
    ]
    load_h1 = load(10, h1_hbm, h2)
    load_w = [load(11 + k, half(w_hbm, k), (ebuf.at[0, 0], ebuf.at[0, 1], dbr)[k]) for k in range(3)]
    load_x = load(14, x_hbm, dat)
    free = [mixed, dmix, ebuf.at[1, 0], dsb.at[0], dsb.at[1], ebuf.at[1, 1]]
    load_m = [pltpu.make_async_copy(half(mw_hbm, k), free[k], mld.at[k]) for k in range(6)]
    load_e = lambda p, slot: pltpu.make_async_copy(e_hbm.at[pl.ds(2 * p, 2)], ebuf.at[slot], eld.at[slot])
    for k in (0, 2, 1):
        loads[k].start()

    for k in range(4 * d // STRIP):
        etmp[k : k + 1, :] = dmodb_ref[:, k * STRIP : (k + 1) * STRIP]
    t = te_ref[...].astype(f32)
    t = t * jax.nn.sigmoid(t)
    at = 4 * d // STRIP
    for k in range(d // STRIP):
        etmp[at + k : at + k + 1, :] = t[:, k * STRIP : (k + 1) * STRIP]
    at += d // STRIP
    etmp[at:, :] = jnp.zeros((etmp.shape[0] - at, STRIP), f32)
    early[ex.z, ex.y, ex.x, ex.c] = etmp[...].astype(bf16)
    mine[0] = jnp.zeros(mine.shape[1:], f32)
    ex.barrier()
    gather_early.start(0)

    def column_sums(value, row, k):
        mine[0, pl.ds(row + k, 1), :] = jnp.sum(value.astype(f32), axis=0, keepdims=True)

    def wgrad_into(left, block_rows, rights, place, zs, before=None):
        parts = block_rows // rows

        def body(i, _):
            n = zs * 4 * block_rows
            if before is not None:
                before(i, n)
            lt = left(i * n, n).T
            for k, right in enumerate(rights):
                r = mm(lt, right(), NN).astype(bf16)
                for b in range(4 * zs):
                    for part in range(parts):
                        strip = place(k, part)
                        lo = b * block_rows + part * rows
                        off = (strip % per) * STRIP
                        cols = pl.ds(off if isinstance(off, int) else pl.multiple_of(off, STRIP), STRIP)
                        own[chunk(strip) % n_own, i * zs + b // 4, (b // 2) % 2, b % 2, :, cols] = r[lo : lo + rows]
            return _

        lax.fori_loop(0, H // zs, body, 0)

    for k in (0, 2):
        loads[k].wait()
    for k in (3, 4, 5, 6, 7):
        loads[k].start()
    wide = lambda ref: lambda lo, n: ref[lo // d, :, pl.ds(pl.multiple_of(lo % d, 128), n)]
    flat = lambda ref: lambda lo, n: ref[:, pl.ds(pl.multiple_of(lo, 128), n)]
    strip_at = lambda k: pl.ds(k * STRIP if isinstance(k, int) else pl.multiple_of(k * STRIP, STRIP), STRIP)
    cut = lambda ref, k: lambda: ref[:, strip_at(k)]

    def second_half(i, n):
        @pl.when(i * n == d)
        def _():
            loads[1].wait()

    wgrad_into(wide(ebuf.at[1]), 2 * rows, [cut(dbr, k) for k in range(2)], lambda k, part: 2 * k + part, 2, second_half)
    for k in range(2):
        column_sums(cut(dbr, k)(), 12, k)
    gather_early.finish(0)
    gather_early.start(1)
    ex.tick(0)
    for k in (3, 4, 5):
        loads[k].wait()
    for k in (8, 9):
        loads[k].start()
    load_e(0, 0).start()
    for h in range(2):
        wgrad_into(flat(h2), rows, [cut(dsb.at[h], k) for k in range(2)], lambda k, part: 4 + 2 * h + k, 2)
        for k in range(2):
            column_sums(cut(dsb.at[h], k)(), 8 + 2 * h, k)
        if h == 0:
            gather_early.finish(1)
            gather_early.start(2)
        ex.tick(1 + h)
    load_h1.start()
    for k in (6, 7):
        loads[k].wait()
    wgrad_into(flat(mixed), rows, [cut(dat, k) for k in range(2)], lambda k, part: 8 + k, 2)
    for k in range(2):
        column_sums(cut(dat, k)(), 6, k)
    gather_early.finish(2)
    gather_early.start(3)
    load_x.start()
    ex.tick(3)
    ex.tick(4)
    for k in (8, 9):
        loads[k].wait()
    gather_early.finish(3)
    lane = lax.broadcasted_iota(jnp.int32, (1, 128), 1)
    even = even_lanes(slots)
    at_once = 256

    def attention(p, slot):
        col = lambda off: pl.ds(pl.multiple_of(off + p * 128, 128), 128)
        qc, kc, vc = col(0), col(d), col(2 * d)
        q, k, v, do = qkv[:, qc], qkv[:, kc], qkv[:, vc], dmix[:, qc]
        dqs = []
        for h in range(2):
            own_lanes = lane < 64 if h == 0 else lane >= 64
            parts = []
            for a in range(0, slots, at_once):
                rws = pl.ds(a, at_once)
                t = dmix[rws, qc]
                t = jnp.where(own_lanes, t, jnp.zeros_like(t))
                inner = jnp.sum(t.astype(f32) * mixed[rws, qc].astype(f32), axis=1, keepdims=True)
                ds = ebuf[slot, h, rws, :] * (mm(t, v, NT) - inner).astype(bf16)
                dsb[h, rws, :] = ds
                parts.append(mm(ds, k, NN))
            dqs.append(jnp.concatenate(parts, axis=0))
        do_t, q_t = do.T, q.T
        dv = jnp.concatenate([mm(do_t[h * 64 : h * 64 + 64], ebuf[slot, h], NN) for h in range(2)], axis=0)
        dk = jnp.concatenate([mm(q_t[h * 64 : h * 64 + 64], dsb[h], NN) for h in range(2)], axis=0)
        cos, sin = cos_ref[...], -sin_ref[...]
        dq = jnp.where(lane < 64, dqs[0], dqs[1]) * 0.125
        qkv[:, qc] = turn(dq, cos, sin, even).astype(bf16)
        qkv[:, kc] = turn(dk.T, cos, sin, even).astype(bf16)
        qkv[:, vc] = dv.T.astype(bf16)

    def qkv_grad(rights, places):
        zs = 2

        def body(i, carry):
            n = zs * 4 * rows
            lt = h2[:, pl.ds(pl.multiple_of(i * n, 128), n)].T
            for right, where in zip(rights, places):
                r = mm(lt, right(), NN).astype(bf16)
                for c, (strip, at) in enumerate(where):
                    lo = (strip % per) * STRIP + at * 128
                    for b in range(4 * zs):
                        own[chunk(strip) % n_own, i * zs + b // 4, (b // 2) % 2, b % 2, :, lo : lo + 128] = (
                            r[b * rows : (b + 1) * rows, c * 128 : (c + 1) * 128]
                        )
            return carry

        lax.fori_loop(0, H // zs, body, 0)

    span = lambda k, lo, hi: lambda: qkv[:, k * d + lo * 128 : k * d + hi * 128]
    late_cols = [(k, p) for k in range(3) for p in range(first, second)] + [(k, p) for k in range(3) for p in range(second, pairs)]
    late_place = {kp: (13 + n // 4, n % 4) for n, kp in enumerate(late_cols)}
    t1 = 5 + first

    def heads(p, carry):
        slot = p % 2
        load_e(p, slot).wait()

        @pl.when(p + 1 < pairs)
        def _():
            load_e(p + 1, 1 - slot).start()

        attention(p, slot)
        ex.tick(5 + p + jnp.where(p >= first, 1, 0) + jnp.where(p >= second, 1, 0), 5, 6 + pairs)

        @pl.when(p == first - 1)
        def _():
            load_h1.wait()
            qkv_grad([cut(qkv, 2 * k) for k in range(3)], [[(10 + k, c) for c in range(4)] for k in range(3)])
            for k in range(3):
                column_sums(cut(qkv, 2 * k)(), 2 * k, 0)
            ex.tick(t1)

        @pl.when(p == second - 1)
        def _():
            for c in load_w:
                c.start()
            qkv_grad([span(k, first, second) for k in range(3)],
                     [[late_place[k, q] for q in range(first, second)] for k in range(3)])
            ex.tick(1 + 5 + second)

        return carry

    lax.fori_loop(0, pairs, heads, 0)
    assert second % 2 == 1
    for t in load_m:
        t.start()
    qkv_grad([lambda: jnp.concatenate([span(k, second, pairs)() for k in range(3)], axis=1)],
             [[late_place[k, q] for k in range(3) for q in range(second, pairs)]])
    t0 = 8 + pairs
    ex.tick(t0 - 1)
    for k in range(3):
        column_sums(cut(qkv, 2 * k + 1)(), 2 * k + 1, 0)
    sums.start(0)
    tile = dmid.shape[1]
    tiles = slots // tile
    row_tile = lambda i: pl.ds(pl.multiple_of(i * tile, tile), tile)
    load_d = lambda i, slot: pltpu.make_async_copy(dmid_hbm.at[row_tile(i)], dmid.at[slot], dld.at[slot])
    store_f = lambda i, slot: pltpu.make_async_copy(fg.at[slot], fg_hbm.at[row_tile(i)], fst.at[slot])
    load_d(0, 0).start()
    load_x.wait()
    for t in load_w:
        t.wait()
    dmoda_ref[...] = jnp.zeros_like(dmoda_ref)
    def front(i, carry):
        slot = i % 2

        @pl.when(i + 1 < tiles)
        def _():
            load_d(i + 1, 1 - slot).start()

        rws = row_tile(i)
        dh = (
            mm(qkv[rws, :d], ebuf[0, 0], NT) + mm(qkv[rws, d : 2 * d], ebuf[0, 1], NT) + mm(qkv[rws, 2 * d :], dbr[...], NT)
        )
        ex.tick(t0 + 2 * i, t0, t0 + 2 * tiles - 2)
        x = dat[rws, :].astype(f32)
        cen = x - jnp.mean(x, axis=1, keepdims=True)
        r = lax.rsqrt(jnp.mean(cen * cen, axis=1, keepdims=True) + EPS)
        n1 = cen * r
        dmoda_ref[:, :d] += jnp.sum(dh, axis=0, keepdims=True)
        dmoda_ref[:, d:] += jnp.sum(dh * n1, axis=0, keepdims=True)
        dn = dh * (1.0 + mod_ref[:, d : 2 * d])
        load_d(i, slot).wait()

        @pl.when(i >= 2)
        def _():
            store_f(i - 2, slot).wait()

        fg[slot] = dmid[slot] + r * (
            dn - jnp.mean(dn, axis=1, keepdims=True) - n1 * jnp.mean(dn * n1, axis=1, keepdims=True)
        )
        store_f(i, slot).start()
        for phase in range(3):

            @pl.when(i == phase)
            def _():
                sums.finish(phase)
                sums.start(phase + 1)

        ex.tick(t0 + 2 * i + 1, t0 + 1, t0 + 2 * tiles - 1)
        return carry

    lax.fori_loop(0, tiles, front, 0)
    for k in range(2 * d // 128):
        ltmp[k : k + 1, :] = dmoda_ref[:, k * 128 : (k + 1) * 128]
    late[ex.z, ex.y, ex.x, ex.c] = ltmp[...].astype(bf16)
    gather_late.start(0)
    sums.finish(3)

    def through_mod(k):
        load_m[k].wait()
        v = dmoda_ref[:, k * d : (k + 1) * d] if k < 2 else dmodb_ref[:, (k - 2) * d : (k - 1) * d]
        v = jnp.broadcast_to(v, (8, d)).astype(bf16)
        tg_ref[...] += mm(v, free[k][...], NT)[:1]

    pieces = [(2 * k + part, 0, dwo.at[part, :, k * STRIP : (k + 1) * STRIP]) for k in range(2) for part in range(2)]
    pieces += [(4 + k, 0, uwo.at[:, k * STRIP : (k + 1) * STRIP]) for k in range(4)]
    pieces += [(8 + k, 0, owo.at[:, k * STRIP : (k + 1) * STRIP]) for k in range(2)]
    pieces += [(10 + k, 0, qwo.at[:, k * d : k * d + STRIP]) for k in range(3)]
    for (k, p), (strip, at) in late_place.items():
        pieces.append((strip, at * 128, qwo.at[:, k * d + p * 128 : k * d + (p + 1) * 128]))
    stores = [pltpu.make_async_copy(early, early_out, ost.at[0])]
    for n, (strip, off, dst) in enumerate(pieces):
        off += (strip % per) * STRIP
        stores.append(pltpu.make_async_copy(out.at[chunk(strip), :, off : off + dst.shape[1]], dst, ost.at[n + 1]))

    def start_stores():
        for c in stores:
            c.start()

    tg_ref[...] = jnp.zeros_like(tg_ref)
    t = t0 + 2 * tiles
    stored = t > ex.last
    if stored:
        start_stores()
    for phase in range(4):
        through_mod(phase)
        if t <= ex.last:
            ex.tick(t)
            t += 1
            if t > ex.last:
                start_stores()
                stored = True
        gather_late.finish(phase)
        if phase < 3:
            gather_late.start(phase + 1)
    through_mod(4)
    through_mod(5)
    for k in range(mine.shape[1]):
        for c in range(STRIP // 128):
            at = k * (STRIP // 128) + c
            bias_out[at : at + 1, :] = mine[4, k : k + 1, c * 128 : (c + 1) * 128]
    for i in range(max(0, tiles - 2), tiles):
        store_f(i, i % 2).wait()
    while t <= ex.last:
        ex.tick(t)
        t += 1
    if not stored:
        start_stores()
    late_store = pltpu.make_async_copy(late, late_out, ost.at[len(stores)])
    late_store.start()
    for c in stores:
        c.wait()
    late_store.wait()


def backward(groups, batch, act, dbr, h2, dup, mixed, dat, dmix, qkv, e, h1, w, x, dmid, mw, cos, sin, mod, dmodb, te):
    slots, d = mixed.shape
    H, rows = groups // 4, d // groups
    per = max(1, 128 * batch // STRIP)
    n_chunks = 16 // per
    S = jax.ShapeDtypeStruct
    hbm = pl.BlockSpec(memory_space=pl.ANY)
    vm = pl.BlockSpec(memory_space=pltpu.VMEM)
    V = pltpu.VMEM
    sc = Exchange.scratch(groups, batch, n_chunks, rows, per * STRIP)
    ns, nsm = Exchange.sems_per_chunk(groups, batch), Small.count(groups, batch)
    dma = pltpu.SemaphoreType.DMA
    tile = 256
    seen = (H, 2, 2, batch)
    return pl.pallas_call(
        lambda *a: back_kernel(groups, batch, per, n_chunks, *a),
        in_specs=[hbm] * 14 + [vm] * 5,
        out_specs=[hbm] * 4 + [vm, hbm, hbm, hbm, vm],
        out_shape=[S((2, rows, d), f32), S((rows, 2 * d), f32), S((rows, d), f32), S((rows, 3 * d), f32),
                   S((16 * STRIP // 128, 128), f32), S(seen + (16, STRIP), bf16), S(seen + (16, 128), bf16),
                   S((slots, d), f32), S((1, d), f32)],
        scratch_shapes=[V((-(-10 // per), H, 2, 2, rows, per * STRIP), bf16),
                        sc["r0"], sc["r1"], sc["r2"], sc["r3"], sc["out"],
                        V((nsm, 16, STRIP), f32), V((5, 16, STRIP), f32), V(seen + (16, STRIP), bf16), V(seen + (16, 128), bf16),
                        V((16, STRIP), f32), V((16, 128), f32),
                        V((2, 2, slots, slots), bf16), V((2, slots, slots), bf16), V((slots, 3 * d), bf16), V((slots, d), bf16),
                        V((slots, d), bf16), V((slots, d), bf16), V((slots, d), bf16), V((slots, d), bf16),
                        V((2, tile, d), f32), V((2, tile, d), f32), V((1, 2 * d), f32),
                        dma((n_chunks, ns)), dma((n_chunks, ns)), dma((nsm,)), dma((nsm,)), dma((nsm,)), dma((nsm,)),
                        dma((nsm,)), dma((nsm,)), dma((15,)), dma((2,)), dma((2,)), dma((2,)), dma((27,)), dma((6,))],
        compiler_params=pltpu.CompilerParams(vmem_limit_bytes=67_000_000, collective_id=0, has_side_effects=True),
        name="backward",
    )(act, dbr, h2, dup, mixed, dat, dmix, qkv, e, h1, w, x, dmid, mw, cos, sin, mod, dmodb, te)


def finish_kernel(
    early_ref, late_ref, bias_ref, tg_ref, te_ref, dw_in, uw_in, ow_in, qw_in, fg_in,
    wg_hbm, tout_ref, mb_ref, qb_ref, ob_ref, ub_ref, db_ref, dw_out, uw_out, ow_out, qw_out, fg_out,
    flat, wg_ref, dw, uw, ow, qw, fg, isem, osem,
):
    rows, d = wg_ref.shape[0], wg_ref.shape[1] // 6
    tile = fg.shape[0] // 8
    cuts = [pl.ds(k * tile, tile) for k in range(8)]
    through = [(dw_in, dw, dw_out), (uw_in, uw, uw_out), (ow_in, ow, ow_out), (qw_in, qw, qw_out)]
    through += [(fg_in.at[c], fg.at[c], fg_out.at[c]) for c in cuts]
    ins = [pltpu.make_async_copy(a, v, isem.at[k]) for k, (a, v, _) in enumerate(through)]
    outs = [pltpu.make_async_copy(v, b, osem.at[k]) for k, (_, v, b) in enumerate(through)]
    for c in ins:
        c.start()
    g = lax.axis_index("groups")
    e, late = early_ref[...], late_ref[...]
    n = e.shape[0] // 16
    at, off = 4 * d // STRIP + (g * rows) // STRIP, (g * rows) % STRIP
    pick = lax.broadcasted_iota(jnp.int32, (STRIP, 128), 0) - lax.broadcasted_iota(jnp.int32, (STRIP, 128), 1) == off
    em = mm(e, jnp.where(pick, 1.0, 0.0).astype(bf16), NN).reshape(n, 16, 128)
    em = jnp.where(lax.broadcasted_iota(jnp.int32, em.shape, 1) == at, em, 0.0)
    em = jnp.broadcast_to(jnp.sum(em, axis=1, keepdims=True), em.shape).reshape(n * 16, 128).T[:rows]
    row = lax.broadcasted_iota(jnp.int32, em.shape, 1) % 16
    for r in range(16):
        left = jnp.where(row == r, em, 0.0).astype(bf16)
        wg_ref[:, r * 128 : (r + 1) * 128] = mm(left, late, NN)
        if r < 4 * d // STRIP:
            lo = 2 * d + r * STRIP
            wg_ref[:, lo : lo + STRIP] = mm(left, e, NN)
    store_wg = pltpu.make_async_copy(wg_ref, wg_hbm, osem.at[len(outs)])
    store_wg.start()
    for a, b in zip(ins, outs):
        a.wait()
        b.start()
    flat[:16, :] = jnp.sum(late.astype(f32).reshape(n, 16, 128), axis=0)
    es = jnp.sum(e.astype(f32).reshape(n, 16, STRIP), axis=0)
    for r in range(4 * d // STRIP):
        for c in range(STRIP // 128):
            k = 16 + r * (STRIP // 128) + c
            flat[k : k + 1, :] = es[r : r + 1, c * 128 : (c + 1) * 128]
    flat[48:, :] = jnp.zeros((flat.shape[0] - 48, 128), f32)
    lane = lax.broadcasted_iota(jnp.int32, (1, 128), 1)
    for ref, src, first in ((mb_ref, flat, 0), (qb_ref, bias_ref, 0), (ob_ref, bias_ref, 3 * d), (ub_ref, bias_ref, 4 * d), (db_ref, bias_ref, 6 * d)):
        width = ref.shape[1]
        at, off = first // 128 + (g * width) // 128, (g * width) % 128
        for k in range(-(-width // 128)):
            turned = [pltpu.roll(src[pl.ds(at + k + i, 1), :], (128 - off) % 128, 1) for i in range(2)]
            v = jnp.where(lane < 128 - off, turned[0], turned[1])
            w = min(128, width - k * 128)
            ref[:, k * 128 : k * 128 + w] = v[:, :w]
    t = te_ref[...].astype(f32)
    s = jax.nn.sigmoid(t)
    tout_ref[...] = tg_ref[...] * (s * (1.0 + t * (1.0 - s)))
    for c in outs:
        c.wait()
    store_wg.wait()


def finish(early, late, bias, tg, te, *results):
    rows, d = results[2].shape
    S = jax.ShapeDtypeStruct
    hbm, vm = pl.BlockSpec(memory_space=pl.ANY), pl.BlockSpec(memory_space=pltpu.VMEM)
    n = len(results)
    return pl.pallas_call(
        finish_kernel,
        in_specs=[vm] * 5 + [hbm] * n,
        out_specs=[hbm] + [vm] * 6 + [hbm] * n,
        out_shape=[S((rows, 6 * d), f32), S((1, d), f32)] + [S((1, k * rows), f32) for k in (6, 3, 1, 2, 1)]
        + [S(r.shape, f32) for r in results],
        scratch_shapes=[pltpu.VMEM((56, 128), f32), pltpu.VMEM((rows, 6 * d), f32)]
        + [pltpu.VMEM(r.shape, f32) for r in results]
        + [pltpu.SemaphoreType.DMA((n + 7,)), pltpu.SemaphoreType.DMA((n + 8,))],
        compiler_params=params(),
        name="finish",
    )(early, late, bias, tg, te, *results)


def solution(mesh):
    groups, batch = mesh.shape["groups"], mesh.shape["batch"]

    def body(frames, te, lengths, mod_w, mod_b, qkv_w, qkv_b, out_w, out_b, up_w, up_b, down_w, down_b, cot):
        x, ct = frames[0], cot[0]
        slots, d = x.shape
        row = lambda b: b.reshape(1, -1)
        biases = row(jnp.concatenate([qkv_b, out_b, up_b, down_b]))
        mod = modulation(te, mod_w, row(mod_b))
        h1, qkv, cos, sin = project_qkv(x, mod, qkv_w, biases, rot_tables(slots, d // HEADS))
        mixed, e, linv = attend(lengths, qkv)
        out, h2, act, dbr, dup, dat, dmix, dmid, dmod_b = middle_part(
            lengths, mixed, x, ct, mod, linv, out_w, up_w, down_w, biases
        )
        dws, uws, ows, qws, bs, early, late, fg, tg = backward(
            groups, batch, act, dbr, h2, dup, mixed, dat, dmix, qkv, e, h1, qkv_w, x, dmid, mod_w, cos, sin, mod, dmod_b, te
        )
        rows, n = d // groups, groups * batch
        mod_wg, time_grad, mb, qb, ob, ub, db, dws, uws, ows, qws, fg = finish(
            early.reshape(n * 16, STRIP), late.reshape(n * 16, 128), bs, tg, te, dws, uws, ows, qws, fg
        )
        return (out[None], fg[None], time_grad, mod_wg, mb[0], qws, qb[0], ows, ob[0], uws, ub[0], dws.reshape(2 * rows, d), db[0])

    split = P(("groups", "batch"))
    own = P("groups")
    return jax.shard_map(
        body, mesh=mesh,
        in_specs=(split,) * 3 + (P(),) * 10 + (split,),
        out_specs=(split,) * 3 + (own,) * 10,
        check_vma=False,
    )
```
